128 devices in a mesh: ctx: 32 (over y_hi, x, z), fsdp: 4 (over y_lo, core).
Axes of the slice: x: 4, y: 4 (y_hi: 2, y_lo: 2; y = y_hi * 2 + y_lo), z: 4, core: 2. Of those that a mesh axis runs over, the one named last changes fastest.
Arguments:
- layer_input: bfloat16 [4, 4096, 1024], P('fsdp', 'ctx'), may hold values from -6 to 6
- cotangent: bfloat16 [4, 4096, 1024], P('fsdp', 'ctx'), may hold values from -6 to 6
- block_order: int32 [4, 64], P('fsdp'), may hold values from 0 to 63, as said below
- query_weight: bfloat16 [1024, 2048], P('fsdp'), may hold values from -0.1875 to 0.1875
- key_projection: bfloat16 [1024, 1024], P('fsdp'), may hold values from -0.1875 to 0.1875
- value_projection: bfloat16 [1024, 1024], P('fsdp'), may hold values from -0.1875 to 0.1875
- output_weight: bfloat16 [2048, 1024], P('fsdp'), may hold values from -0.75 to 0.75
- gate_weight: bfloat16 [1024, 3072], P('fsdp'), may hold values from -0.1875 to 0.1875
- up_weight: bfloat16 [1024, 3072], P('fsdp'), may hold values from -0.1875 to 0.1875
- down_weight: bfloat16 [3072, 1024], P('fsdp'), may hold values from -0.109375 to 0.109375
- first_gain: float32 [1024], replicated, may hold values from 0.5 to 1.5
- second_gain: float32 [1024], replicated, may hold values from 0.5 to 1.5
- query_gain: float32 [128], replicated, may hold values from 0.25 to 1.75
- key_norm_gain: float32 [128], replicated, may hold values from 0.25 to 1.75
Outputs:
- layer_output: bfloat16 [4, 4096, 1024], P('fsdp', 'ctx')
- input_gradient: float32 [4, 4096, 1024], P('fsdp', 'ctx')
- query_weight_gradient: float32 [1024, 2048], P('fsdp')
- key_weight_gradient: float32 [1024, 1024], P('fsdp')
- value_weight_gradient: float32 [1024, 1024], P('fsdp')
- output_weight_gradient: float32 [2048, 1024], P('fsdp')
- gate_weight_gradient: float32 [1024, 3072], P('fsdp')
- up_weight_gradient: float32 [1024, 3072], P('fsdp')
- down_weight_gradient: float32 [3072, 1024], P('fsdp')
- first_gain_gradient: float32 [1024], P('fsdp')
- second_gain_gradient: float32 [1024], P('fsdp')
- query_gain_gradient: float32 [128], P('fsdp')
- key_gain_gradient: float32 [128], P('fsdp')
The draws below stay inside these ranges and needn't reach their ends.
Inputs may be any that keep to these rules, and one draw needn't show every extreme that they name: Each row of block_order names every block of 64 positions of its sequence exactly once; the two blocks of rows 2 c and 2 c + 1 are mirrored, block b together with block 2 * 32 - 1 - b, in either order.
All inputs are finite; a program needn't handle non-finite values.
Results may differ from the reference program's by a relative error of at most 0.034.
Values may be sent and summed in bfloat16 or wider, within the bound.
No kernel may reach another device: no remote copies, remote signals or barrier semaphores. Data moves between devices by JAX's collectives and lax.ppermute only.
A program may use at most 320 MiB of HBM per device.

```python
import math
import jax
import jax.numpy as jnp
from jax import lax

MODEL_WIDTH = 1024
HQ = 16
KEY_VALUE_HEADS = 8
HEAD_SIZE = 128
FF = 3072
LEN = 4096
SEQS = 4
N_CTX = 32


def draw_block_order(key, part):
    pair_count = N_CTX

    def one_order(row_key):
        lower_blocks = jax.random.permutation(jax.random.fold_in(row_key, 11), pair_count).astype(jnp.int32)
        flip_bits = jax.random.randint(jax.random.fold_in(row_key, 12), (pair_count,), 0, 2).astype(jnp.int32)
        first_block = jnp.where(flip_bits == 1, 2 * pair_count - 1 - lower_blocks, lower_blocks)
        second_block = 2 * pair_count - 1 - first_block
        return jnp.stack([first_block, second_block], axis=1).reshape(2 * pair_count).astype(jnp.int32)
    row_keys = jax.random.split(jax.random.fold_in(key, 7), SEQS)
    return jax.vmap(one_order)(row_keys)


def shard_levels(rng, shape, cuts, low, largest):
    factor_of = 1.0
    for axis_at, parts in cuts:
        draws = jax.random.uniform(jax.random.fold_in(jax.random.fold_in(rng, 6), axis_at), (parts,), jnp.float32, low / len(cuts), largest / len(cuts))
        factor_of = factor_of * jnp.repeat(jnp.exp(draws), shape[axis_at] // parts).reshape((-1,) + (1,) * (len(shape) - 1 - axis_at))
    return factor_of


def scatter_about(key, shape, scale, most, shards=(), kind=jnp.bfloat16):
    factor_of = shard_levels(key, shape, shards, -0.22, 0.18) if shards else 1.0
    result = jax.random.normal(key, shape, jnp.float32) * scale * factor_of
    return jnp.minimum(jnp.maximum(result, -most), most).astype(kind)


def setup_inputs(seed: int = 0) -> dict:
    seeds = jax.random.split(jax.random.key(seed), 15)
    return {
        "layer_input": scatter_about(seeds[0], (SEQS, LEN, MODEL_WIDTH), 1.0, 6.0, ((0, 4), (1, 32))),
        "cotangent": scatter_about(seeds[1], (SEQS, LEN, MODEL_WIDTH), 1.0, 6.0, ((0, 4), (1, 32))),
        "block_order": draw_block_order(jax.random.fold_in(seeds[14], 71), 0),
        "query_weight": scatter_about(seeds[3], (MODEL_WIDTH, HQ * HEAD_SIZE), MODEL_WIDTH ** -0.5, 0.1875, ((0, 4),)),
        "key_projection": scatter_about(seeds[4], (MODEL_WIDTH, KEY_VALUE_HEADS * HEAD_SIZE), MODEL_WIDTH ** -0.5, 0.1875, ((0, 4),)),
        "value_projection": scatter_about(seeds[5], (MODEL_WIDTH, KEY_VALUE_HEADS * HEAD_SIZE), MODEL_WIDTH ** -0.5, 0.1875, ((0, 4),)),
        "output_weight": scatter_about(seeds[6], (HQ * HEAD_SIZE, MODEL_WIDTH), (HQ * HEAD_SIZE // 32) ** -0.5, 0.75, ((0, 4),)),
        "gate_weight": scatter_about(seeds[7], (MODEL_WIDTH, FF), MODEL_WIDTH ** -0.5, 0.1875, ((0, 4),)),
        "up_weight": scatter_about(seeds[8], (MODEL_WIDTH, FF), MODEL_WIDTH ** -0.5, 0.1875, ((0, 4),)),
        "down_weight": scatter_about(seeds[9], (FF, MODEL_WIDTH), FF ** -0.5, 0.109375, ((0, 4),)),
        "first_gain": jnp.clip(1.0 + 0.1 * jax.random.normal(seeds[10], (MODEL_WIDTH,), jnp.float32), 0.5, 1.5),
        "second_gain": jnp.clip(1.0 + 0.1 * jax.random.normal(seeds[11], (MODEL_WIDTH,), jnp.float32), 0.5, 1.5),
        "query_gain": jnp.clip(1.0 + 0.15 * jax.random.normal(seeds[12], (HEAD_SIZE,), jnp.float32), 0.25, 1.75),
        "key_norm_gain": jnp.clip(1.0 + 0.15 * jax.random.normal(seeds[13], (HEAD_SIZE,), jnp.float32), 0.25, 1.75),
    }


EPSILON = 1e-06
THETA = 1000000.0
MASKED = -1e+30

def stored_state(values):
    return lax.optimization_barrier(values.astype(jnp.bfloat16))

def rms_apply(values, norm_gain):
    row_scale = lax.rsqrt(lax.optimization_barrier(jnp.mean(values * values, axis=-1, keepdims=True)) + EPSILON)
    normed = values * row_scale
    return (normed * norm_gain, normed, row_scale)

def root_mean_square_backward(gradient, normed, row_scale, norm_gain):
    normed_grad = gradient * norm_gain
    return row_scale * (normed_grad - normed * lax.optimization_barrier(jnp.mean(normed_grad * normed, axis=-1, keepdims=True)))

def rope_tables(positions, head_width):
    half_width = head_width // 2
    inverse_freq = jnp.power(THETA, -2.0 * jnp.arange(half_width, dtype=jnp.float32) / head_width)
    angles = positions.astype(jnp.float32)[:, None] * inverse_freq[None, :]
    return (jnp.cos(angles)[:, None, :], jnp.sin(angles)[:, None, :])

def rotary_apply(values, cosine_table, sine_values_table):
    half_width = values.shape[-1] // 2
    front_half = values[..., :half_width]
    back_half = values[..., half_width:]
    return jnp.concatenate([front_half * cosine_table - back_half * sine_values_table, back_half * cosine_table + front_half * sine_values_table], axis=-1)

def rotary_backward(gradient, cosine_table, sine_values_table):
    half_width = gradient.shape[-1] // 2
    front_half = gradient[..., :half_width]
    back_half = gradient[..., half_width:]
    return jnp.concatenate([front_half * cosine_table + back_half * sine_values_table, back_half * cosine_table - front_half * sine_values_table], axis=-1)

def left_dot(left_side, right_side):
    return lax.dot_general(left_side, right_side, (((0,), (0,)), ((), ())), preferred_element_type=jnp.float32)

def right_dot(left_side, right_side):
    return lax.dot_general(left_side, right_side, (((1,), (1,)), ((), ())), preferred_element_type=jnp.float32)

def masked_scores(queries, key_rows, query_pos, key_pos):
    raw_scores = jnp.einsum('qjed,kjd->jeqk', queries.astype(jnp.float32), key_rows.astype(jnp.float32)) * (1.0 / math.sqrt(HEAD_SIZE))
    allowed = key_pos[None, None, None, :] <= query_pos[None, None, :, None]
    return jnp.where(allowed, raw_scores, MASKED)

def one_sequence(seq_input, seq_cotangent, seq_order, weights, gains):
    query_weight, key_projection, value_projection, output_weight, gate_weight, up_weight, down_weight = weights
    first_gain, second_gain, query_gain, key_norm_gain = gains
    sequence_length = seq_input.shape[0]
    block_rows = sequence_length // seq_order.shape[0]
    positions = (seq_order[:, None] * block_rows + jnp.arange(block_rows, dtype=jnp.int32)[None, :]).reshape(-1).astype(jnp.int32)
    cosine_table, sine_values_table = rope_tables(positions, HEAD_SIZE)
    input_f32 = seq_input.astype(jnp.float32)
    gained, first_normed, first_scale = rms_apply(input_f32, first_gain)
    attention_input = stored_state(gained)
    query_pre = jnp.dot(attention_input, query_weight, preferred_element_type=jnp.float32).reshape(sequence_length, HQ, HEAD_SIZE)
    query_gained, query_normed, query_scale = rms_apply(query_pre, query_gain)
    query_rotated = stored_state(rotary_apply(query_gained, cosine_table, sine_values_table))
    key_before_norm = jnp.dot(attention_input, key_projection, preferred_element_type=jnp.float32).reshape(sequence_length, KEY_VALUE_HEADS, HEAD_SIZE)
    key_after_gain, key_after_norm, key_norm_scale = rms_apply(key_before_norm, key_norm_gain)
    key_rot = stored_state(rotary_apply(key_after_gain, cosine_table, sine_values_table))
    value_row_block = stored_state(jnp.dot(attention_input, value_projection, preferred_element_type=jnp.float32)).reshape(sequence_length, KEY_VALUE_HEADS, HEAD_SIZE)
    query_block_rows = min(512, sequence_length)
    count_of_blocks = sequence_length // query_block_rows
    grouped_queries = query_rotated.reshape(count_of_blocks, query_block_rows, KEY_VALUE_HEADS, 2, HEAD_SIZE)
    position_groups = positions.reshape(count_of_blocks, query_block_rows)

    def forward_block(block_item):
        queries, query_pos = block_item
        raw_scores = masked_scores(queries, key_rot, query_pos, positions)
        row_max = lax.optimization_barrier(jnp.max(raw_scores, axis=-1, keepdims=True))
        log_total = row_max + jnp.log(lax.optimization_barrier(jnp.sum(jnp.exp(raw_scores - row_max), axis=-1, keepdims=True)))
        weights_b = stored_state(jnp.exp(raw_scores - log_total))
        mixture = jnp.einsum('jeqk,kjd->qjed', weights_b.astype(jnp.float32), value_row_block.astype(jnp.float32))
        return (mixture, log_total)
    mixtures, log_totals = lax.map(forward_block, (grouped_queries, position_groups))
    mixed = mixtures.reshape(sequence_length, HQ * HEAD_SIZE)
    mixed_b = stored_state(mixed)
    residual_mid = input_f32 + jnp.dot(mixed_b, output_weight, preferred_element_type=jnp.float32)
    gained_mid, second_normed, second_scale = rms_apply(residual_mid, second_gain)
    mlp_in = stored_state(gained_mid)
    gate_pre = jnp.dot(mlp_in, gate_weight, preferred_element_type=jnp.float32)
    up_pre = jnp.dot(mlp_in, up_weight, preferred_element_type=jnp.float32)
    sigmoid_gate = jax.nn.sigmoid(gate_pre)
    silu_gate = gate_pre * sigmoid_gate
    hidden = stored_state(silu_gate * up_pre)
    layer_output = (residual_mid + jnp.dot(hidden, down_weight, preferred_element_type=jnp.float32)).astype(jnp.bfloat16)
    down_weight_grad = left_dot(hidden, seq_cotangent)
    hidden_grad = right_dot(seq_cotangent, down_weight)
    gate_grad = stored_state(hidden_grad * up_pre * sigmoid_gate * (1.0 + gate_pre * (1.0 - sigmoid_gate)))
    up_grad = stored_state(hidden_grad * silu_gate)
    gate_weight_grad = left_dot(mlp_in, gate_grad)
    up_weight_grad = left_dot(mlp_in, up_grad)
    mlp_in_grad = right_dot(gate_grad, gate_weight) + right_dot(up_grad, up_weight)
    second_gain_grad = lax.optimization_barrier(jnp.sum(mlp_in_grad * second_normed, axis=0))
    mid_grad = seq_cotangent.astype(jnp.float32) + root_mean_square_backward(mlp_in_grad, second_normed, second_scale, second_gain)
    mid_grad_b = stored_state(mid_grad)
    output_weight_grad = left_dot(mixed_b, mid_grad_b)
    mixed_gradient = stored_state(right_dot(mid_grad_b, output_weight))
    delta_rows = lax.optimization_barrier(jnp.sum(mixed_gradient.astype(jnp.float32).reshape(sequence_length, HQ, HEAD_SIZE) * mixed.reshape(sequence_length, HQ, HEAD_SIZE), axis=-1))
    grouped_gradient = mixed_gradient.reshape(count_of_blocks, query_block_rows, KEY_VALUE_HEADS, 2, HEAD_SIZE)
    grouped_delta = delta_rows.reshape(count_of_blocks, query_block_rows, KEY_VALUE_HEADS, 2)
    scale_factor = 1.0 / math.sqrt(HEAD_SIZE)

    def backward_block(running, block_item):
        key_sum, value_running_sum = running
        queries, query_pos, out_grad, delta_part, log_total = block_item
        probabilities = jnp.exp(masked_scores(queries, key_rot, query_pos, positions) - log_total)
        weights_f = stored_state(probabilities).astype(jnp.float32)
        out_grad_f = out_grad.astype(jnp.float32)
        value_running_sum = value_running_sum + jnp.einsum('jeqk,qjed->kjd', weights_f, out_grad_f)
        prob_grad = jnp.einsum('qjed,kjd->jeqk', out_grad_f, value_row_block.astype(jnp.float32))
        score_grad = stored_state(probabilities * (prob_grad - jnp.transpose(delta_part, (1, 2, 0))[..., None])).astype(jnp.float32)
        query_grad = jnp.einsum('jeqk,kjd->qjed', score_grad, key_rot.astype(jnp.float32)) * scale_factor
        key_sum = key_sum + jnp.einsum('jeqk,qjed->kjd', score_grad, queries.astype(jnp.float32)) * scale_factor
        return ((key_sum, value_running_sum), query_grad)
    empty_zero_block = jnp.zeros((sequence_length, KEY_VALUE_HEADS, HEAD_SIZE), jnp.float32)
    (key_sum, value_running_sum), query_grads = lax.scan(backward_block, (empty_zero_block, empty_zero_block), (grouped_queries, position_groups, grouped_gradient, grouped_delta, log_totals))
    query_back = rotary_backward(query_grads.reshape(sequence_length, HQ, HEAD_SIZE), cosine_table, sine_values_table)
    query_gain_grad = lax.optimization_barrier(jnp.sum(query_back * query_normed, axis=(0, 1)))
    query_pre_grad = stored_state(root_mean_square_backward(query_back, query_normed, query_scale, query_gain)).reshape(sequence_length, HQ * HEAD_SIZE)
    key_backward_pass = rotary_backward(key_sum, cosine_table, sine_values_table)
    key_gain_grad = lax.optimization_barrier(jnp.sum(key_backward_pass * key_after_norm, axis=(0, 1)))
    key_before_norm_gradient = stored_state(root_mean_square_backward(key_backward_pass, key_after_norm, key_norm_scale, key_norm_gain)).reshape(sequence_length, KEY_VALUE_HEADS * HEAD_SIZE)
    value_gradient_second = stored_state(value_running_sum).reshape(sequence_length, KEY_VALUE_HEADS * HEAD_SIZE)
    query_weight_grad = left_dot(attention_input, query_pre_grad)
    key_weight_grad = left_dot(attention_input, key_before_norm_gradient)
    value_weight_grad = left_dot(attention_input, value_gradient_second)
    attn_in_grad = right_dot(query_pre_grad, query_weight) + right_dot(key_before_norm_gradient, key_projection) + right_dot(value_gradient_second, value_projection)
    first_gain_grad = lax.optimization_barrier(jnp.sum(attn_in_grad * first_normed, axis=0))
    input_grad = mid_grad + root_mean_square_backward(attn_in_grad, first_normed, first_scale, first_gain)
    gradients = (query_weight_grad, key_weight_grad, value_weight_grad, output_weight_grad, gate_weight_grad, up_weight_grad, down_weight_grad, first_gain_grad, second_gain_grad, query_gain_grad, key_gain_grad)
    return (layer_output, input_grad, gradients)

def reference(layer_input, cotangent, block_order, query_weight, key_projection, value_projection, output_weight, gate_weight, up_weight, down_weight, first_gain, second_gain, query_gain, key_norm_gain):
    weights = (query_weight, key_projection, value_projection, output_weight, gate_weight, up_weight, down_weight)
    gains = (first_gain, second_gain, query_gain, key_norm_gain)

    def sequence_step(running, block_item):
        seq_input, seq_cotangent, seq_order = block_item
        seq_output, seq_grad, gradients = one_sequence(seq_input, seq_cotangent, seq_order, weights, gains)
        return (jax.tree.map(jnp.add, running, gradients), (seq_output, seq_grad))
    initial = tuple((jnp.zeros(member.shape, jnp.float32) for member in weights + gains))
    totals, (layer_output, input_gradient) = lax.scan(sequence_step, initial, (layer_input, cotangent, block_order))
    return (layer_output, input_gradient, totals[0], totals[1], totals[2], totals[3], totals[4], totals[5], totals[6], totals[7], totals[8], totals[9], totals[10])
```

```python
import math

import jax
import jax.numpy as jnp
from jax import lax
from jax.sharding import PartitionSpec as P

HQ = 16
KEY_VALUE_HEADS = 8
HEAD_SIZE = 128


EPSILON = 1e-06
THETA = 1000000.0
MASKED = -1e30


def rms_apply(values, norm_gain):
    row_scale = lax.rsqrt(jnp.mean(values * values, axis=-1, keepdims=True) + EPSILON)
    normed = values * row_scale
    return (normed * norm_gain, normed, row_scale)


def root_mean_square_backward(gradient, normed, row_scale, norm_gain):
    normed_grad = gradient * norm_gain
    return row_scale * (
        normed_grad - normed * jnp.mean(normed_grad * normed, axis=-1, keepdims=True)
    )


def rope_tables(positions, head_width):
    half_width = head_width // 2
    inverse_freq = jnp.power(THETA, -2.0 * jnp.arange(half_width, dtype=jnp.float32) / head_width)
    angles = positions.astype(jnp.float32)[:, None] * inverse_freq[None, :]
    return (jnp.cos(angles)[:, None, :], jnp.sin(angles)[:, None, :])


def rotary_apply(values, cosine_table, sine_values_table):
    half_width = values.shape[-1] // 2
    front_half = values[..., :half_width]
    back_half = values[..., half_width:]
    return jnp.concatenate(
        [
            front_half * cosine_table - back_half * sine_values_table,
            back_half * cosine_table + front_half * sine_values_table,
        ],
        axis=-1,
    )


def rotary_backward(gradient, cosine_table, sine_values_table):
    half_width = gradient.shape[-1] // 2
    front_half = gradient[..., :half_width]
    back_half = gradient[..., half_width:]
    return jnp.concatenate(
        [
            front_half * cosine_table + back_half * sine_values_table,
            back_half * cosine_table - front_half * sine_values_table,
        ],
        axis=-1,
    )


def left_dot(left_side, right_side):
    return lax.dot_general(
        left_side, right_side, (((0,), (0,)), ((), ())), preferred_element_type=jnp.float32
    )


def right_dot(left_side, right_side):
    return lax.dot_general(
        left_side, right_side, (((1,), (1,)), ((), ())), preferred_element_type=jnp.float32
    )


def on_device(
    layer_input,
    cotangent,
    block_order,
    query_weight,
    key_projection,
    value_projection,
    output_weight,
    gate_weight,
    up_weight,
    down_weight,
    first_gain,
    second_gain,
    query_gain,
    key_norm_gain,
):
    local_rows = layer_input.shape[1]
    block_rows = local_rows // 2
    ctx_size = lax.axis_size("ctx")
    halves = ctx_size // HQ
    half_devices = ctx_size // halves
    order_row = block_order[0]
    device_place = lax.axis_index("ctx")
    my_half = device_place // half_devices
    all_positions = (
        order_row[:, None] * block_rows + jnp.arange(block_rows, dtype=jnp.int32)[None, :]
    ).reshape(-1)
    own_positions = lax.dynamic_slice_in_dim(all_positions, device_place * local_rows, local_rows)
    cosine_table, sine_values_table = rope_tables(own_positions, HEAD_SIZE)
    scale_factor = 1.0 / math.sqrt(HEAD_SIZE)
    half_rows = half_devices * local_rows
    query_positions = lax.dynamic_slice_in_dim(all_positions, my_half * half_rows, half_rows)
    allowed = all_positions[None, :] <= query_positions[:, None]
    half_select = (jnp.arange(halves, dtype=jnp.int32) == my_half)[:, None, None, None]

    def to_heads(per_head):
        by_head = jnp.transpose(per_head, (1, 0, 2))
        return jnp.where(half_select, by_head[None], jnp.zeros_like(by_head)[None]).reshape(
            ctx_size, local_rows, per_head.shape[-1]
        )

    def gather_half(received):
        return lax.dynamic_slice_in_dim(received, my_half * half_devices, half_devices, 0).reshape(
            half_rows, received.shape[-1]
        )

    def from_heads(per_head):
        blocks = per_head.reshape(half_devices, local_rows, per_head.shape[-1])
        return jnp.where(half_select, blocks[None], jnp.zeros_like(blocks)[None]).reshape(
            ctx_size, local_rows, per_head.shape[-1]
        )

    def own_heads(received):
        mine = lax.dynamic_slice_in_dim(received, my_half * half_devices, half_devices, 0)
        return jnp.transpose(mine, (1, 0, 2))

    def exchange(values):
        return lax.all_to_all(values, "ctx", split_axis=0, concat_axis=0, tiled=True)

    full_query, full_key, full_value, full_output, full_gate, full_up, full_down = (
        lax.all_gather(query_weight, "fsdp", axis=0, tiled=True),
        lax.all_gather(key_projection, "fsdp", axis=0, tiled=True),
        lax.all_gather(value_projection, "fsdp", axis=0, tiled=True),
        lax.all_gather(output_weight, "fsdp", axis=0, tiled=True),
        lax.all_gather(gate_weight, "fsdp", axis=0, tiled=True),
        lax.all_gather(up_weight, "fsdp", axis=0, tiled=True),
        lax.all_gather(down_weight, "fsdp", axis=0, tiled=True),
    )
    input_f32 = layer_input[0].astype(jnp.float32)
    gained, first_normed, first_scale = rms_apply(input_f32, first_gain)
    attention_input = gained.astype(jnp.bfloat16)
    query_pre = jnp.dot(attention_input, full_query, preferred_element_type=jnp.float32).reshape(
        local_rows, HQ, HEAD_SIZE
    )
    query_gained, query_normed, query_scale = rms_apply(query_pre, query_gain)
    query_rotated = rotary_apply(query_gained, cosine_table, sine_values_table).astype(jnp.bfloat16)
    key_before_norm = jnp.dot(
        attention_input, full_key, preferred_element_type=jnp.float32
    ).reshape(local_rows, KEY_VALUE_HEADS, HEAD_SIZE)
    key_after_gain, key_after_norm, key_norm_scale = rms_apply(key_before_norm, key_norm_gain)
    own_keys = rotary_apply(key_after_gain, cosine_table, sine_values_table).astype(jnp.bfloat16)
    own_values = (
        jnp.dot(attention_input, full_value, preferred_element_type=jnp.float32)
        .astype(jnp.bfloat16)
        .reshape(local_rows, KEY_VALUE_HEADS, HEAD_SIZE)
    )
    group = HQ // KEY_VALUE_HEADS
    key_value = jnp.repeat(jnp.concatenate([own_keys, own_values], axis=-1), group, axis=1)
    sent = jnp.concatenate([to_heads(query_rotated), jnp.tile(
        jnp.transpose(key_value, (1, 0, 2)), (halves, 1, 1))], axis=-1)
    received = exchange(sent)
    head_query = gather_half(received[..., :HEAD_SIZE])
    head_key = received[..., HEAD_SIZE : 2 * HEAD_SIZE].reshape(-1, HEAD_SIZE)
    head_value = received[..., 2 * HEAD_SIZE :].reshape(-1, HEAD_SIZE)

    def head_scores():
        raw_scores = (
            jnp.einsum("qd,kd->qk", head_query, head_key, preferred_element_type=jnp.float32)
            * scale_factor
        )
        return jnp.where(allowed, raw_scores, MASKED)

    raw_scores = head_scores()
    row_max = jnp.max(raw_scores, axis=-1, keepdims=True)
    log_total = row_max + jnp.log(jnp.sum(jnp.exp(raw_scores - row_max), axis=-1, keepdims=True))
    weights_b = jnp.exp(raw_scores - log_total).astype(jnp.bfloat16)
    head_mixed = jnp.dot(weights_b, head_value, preferred_element_type=jnp.float32)
    mixed_b = own_heads(exchange(from_heads(head_mixed.astype(jnp.bfloat16)))).reshape(
        local_rows, HQ * HEAD_SIZE
    )
    residual_mid = input_f32 + jnp.dot(mixed_b, full_output, preferred_element_type=jnp.float32)
    gained_mid, second_normed, second_scale = rms_apply(residual_mid, second_gain)
    mlp_in = gained_mid.astype(jnp.bfloat16)
    gate_pre = jnp.dot(mlp_in, full_gate, preferred_element_type=jnp.float32)
    up_pre = jnp.dot(mlp_in, full_up, preferred_element_type=jnp.float32)
    sigmoid_gate = jax.nn.sigmoid(gate_pre)
    silu_gate = gate_pre * sigmoid_gate
    hidden = (silu_gate * up_pre).astype(jnp.bfloat16)
    layer_output = (
        residual_mid + jnp.dot(hidden, full_down, preferred_element_type=jnp.float32)
    ).astype(jnp.bfloat16)
    own_cotangent = cotangent[0]
    hidden_grad = right_dot(own_cotangent, full_down)
    gate_grad = (
        hidden_grad * up_pre * sigmoid_gate * (1.0 + gate_pre * (1.0 - sigmoid_gate))
    ).astype(jnp.bfloat16)
    up_grad = (hidden_grad * silu_gate).astype(jnp.bfloat16)
    mlp_in_grad = right_dot(gate_grad, full_gate) + right_dot(up_grad, full_up)
    second_gain_grad = jnp.sum(mlp_in_grad * second_normed, axis=0)
    mid_grad = own_cotangent.astype(jnp.float32) + root_mean_square_backward(
        mlp_in_grad, second_normed, second_scale, second_gain
    )
    mid_grad_b = mid_grad.astype(jnp.bfloat16)
    mixed_gradient = right_dot(mid_grad_b, full_output).astype(jnp.bfloat16)
    head_out_grad = gather_half(
        exchange(to_heads(mixed_gradient.reshape(local_rows, HQ, HEAD_SIZE)))
    )
    out_grad_f = head_out_grad.astype(jnp.float32)
    delta = jnp.sum(out_grad_f * head_mixed, axis=-1, keepdims=True)
    probabilities = jnp.exp(head_scores() - log_total)
    value_part = left_dot(probabilities.astype(jnp.bfloat16), head_out_grad)
    prob_grad = right_dot(head_out_grad, head_value)
    score_grad = (probabilities * (prob_grad - delta)).astype(jnp.bfloat16)
    query_part = jnp.dot(score_grad, head_key, preferred_element_type=jnp.float32) * scale_factor
    key_part = left_dot(score_grad, head_query) * scale_factor
    returned = exchange(jnp.concatenate([
        from_heads(query_part.astype(jnp.bfloat16)),
        jnp.concatenate([key_part, value_part], axis=-1).astype(jnp.bfloat16).reshape(
            ctx_size, local_rows, 2 * HEAD_SIZE),
    ], axis=-1))
    query_grad_rows = own_heads(returned[..., :HEAD_SIZE]).astype(jnp.float32)
    kv_parts = returned[..., HEAD_SIZE:].astype(jnp.float32).reshape(
        halves, KEY_VALUE_HEADS, group, local_rows, 2 * HEAD_SIZE)
    kv_grad = jnp.transpose(jnp.sum(kv_parts, axis=(0, 2)), (1, 0, 2))
    local_key_gradient = kv_grad[..., :HEAD_SIZE]
    own_value_grad = kv_grad[..., HEAD_SIZE:].reshape(local_rows, KEY_VALUE_HEADS * HEAD_SIZE)
    query_back = rotary_backward(query_grad_rows, cosine_table, sine_values_table)
    query_gain_grad = jnp.sum(query_back * query_normed, axis=(0, 1))
    query_pre_grad = (
        root_mean_square_backward(query_back, query_normed, query_scale, query_gain)
        .astype(jnp.bfloat16)
        .reshape(local_rows, HQ * HEAD_SIZE)
    )
    key_backward_pass = rotary_backward(
        local_key_gradient,
        cosine_table,
        sine_values_table,
    )
    key_gain_grad = jnp.sum(key_backward_pass * key_after_norm, axis=(0, 1))
    key_before_norm_gradient = (
        root_mean_square_backward(key_backward_pass, key_after_norm, key_norm_scale, key_norm_gain)
        .astype(jnp.bfloat16)
        .reshape(local_rows, KEY_VALUE_HEADS * HEAD_SIZE)
    )
    value_gradient_second = own_value_grad.astype(jnp.bfloat16)
    attn_in_grad = (
        right_dot(query_pre_grad, full_query)
        + right_dot(key_before_norm_gradient, full_key)
        + right_dot(value_gradient_second, full_value)
    )
    first_gain_grad = jnp.sum(attn_in_grad * first_normed, axis=0)
    input_grad = mid_grad + root_mean_square_backward(
        attn_in_grad, first_normed, first_scale, first_gain
    )
    attn_cols, mixed_cols, mlp_cols, hidden_cols = (
        lax.all_to_all(attention_input, "fsdp", split_axis=1, concat_axis=0, tiled=True),
        lax.all_to_all(mixed_b, "fsdp", split_axis=1, concat_axis=0, tiled=True),
        lax.all_to_all(mlp_in, "fsdp", split_axis=1, concat_axis=0, tiled=True),
        lax.all_to_all(hidden, "fsdp", split_axis=1, concat_axis=0, tiled=True),
    )
    cot_rows, gate_rows, up_rows, mid_rows, query_rows, key_rows, value_row_block = (
        lax.all_gather(own_cotangent, "fsdp", axis=0, tiled=True),
        lax.all_gather(gate_grad, "fsdp", axis=0, tiled=True),
        lax.all_gather(up_grad, "fsdp", axis=0, tiled=True),
        lax.all_gather(mid_grad_b, "fsdp", axis=0, tiled=True),
        lax.all_gather(query_pre_grad, "fsdp", axis=0, tiled=True),
        lax.all_gather(key_before_norm_gradient, "fsdp", axis=0, tiled=True),
        lax.all_gather(value_gradient_second, "fsdp", axis=0, tiled=True),
    )
    query_shard = left_dot(attn_cols, query_rows)
    key_shard = left_dot(attn_cols, key_rows)
    value_shard = left_dot(attn_cols, value_row_block)
    output_shard = left_dot(mixed_cols, mid_rows)
    gate_shard = left_dot(mlp_cols, gate_rows)
    up_shard = left_dot(mlp_cols, up_rows)
    down_shard = left_dot(hidden_cols, cot_rows)
    first_shard, second_shard, query_gain_shard, key_gain_shard = (
        lax.psum_scatter(first_gain_grad, "fsdp", scatter_dimension=0, tiled=True),
        lax.psum_scatter(second_gain_grad, "fsdp", scatter_dimension=0, tiled=True),
        lax.psum_scatter(query_gain_grad, "fsdp", scatter_dimension=0, tiled=True),
        lax.psum_scatter(key_gain_grad, "fsdp", scatter_dimension=0, tiled=True),
    )
    (
        query_total,
        key_total,
        value_total,
        output_total,
        gate_total,
        up_total,
        down_total,
        first_total,
        second_total,
        query_gain_total,
        key_gain_total,
    ) = (
        lax.psum(query_shard.astype(jnp.bfloat16), "ctx").astype(jnp.float32),
        lax.psum(key_shard.astype(jnp.bfloat16), "ctx").astype(jnp.float32),
        lax.psum(value_shard.astype(jnp.bfloat16), "ctx").astype(jnp.float32),
        lax.psum(output_shard.astype(jnp.bfloat16), "ctx").astype(jnp.float32),
        lax.psum(gate_shard.astype(jnp.bfloat16), "ctx").astype(jnp.float32),
        lax.psum(up_shard.astype(jnp.bfloat16), "ctx").astype(jnp.float32),
        lax.psum(down_shard.astype(jnp.bfloat16), "ctx").astype(jnp.float32),
        lax.psum(first_shard.astype(jnp.bfloat16), "ctx").astype(jnp.float32),
        lax.psum(second_shard.astype(jnp.bfloat16), "ctx").astype(jnp.float32),
        lax.psum(query_gain_shard.astype(jnp.bfloat16), "ctx").astype(jnp.float32),
        lax.psum(key_gain_shard.astype(jnp.bfloat16), "ctx").astype(jnp.float32),
    )
    return (
        layer_output[None],
        input_grad[None],
        query_total,
        key_total,
        value_total,
        output_total,
        gate_total,
        up_total,
        down_total,
        first_total,
        second_total,
        query_gain_total,
        key_gain_total,
    )


def solution(mesh):
    in_specs = (
        P("fsdp", "ctx", None),
        P("fsdp", "ctx", None),
        P("fsdp", None),
        P("fsdp", None),
        P("fsdp", None),
        P("fsdp", None),
        P("fsdp", None),
        P("fsdp", None),
        P("fsdp", None),
        P("fsdp", None),
        P(),
        P(),
        P(),
        P(),
    )
    out_specs = (
        P("fsdp", "ctx", None),
        P("fsdp", "ctx", None),
        P("fsdp", None),
        P("fsdp", None),
        P("fsdp", None),
        P("fsdp", None),
        P("fsdp", None),
        P("fsdp", None),
        P("fsdp", None),
        P("fsdp"),
        P("fsdp"),
        P("fsdp"),
        P("fsdp"),
    )
    return jax.shard_map(
        on_device, mesh=mesh, in_specs=in_specs, out_specs=out_specs, check_vma=False
    )
```

```python
import math

import jax
import jax.numpy as jnp
from jax import lax
from jax.sharding import PartitionSpec as P

HQ = 16
KEY_VALUE_HEADS = 8
HEAD_SIZE = 128
CTX = ("yh", "x", "z")
FSDP = ("yl", "c")


EPSILON = 1e-06
THETA = 1000000.0
MASKED = -1e30


def rms_apply(values, norm_gain):
    row_scale = lax.rsqrt(jnp.mean(values * values, axis=-1, keepdims=True) + EPSILON)
    normed = values * row_scale
    return (normed * norm_gain, normed, row_scale)


def root_mean_square_backward(gradient, normed, row_scale, norm_gain):
    normed_grad = gradient * norm_gain
    return row_scale * (
        normed_grad - normed * jnp.mean(normed_grad * normed, axis=-1, keepdims=True)
    )


def rope_tables(positions, head_width):
    half_width = head_width // 2
    inverse_freq = jnp.power(THETA, -2.0 * jnp.arange(half_width, dtype=jnp.float32) / head_width)
    angles = positions.astype(jnp.float32)[:, None] * inverse_freq[None, :]
    return (jnp.cos(angles)[:, None, :], jnp.sin(angles)[:, None, :])


def rotary_apply(values, cosine_table, sine_values_table):
    half_width = values.shape[-1] // 2
    front_half = values[..., :half_width]
    back_half = values[..., half_width:]
    return jnp.concatenate(
        [
            front_half * cosine_table - back_half * sine_values_table,
            back_half * cosine_table + front_half * sine_values_table,
        ],
        axis=-1,
    )


def rotary_backward(gradient, cosine_table, sine_values_table):
    half_width = gradient.shape[-1] // 2
    front_half = gradient[..., :half_width]
    back_half = gradient[..., half_width:]
    return jnp.concatenate(
        [
            front_half * cosine_table + back_half * sine_values_table,
            back_half * cosine_table - front_half * sine_values_table,
        ],
        axis=-1,
    )


def left_dot(left_side, right_side):
    return lax.dot_general(
        left_side, right_side, (((0,), (0,)), ((), ())), preferred_element_type=jnp.float32
    )


def right_dot(left_side, right_side):
    return lax.dot_general(
        left_side, right_side, (((1,), (1,)), ((), ())), preferred_element_type=jnp.float32
    )


def gather_fsdp(values):
    across = lax.all_gather(values, "yl", axis=0, tiled=False)
    both = lax.all_gather(across, "c", axis=1, tiled=False)
    return both.reshape((-1,) + values.shape[1:])


def reduce_ctx(shards):
    flat = jnp.concatenate([s.astype(jnp.bfloat16).reshape(-1) for s in shards])
    lanes = 128
    step = 256 * lanes
    padded = -(-flat.shape[0] // step) * step
    flat = jnp.pad(flat, (0, padded - flat.shape[0])).reshape(padded // lanes, lanes)
    part = lax.psum_scatter(flat, "z", scatter_dimension=0, tiled=True)
    part = lax.psum_scatter(part, "x", scatter_dimension=0, tiled=True)
    part = lax.psum(part, "yh")
    part = lax.all_gather(part, "x", axis=0, tiled=True)
    full = lax.all_gather(part, "z", axis=0, tiled=True).reshape(-1)
    out = []
    at = 0
    for s in shards:
        out.append(full[at : at + s.size].reshape(s.shape).astype(jnp.float32))
        at += s.size
    return tuple(out)


def on_device(
    layer_input,
    cotangent,
    block_order,
    query_weight,
    key_projection,
    value_projection,
    output_weight,
    gate_weight,
    up_weight,
    down_weight,
    first_gain,
    second_gain,
    query_gain,
    key_norm_gain,
):
    local_rows = layer_input.shape[1]
    block_rows = local_rows // 2
    ctx_size = lax.axis_size(CTX)
    halves = ctx_size // HQ
    half_devices = ctx_size // halves
    order_row = block_order[0]
    device_place = lax.axis_index(CTX)
    my_half = device_place // half_devices
    all_positions = (
        order_row[:, None] * block_rows + jnp.arange(block_rows, dtype=jnp.int32)[None, :]
    ).reshape(-1)
    own_positions = lax.dynamic_slice_in_dim(all_positions, device_place * local_rows, local_rows)
    cosine_table, sine_values_table = rope_tables(own_positions, HEAD_SIZE)
    scale_factor = 1.0 / math.sqrt(HEAD_SIZE)
    half_rows = half_devices * local_rows
    query_positions = lax.dynamic_slice_in_dim(all_positions, my_half * half_rows, half_rows)
    allowed = all_positions[None, :] <= query_positions[:, None]
    half_select = (jnp.arange(halves, dtype=jnp.int32) == my_half)[:, None, None, None]

    def to_heads(per_head):
        by_head = jnp.transpose(per_head, (1, 0, 2))
        return jnp.where(half_select, by_head[None], jnp.zeros_like(by_head)[None]).reshape(
            ctx_size, local_rows, per_head.shape[-1]
        )

    def gather_half(received):
        return lax.dynamic_slice_in_dim(received, my_half * half_devices, half_devices, 0).reshape(
            half_rows, received.shape[-1]
        )

    def from_heads(per_head):
        blocks = per_head.reshape(half_devices, local_rows, per_head.shape[-1])
        return jnp.where(half_select, blocks[None], jnp.zeros_like(blocks)[None]).reshape(
            ctx_size, local_rows, per_head.shape[-1]
        )

    def own_heads(received):
        mine = lax.dynamic_slice_in_dim(received, my_half * half_devices, half_devices, 0)
        return jnp.transpose(mine, (1, 0, 2))

    def exchange(values):
        return lax.all_to_all(values, CTX, split_axis=0, concat_axis=0, tiled=True)

    full_query, full_key, full_value, full_output, full_gate, full_up, full_down = (
        gather_fsdp(query_weight),
        gather_fsdp(key_projection),
        gather_fsdp(value_projection),
        gather_fsdp(output_weight),
        gather_fsdp(gate_weight),
        gather_fsdp(up_weight),
        gather_fsdp(down_weight),
    )
    input_f32 = layer_input[0].astype(jnp.float32)
    gained, first_normed, first_scale = rms_apply(input_f32, first_gain)
    attention_input = gained.astype(jnp.bfloat16)
    query_pre = jnp.dot(attention_input, full_query, preferred_element_type=jnp.float32).reshape(
        local_rows, HQ, HEAD_SIZE
    )
    query_gained, query_normed, query_scale = rms_apply(query_pre, query_gain)
    query_rotated = rotary_apply(query_gained, cosine_table, sine_values_table).astype(jnp.bfloat16)
    key_before_norm = jnp.dot(
        attention_input, full_key, preferred_element_type=jnp.float32
    ).reshape(local_rows, KEY_VALUE_HEADS, HEAD_SIZE)
    key_after_gain, key_after_norm, key_norm_scale = rms_apply(key_before_norm, key_norm_gain)
    own_keys = rotary_apply(key_after_gain, cosine_table, sine_values_table).astype(jnp.bfloat16)
    own_values = (
        jnp.dot(attention_input, full_value, preferred_element_type=jnp.float32)
        .astype(jnp.bfloat16)
        .reshape(local_rows, KEY_VALUE_HEADS, HEAD_SIZE)
    )
    group = HQ // KEY_VALUE_HEADS
    key_value = jnp.repeat(jnp.concatenate([own_keys, own_values], axis=-1), group, axis=1)
    sent = jnp.concatenate([to_heads(query_rotated), jnp.tile(
        jnp.transpose(key_value, (1, 0, 2)), (halves, 1, 1))], axis=-1)
    received = exchange(sent)
    head_query = gather_half(received[..., :HEAD_SIZE])
    head_key = received[..., HEAD_SIZE : 2 * HEAD_SIZE].reshape(-1, HEAD_SIZE)
    head_value = received[..., 2 * HEAD_SIZE :].reshape(-1, HEAD_SIZE)

    def head_scores():
        raw_scores = (
            jnp.einsum("qd,kd->qk", head_query, head_key, preferred_element_type=jnp.float32)
            * scale_factor
        )
        return jnp.where(allowed, raw_scores, MASKED)

    raw_scores = head_scores()
    row_max = jnp.max(raw_scores, axis=-1, keepdims=True)
    log_total = row_max + jnp.log(jnp.sum(jnp.exp(raw_scores - row_max), axis=-1, keepdims=True))
    weights_b = jnp.exp(raw_scores - log_total).astype(jnp.bfloat16)
    head_mixed = jnp.dot(weights_b, head_value, preferred_element_type=jnp.float32)
    mixed_b = own_heads(exchange(from_heads(head_mixed.astype(jnp.bfloat16)))).reshape(
        local_rows, HQ * HEAD_SIZE
    )
    residual_mid = input_f32 + jnp.dot(mixed_b, full_output, preferred_element_type=jnp.float32)
    gained_mid, second_normed, second_scale = rms_apply(residual_mid, second_gain)
    mlp_in = gained_mid.astype(jnp.bfloat16)
    gate_pre = jnp.dot(mlp_in, full_gate, preferred_element_type=jnp.float32)
    up_pre = jnp.dot(mlp_in, full_up, preferred_element_type=jnp.float32)
    sigmoid_gate = jax.nn.sigmoid(gate_pre)
    silu_gate = gate_pre * sigmoid_gate
    hidden = (silu_gate * up_pre).astype(jnp.bfloat16)
    layer_output = (
        residual_mid + jnp.dot(hidden, full_down, preferred_element_type=jnp.float32)
    ).astype(jnp.bfloat16)
    own_cotangent = cotangent[0]
    hidden_grad = right_dot(own_cotangent, full_down)
    gate_grad = (
        hidden_grad * up_pre * sigmoid_gate * (1.0 + gate_pre * (1.0 - sigmoid_gate))
    ).astype(jnp.bfloat16)
    up_grad = (hidden_grad * silu_gate).astype(jnp.bfloat16)
    mlp_in_grad = right_dot(gate_grad, full_gate) + right_dot(up_grad, full_up)
    second_gain_grad = jnp.sum(mlp_in_grad * second_normed, axis=0)
    mid_grad = own_cotangent.astype(jnp.float32) + root_mean_square_backward(
        mlp_in_grad, second_normed, second_scale, second_gain
    )
    mid_grad_b = mid_grad.astype(jnp.bfloat16)
    mixed_gradient = right_dot(mid_grad_b, full_output).astype(jnp.bfloat16)
    head_out_grad = gather_half(
        exchange(to_heads(mixed_gradient.reshape(local_rows, HQ, HEAD_SIZE)))
    )
    out_grad_f = head_out_grad.astype(jnp.float32)
    delta = jnp.sum(out_grad_f * head_mixed, axis=-1, keepdims=True)
    probabilities = jnp.exp(head_scores() - log_total)
    value_part = left_dot(probabilities.astype(jnp.bfloat16), head_out_grad)
    prob_grad = right_dot(head_out_grad, head_value)
    score_grad = (probabilities * (prob_grad - delta)).astype(jnp.bfloat16)
    query_part = jnp.dot(score_grad, head_key, preferred_element_type=jnp.float32) * scale_factor
    key_part = left_dot(score_grad, head_query) * scale_factor
    returned = exchange(jnp.concatenate([
        from_heads(query_part.astype(jnp.bfloat16)),
        jnp.concatenate([key_part, value_part], axis=-1).astype(jnp.bfloat16).reshape(
            ctx_size, local_rows, 2 * HEAD_SIZE),
    ], axis=-1))
    query_grad_rows = own_heads(returned[..., :HEAD_SIZE]).astype(jnp.float32)
    kv_parts = returned[..., HEAD_SIZE:].astype(jnp.float32).reshape(
        halves, KEY_VALUE_HEADS, group, local_rows, 2 * HEAD_SIZE)
    kv_grad = jnp.transpose(jnp.sum(kv_parts, axis=(0, 2)), (1, 0, 2))
    local_key_gradient = kv_grad[..., :HEAD_SIZE]
    own_value_grad = kv_grad[..., HEAD_SIZE:].reshape(local_rows, KEY_VALUE_HEADS * HEAD_SIZE)
    query_back = rotary_backward(query_grad_rows, cosine_table, sine_values_table)
    query_gain_grad = jnp.sum(query_back * query_normed, axis=(0, 1))
    query_pre_grad = (
        root_mean_square_backward(query_back, query_normed, query_scale, query_gain)
        .astype(jnp.bfloat16)
        .reshape(local_rows, HQ * HEAD_SIZE)
    )
    key_backward_pass = rotary_backward(
        local_key_gradient,
        cosine_table,
        sine_values_table,
    )
    key_gain_grad = jnp.sum(key_backward_pass * key_after_norm, axis=(0, 1))
    key_before_norm_gradient = (
        root_mean_square_backward(key_backward_pass, key_after_norm, key_norm_scale, key_norm_gain)
        .astype(jnp.bfloat16)
        .reshape(local_rows, KEY_VALUE_HEADS * HEAD_SIZE)
    )
    value_gradient_second = own_value_grad.astype(jnp.bfloat16)
    attn_in_grad = (
        right_dot(query_pre_grad, full_query)
        + right_dot(key_before_norm_gradient, full_key)
        + right_dot(value_gradient_second, full_value)
    )
    first_gain_grad = jnp.sum(attn_in_grad * first_normed, axis=0)
    input_grad = mid_grad + root_mean_square_backward(
        attn_in_grad, first_normed, first_scale, first_gain
    )
    attn_cols, mixed_cols, mlp_cols, hidden_cols = (
        lax.all_to_all(attention_input, FSDP, split_axis=1, concat_axis=0, tiled=True),
        lax.all_to_all(mixed_b, FSDP, split_axis=1, concat_axis=0, tiled=True),
        lax.all_to_all(mlp_in, FSDP, split_axis=1, concat_axis=0, tiled=True),
        lax.all_to_all(hidden, FSDP, split_axis=1, concat_axis=0, tiled=True),
    )
    cot_rows, gate_rows, up_rows, mid_rows, query_rows, key_rows, value_row_block = (
        gather_fsdp(own_cotangent),
        gather_fsdp(gate_grad),
        gather_fsdp(up_grad),
        gather_fsdp(mid_grad_b),
        gather_fsdp(query_pre_grad),
        gather_fsdp(key_before_norm_gradient),
        gather_fsdp(value_gradient_second),
    )
    query_shard = left_dot(attn_cols, query_rows)
    key_shard = left_dot(attn_cols, key_rows)
    value_shard = left_dot(attn_cols, value_row_block)
    output_shard = left_dot(mixed_cols, mid_rows)
    gate_shard = left_dot(mlp_cols, gate_rows)
    up_shard = left_dot(mlp_cols, up_rows)
    down_shard = left_dot(hidden_cols, cot_rows)
    first_shard, second_shard, query_gain_shard, key_gain_shard = (
        lax.psum_scatter(first_gain_grad, FSDP, scatter_dimension=0, tiled=True),
        lax.psum_scatter(second_gain_grad, FSDP, scatter_dimension=0, tiled=True),
        lax.psum_scatter(query_gain_grad, FSDP, scatter_dimension=0, tiled=True),
        lax.psum_scatter(key_gain_grad, FSDP, scatter_dimension=0, tiled=True),
    )
    shards = (query_shard, key_shard, value_shard, output_shard, gate_shard, up_shard, down_shard,
              first_shard, second_shard, query_gain_shard, key_gain_shard)
    totals = reduce_ctx(shards)
    (
        query_total,
        key_total,
        value_total,
        output_total,
        gate_total,
        up_total,
        down_total,
        first_total,
        second_total,
        query_gain_total,
        key_gain_total,
    ) = totals
    return (
        layer_output[None],
        input_grad[None],
        query_total,
        key_total,
        value_total,
        output_total,
        gate_total,
        up_total,
        down_total,
        first_total,
        second_total,
        query_gain_total,
        key_gain_total,
    )


def solution(mesh):
    in_specs = (
        P(FSDP, CTX, None),
        P(FSDP, CTX, None),
        P(FSDP, None),
        P(FSDP, None),
        P(FSDP, None),
        P(FSDP, None),
        P(FSDP, None),
        P(FSDP, None),
        P(FSDP, None),
        P(FSDP, None),
        P(),
        P(),
        P(),
        P(),
    )
    out_specs = (
        P(FSDP, CTX, None),
        P(FSDP, CTX, None),
        P(FSDP, None),
        P(FSDP, None),
        P(FSDP, None),
        P(FSDP, None),
        P(FSDP, None),
        P(FSDP, None),
        P(FSDP, None),
        P(FSDP),
        P(FSDP),
        P(FSDP),
        P(FSDP),
    )
    torus_mesh = jax.sharding.Mesh(mesh.devices.reshape(2, 4, 4, 2, 2), ("yh", "x", "z", "yl", "c"))
    return jax.shard_map(
        on_device, mesh=torus_mesh, in_specs=in_specs, out_specs=out_specs, check_vma=False
    )
```

```python
import math

import jax
import jax.numpy as jnp
from jax import lax
from jax.sharding import PartitionSpec as P

HQ = 16
KEY_VALUE_HEADS = 8
HEAD_SIZE = 128
CTX = ("yh", "x", "z")
FSDP = ("yl", "c")


EPSILON = 1e-06
THETA = 1000000.0
MASKED = -1e30


def rms_apply(values, norm_gain):
    row_scale = lax.rsqrt(jnp.mean(values * values, axis=-1, keepdims=True) + EPSILON)
    normed = values * row_scale
    return (normed * norm_gain, normed, row_scale)


def root_mean_square_backward(gradient, normed, row_scale, norm_gain):
    normed_grad = gradient * norm_gain
    return row_scale * (
        normed_grad - normed * jnp.mean(normed_grad * normed, axis=-1, keepdims=True)
    )


def rope_tables(positions, head_width):
    half_width = head_width // 2
    inverse_freq = jnp.power(THETA, -2.0 * jnp.arange(half_width, dtype=jnp.float32) / head_width)
    angles = positions.astype(jnp.float32)[:, None] * inverse_freq[None, :]
    return (jnp.cos(angles)[:, None, :], jnp.sin(angles)[:, None, :])


def rotary_apply(values, cosine_table, sine_values_table):
    half_width = values.shape[-1] // 2
    front_half = values[..., :half_width]
    back_half = values[..., half_width:]
    return jnp.concatenate(
        [
            front_half * cosine_table - back_half * sine_values_table,
            back_half * cosine_table + front_half * sine_values_table,
        ],
        axis=-1,
    )


def rotary_backward(gradient, cosine_table, sine_values_table):
    half_width = gradient.shape[-1] // 2
    front_half = gradient[..., :half_width]
    back_half = gradient[..., half_width:]
    return jnp.concatenate(
        [
            front_half * cosine_table + back_half * sine_values_table,
            back_half * cosine_table - front_half * sine_values_table,
        ],
        axis=-1,
    )


def left_dot(left_side, right_side):
    return lax.dot_general(
        left_side, right_side, (((0,), (0,)), ((), ())), preferred_element_type=jnp.float32
    )


def right_dot(left_side, right_side):
    return lax.dot_general(
        left_side, right_side, (((1,), (1,)), ((), ())), preferred_element_type=jnp.float32
    )


def gather_fsdp(values):
    across = lax.all_gather(values, "yl", axis=0, tiled=False)
    both = lax.all_gather(across, "c", axis=1, tiled=False)
    return both.reshape((-1,) + values.shape[1:])


def reduce_ctx(packed):
    part = lax.psum_scatter(packed, "z", scatter_dimension=0, tiled=True)
    part = lax.psum_scatter(part, "x", scatter_dimension=0, tiled=True)
    part = lax.psum(part, "yh")
    part = lax.all_gather(part, "x", axis=0, tiled=True)
    return lax.all_gather(part, "z", axis=0, tiled=True).astype(jnp.float32)


def on_device(
    layer_input,
    cotangent,
    block_order,
    query_weight,
    key_projection,
    value_projection,
    output_weight,
    gate_weight,
    up_weight,
    down_weight,
    first_gain,
    second_gain,
    query_gain,
    key_norm_gain,
):
    local_rows = layer_input.shape[1]
    block_rows = local_rows // 2
    ctx_size = lax.axis_size(CTX)
    halves = ctx_size // HQ
    half_devices = ctx_size // halves
    order_row = block_order[0]
    device_place = lax.axis_index(CTX)
    my_half = device_place // half_devices
    all_positions = (
        order_row[:, None] * block_rows + jnp.arange(block_rows, dtype=jnp.int32)[None, :]
    ).reshape(-1)
    own_positions = lax.dynamic_slice_in_dim(all_positions, device_place * local_rows, local_rows)
    cosine_table, sine_values_table = rope_tables(own_positions, HEAD_SIZE)
    scale_factor = 1.0 / math.sqrt(HEAD_SIZE)
    half_rows = half_devices * local_rows
    query_positions = lax.dynamic_slice_in_dim(all_positions, my_half * half_rows, half_rows)
    allowed = all_positions[None, :] <= query_positions[:, None]
    half_select = (jnp.arange(halves, dtype=jnp.int32) == my_half)[:, None, None, None]

    def to_heads(per_head):
        by_head = jnp.transpose(per_head, (1, 0, 2))
        return jnp.where(half_select, by_head[None], jnp.zeros_like(by_head)[None]).reshape(
            ctx_size, local_rows, per_head.shape[-1]
        )

    def gather_half(received):
        return lax.dynamic_slice_in_dim(received, my_half * half_devices, half_devices, 0).reshape(
            half_rows, received.shape[-1]
        )

    def from_heads(per_head):
        blocks = per_head.reshape(half_devices, local_rows, per_head.shape[-1])
        return jnp.where(half_select, blocks[None], jnp.zeros_like(blocks)[None]).reshape(
            ctx_size, local_rows, per_head.shape[-1]
        )

    def own_heads(received):
        mine = lax.dynamic_slice_in_dim(received, my_half * half_devices, half_devices, 0)
        return jnp.transpose(mine, (1, 0, 2))

    def exchange(values):
        return lax.all_to_all(values, CTX, split_axis=0, concat_axis=0, tiled=True)

    qkv_cols = (query_weight.shape[1], key_projection.shape[1], value_projection.shape[1])
    full_qkv = lax.all_gather(
        jnp.concatenate([query_weight, key_projection, value_projection], axis=1), FSDP, axis=0, tiled=True
    )
    full_output = lax.all_gather(output_weight, FSDP, axis=0, tiled=True)
    ff_cols = gate_weight.shape[1]
    full_gate_up = lax.all_gather(
        jnp.concatenate([gate_weight, up_weight], axis=1), FSDP, axis=0, tiled=True
    )
    full_down = lax.all_gather(down_weight, FSDP, axis=0, tiled=True)
    input_f32 = layer_input[0].astype(jnp.float32)
    gained, first_normed, first_scale = rms_apply(input_f32, first_gain)
    attention_input = gained.astype(jnp.bfloat16)
    qkv_pre = jnp.dot(attention_input, full_qkv, preferred_element_type=jnp.float32)
    query_pre = qkv_pre[:, : qkv_cols[0]].reshape(local_rows, HQ, HEAD_SIZE)
    query_gained, query_normed, query_scale = rms_apply(query_pre, query_gain)
    query_rotated = rotary_apply(query_gained, cosine_table, sine_values_table).astype(jnp.bfloat16)
    key_before_norm = qkv_pre[:, qkv_cols[0] : qkv_cols[0] + qkv_cols[1]].reshape(
        local_rows, KEY_VALUE_HEADS, HEAD_SIZE
    )
    key_after_gain, key_after_norm, key_norm_scale = rms_apply(key_before_norm, key_norm_gain)
    own_keys = rotary_apply(key_after_gain, cosine_table, sine_values_table).astype(jnp.bfloat16)
    own_values = (
        qkv_pre[:, qkv_cols[0] + qkv_cols[1] :]
        .astype(jnp.bfloat16)
        .reshape(local_rows, KEY_VALUE_HEADS, HEAD_SIZE)
    )
    group = HQ // KEY_VALUE_HEADS
    key_value = jnp.repeat(jnp.concatenate([own_keys, own_values], axis=-1), group, axis=1)
    sent = jnp.concatenate([to_heads(query_rotated), jnp.tile(
        jnp.transpose(key_value, (1, 0, 2)), (halves, 1, 1))], axis=-1)
    received = exchange(sent)
    head_query = gather_half(received[..., :HEAD_SIZE])
    head_key = received[..., HEAD_SIZE : 2 * HEAD_SIZE].reshape(-1, HEAD_SIZE)
    head_value = received[..., 2 * HEAD_SIZE :].reshape(-1, HEAD_SIZE)

    def head_scores():
        raw_scores = (
            jnp.einsum("qd,kd->qk", head_query, head_key, preferred_element_type=jnp.float32)
            * scale_factor
        )
        return jnp.where(allowed, raw_scores, MASKED)

    raw_scores = head_scores()
    row_max = jnp.max(raw_scores, axis=-1, keepdims=True)
    log_total = row_max + jnp.log(jnp.sum(jnp.exp(raw_scores - row_max), axis=-1, keepdims=True))
    weights_b = jnp.exp(raw_scores - log_total).astype(jnp.bfloat16)
    head_mixed = jnp.dot(weights_b, head_value, preferred_element_type=jnp.float32)
    mixed_b = own_heads(exchange(from_heads(head_mixed.astype(jnp.bfloat16)))).reshape(
        local_rows, HQ * HEAD_SIZE
    )
    residual_mid = input_f32 + jnp.dot(mixed_b, full_output, preferred_element_type=jnp.float32)
    gained_mid, second_normed, second_scale = rms_apply(residual_mid, second_gain)
    mlp_in = gained_mid.astype(jnp.bfloat16)
    gate_up_pre = jnp.dot(mlp_in, full_gate_up, preferred_element_type=jnp.float32)
    gate_pre = gate_up_pre[:, :ff_cols]
    up_pre = gate_up_pre[:, ff_cols:]
    sigmoid_gate = jax.nn.sigmoid(gate_pre)
    silu_gate = gate_pre * sigmoid_gate
    hidden = (silu_gate * up_pre).astype(jnp.bfloat16)
    layer_output = (
        residual_mid + jnp.dot(hidden, full_down, preferred_element_type=jnp.float32)
    ).astype(jnp.bfloat16)
    own_cotangent = cotangent[0]
    hidden_grad = right_dot(own_cotangent, full_down)
    gate_grad = (
        hidden_grad * up_pre * sigmoid_gate * (1.0 + gate_pre * (1.0 - sigmoid_gate))
    ).astype(jnp.bfloat16)
    up_grad = (hidden_grad * silu_gate).astype(jnp.bfloat16)
    gate_up_grad = jnp.concatenate([gate_grad, up_grad], axis=1)
    mlp_in_grad = right_dot(gate_up_grad, full_gate_up)
    second_gain_grad = jnp.sum(mlp_in_grad * second_normed, axis=0)
    mid_grad = own_cotangent.astype(jnp.float32) + root_mean_square_backward(
        mlp_in_grad, second_normed, second_scale, second_gain
    )
    mid_grad_b = mid_grad.astype(jnp.bfloat16)
    mixed_gradient = right_dot(mid_grad_b, full_output).astype(jnp.bfloat16)
    head_out_grad = gather_half(
        exchange(to_heads(mixed_gradient.reshape(local_rows, HQ, HEAD_SIZE)))
    )
    out_grad_f = head_out_grad.astype(jnp.float32)
    delta = jnp.sum(out_grad_f * head_mixed, axis=-1, keepdims=True)
    probabilities = jnp.exp(head_scores() - log_total)
    value_part = left_dot(probabilities.astype(jnp.bfloat16), head_out_grad)
    prob_grad = right_dot(head_out_grad, head_value)
    score_grad = (probabilities * (prob_grad - delta)).astype(jnp.bfloat16)
    query_part = jnp.dot(score_grad, head_key, preferred_element_type=jnp.float32) * scale_factor
    key_part = left_dot(score_grad, head_query) * scale_factor
    returned = exchange(jnp.concatenate([
        from_heads(query_part.astype(jnp.bfloat16)),
        jnp.concatenate([key_part, value_part], axis=-1).astype(jnp.bfloat16).reshape(
            ctx_size, local_rows, 2 * HEAD_SIZE),
    ], axis=-1))
    query_grad_rows = own_heads(returned[..., :HEAD_SIZE]).astype(jnp.float32)
    kv_parts = returned[..., HEAD_SIZE:].astype(jnp.float32).reshape(
        halves, KEY_VALUE_HEADS, group, local_rows, 2 * HEAD_SIZE)
    kv_grad = jnp.transpose(jnp.sum(kv_parts, axis=(0, 2)), (1, 0, 2))
    local_key_gradient = kv_grad[..., :HEAD_SIZE]
    own_value_grad = kv_grad[..., HEAD_SIZE:].reshape(local_rows, KEY_VALUE_HEADS * HEAD_SIZE)
    query_back = rotary_backward(query_grad_rows, cosine_table, sine_values_table)
    query_gain_grad = jnp.sum(query_back * query_normed, axis=(0, 1))
    query_pre_grad = (
        root_mean_square_backward(query_back, query_normed, query_scale, query_gain)
        .astype(jnp.bfloat16)
        .reshape(local_rows, HQ * HEAD_SIZE)
    )
    key_backward_pass = rotary_backward(
        local_key_gradient,
        cosine_table,
        sine_values_table,
    )
    key_gain_grad = jnp.sum(key_backward_pass * key_after_norm, axis=(0, 1))
    key_before_norm_gradient = (
        root_mean_square_backward(key_backward_pass, key_after_norm, key_norm_scale, key_norm_gain)
        .astype(jnp.bfloat16)
        .reshape(local_rows, KEY_VALUE_HEADS * HEAD_SIZE)
    )
    value_gradient_second = own_value_grad.astype(jnp.bfloat16)
    qkv_grad = jnp.concatenate([query_pre_grad, key_before_norm_gradient, value_gradient_second], axis=1)
    attn_in_grad = (
        right_dot(qkv_grad, full_qkv)
    )
    first_gain_grad = jnp.sum(attn_in_grad * first_normed, axis=0)
    input_grad = mid_grad + root_mean_square_backward(
        attn_in_grad, first_normed, first_scale, first_gain
    )
    fsdp_size = lax.axis_size(FSDP)
    col_parts = (attention_input, mixed_b, mlp_in, hidden)
    widths = [p.shape[1] // fsdp_size for p in col_parts]
    stacked = jnp.concatenate(
        [p.reshape(local_rows, fsdp_size, w) for p, w in zip(col_parts, widths)], axis=2
    )
    cols = lax.all_to_all(stacked, FSDP, split_axis=1, concat_axis=0, tiled=True).reshape(
        fsdp_size * local_rows, sum(widths)
    )
    bounds = [sum(widths[:i]) for i in range(5)]
    attn_cols, mixed_cols, mlp_cols, hidden_cols = (
        cols[:, bounds[i] : bounds[i + 1]] for i in range(4)
    )
    qkv_rows = lax.all_gather(qkv_grad, FSDP, axis=0, tiled=True)
    gate_up_rows = lax.all_gather(gate_up_grad, FSDP, axis=0, tiled=True)
    cot_mid_rows = lax.all_gather(
        jnp.concatenate([own_cotangent, mid_grad_b], axis=1), FSDP, axis=0, tiled=True
    )
    model_width = own_cotangent.shape[1]
    qkv_shard = left_dot(attn_cols, qkv_rows)
    output_shard = left_dot(mixed_cols, cot_mid_rows[:, model_width:])
    gate_up_shard = left_dot(mlp_cols, gate_up_rows)
    down_shard = left_dot(hidden_cols, cot_mid_rows[:, :model_width])
    shard_rows = qkv_shard.shape[0]
    packed = jnp.concatenate(
        [
            qkv_shard,
            output_shard.reshape(shard_rows, -1),
            gate_up_shard,
            down_shard.reshape(shard_rows, -1),
        ],
        axis=1,
    ).astype(jnp.bfloat16)
    reduced = reduce_ctx(packed)
    pieces = []
    at = 0
    for width in (qkv_cols[0], qkv_cols[1], qkv_cols[2], output_shard.size // shard_rows, ff_cols, ff_cols,
                  down_shard.size // shard_rows):
        pieces.append(reduced[:, at : at + width])
        at += width
    query_total, key_total, value_total, output_total, gate_total, up_total, down_total = pieces
    output_total = output_total.reshape(output_shard.shape)
    down_total = down_total.reshape(down_shard.shape)
    first_shard, second_shard, query_gain_shard, key_gain_shard = (
        lax.psum_scatter(first_gain_grad, FSDP, scatter_dimension=0, tiled=True),
        lax.psum_scatter(second_gain_grad, FSDP, scatter_dimension=0, tiled=True),
        lax.psum_scatter(query_gain_grad, FSDP, scatter_dimension=0, tiled=True),
        lax.psum_scatter(key_gain_grad, FSDP, scatter_dimension=0, tiled=True),
    )
    first_total, second_total, query_gain_total, key_gain_total = (
        lax.psum(g.astype(jnp.bfloat16), CTX).astype(jnp.float32)
        for g in (first_shard, second_shard, query_gain_shard, key_gain_shard)
    )
    return (
        layer_output[None],
        input_grad[None],
        query_total,
        key_total,
        value_total,
        output_total,
        gate_total,
        up_total,
        down_total,
        first_total,
        second_total,
        query_gain_total,
        key_gain_total,
    )


def solution(mesh):
    in_specs = (
        P(FSDP, CTX, None),
        P(FSDP, CTX, None),
        P(FSDP, None),
        P(FSDP, None),
        P(FSDP, None),
        P(FSDP, None),
        P(FSDP, None),
        P(FSDP, None),
        P(FSDP, None),
        P(FSDP, None),
        P(),
        P(),
        P(),
        P(),
    )
    out_specs = (
        P(FSDP, CTX, None),
        P(FSDP, CTX, None),
        P(FSDP, None),
        P(FSDP, None),
        P(FSDP, None),
        P(FSDP, None),
        P(FSDP, None),
        P(FSDP, None),
        P(FSDP, None),
        P(FSDP),
        P(FSDP),
        P(FSDP),
        P(FSDP),
    )
    torus_mesh = jax.sharding.Mesh(mesh.devices.reshape(2, 4, 4, 2, 2), ("yh", "x", "z", "yl", "c"))
    return jax.shard_map(
        on_device, mesh=torus_mesh, in_specs=in_specs, out_specs=out_specs, check_vma=False
    )
```

```python
import math

import jax
import jax.numpy as jnp
from jax import lax
from jax.sharding import PartitionSpec as P

HQ = 16
KEY_VALUE_HEADS = 8
HEAD_SIZE = 128
CTX = ("yh", "x", "z")
FSDP = ("yl", "c")


EPSILON = 1e-06
THETA = 1000000.0
MASKED = -1e30


def rms_apply(values, norm_gain):
    row_scale = lax.rsqrt(jnp.mean(values * values, axis=-1, keepdims=True) + EPSILON)
    normed = values * row_scale
    return (normed * norm_gain, normed, row_scale)


def root_mean_square_backward(gradient, normed, row_scale, norm_gain):
    normed_grad = gradient * norm_gain
    return row_scale * (
        normed_grad - normed * jnp.mean(normed_grad * normed, axis=-1, keepdims=True)
    )


def rope_tables(positions, head_width):
    half_width = head_width // 2
    inverse_freq = jnp.power(THETA, -2.0 * jnp.arange(half_width, dtype=jnp.float32) / head_width)
    angles = positions.astype(jnp.float32)[:, None] * inverse_freq[None, :]
    return (jnp.cos(angles)[:, None, :], jnp.sin(angles)[:, None, :])


def rotary_apply(values, cosine_table, sine_values_table):
    half_width = values.shape[-1] // 2
    front_half = values[..., :half_width]
    back_half = values[..., half_width:]
    return jnp.concatenate(
        [
            front_half * cosine_table - back_half * sine_values_table,
            back_half * cosine_table + front_half * sine_values_table,
        ],
        axis=-1,
    )


def rotary_backward(gradient, cosine_table, sine_values_table):
    half_width = gradient.shape[-1] // 2
    front_half = gradient[..., :half_width]
    back_half = gradient[..., half_width:]
    return jnp.concatenate(
        [
            front_half * cosine_table + back_half * sine_values_table,
            back_half * cosine_table - front_half * sine_values_table,
        ],
        axis=-1,
    )


def left_dot(left_side, right_side):
    return lax.dot_general(
        left_side, right_side, (((0,), (0,)), ((), ())), preferred_element_type=jnp.float32
    )


def right_dot(left_side, right_side):
    return lax.dot_general(
        left_side, right_side, (((1,), (1,)), ((), ())), preferred_element_type=jnp.float32
    )


def gather_fsdp(values):
    across = lax.all_gather(values, "yl", axis=0, tiled=False)
    both = lax.all_gather(across, "c", axis=1, tiled=False)
    return both.reshape((-1,) + values.shape[1:])


def permute_gather(values):
    size = lax.axis_size(FSDP)
    me = lax.axis_index(FSDP)
    received = [values]
    for s in range(1, size):
        pairs = [(i, i ^ s) for i in range(size)]
        received.append(lax.ppermute(values, FSDP, pairs))
    stacked = jnp.stack(received)
    ordered = [lax.dynamic_index_in_dim(stacked, me ^ j, 0, False) for j in range(size)]
    return jnp.concatenate(ordered, axis=0)


def reduce_ctx(packed):
    part = lax.psum_scatter(packed, "z", scatter_dimension=0, tiled=True)
    part = lax.psum_scatter(part, "x", scatter_dimension=0, tiled=True)
    part = lax.psum(part, "yh")
    part = lax.all_gather(part, "x", axis=0, tiled=True)
    return lax.all_gather(part, "z", axis=0, tiled=True).astype(jnp.float32)


def on_device(
    layer_input,
    cotangent,
    block_order,
    query_weight,
    key_projection,
    value_projection,
    output_weight,
    gate_weight,
    up_weight,
    down_weight,
    first_gain,
    second_gain,
    query_gain,
    key_norm_gain,
):
    local_rows = layer_input.shape[1]
    block_rows = local_rows // 2
    ctx_size = lax.axis_size(CTX)
    halves = ctx_size // HQ
    half_devices = ctx_size // halves
    order_row = block_order[0]
    device_place = lax.axis_index(CTX)
    my_half = device_place // half_devices
    all_positions = (
        order_row[:, None] * block_rows + jnp.arange(block_rows, dtype=jnp.int32)[None, :]
    ).reshape(-1)
    own_positions = lax.dynamic_slice_in_dim(all_positions, device_place * local_rows, local_rows)
    cosine_table, sine_values_table = rope_tables(own_positions, HEAD_SIZE)
    scale_factor = 1.0 / math.sqrt(HEAD_SIZE)
    half_rows = half_devices * local_rows
    query_positions = lax.dynamic_slice_in_dim(all_positions, my_half * half_rows, half_rows)
    allowed = all_positions[None, :] <= query_positions[:, None]
    half_select = (jnp.arange(halves, dtype=jnp.int32) == my_half)[:, None, None, None]

    def to_heads(per_head):
        by_head = jnp.transpose(per_head, (1, 0, 2))
        return jnp.where(half_select, by_head[None], jnp.zeros_like(by_head)[None]).reshape(
            ctx_size, local_rows, per_head.shape[-1]
        )

    def gather_half(received):
        return lax.dynamic_slice_in_dim(received, my_half * half_devices, half_devices, 0).reshape(
            half_rows, received.shape[-1]
        )

    def from_heads(per_head):
        blocks = per_head.reshape(half_devices, local_rows, per_head.shape[-1])
        return jnp.where(half_select, blocks[None], jnp.zeros_like(blocks)[None]).reshape(
            ctx_size, local_rows, per_head.shape[-1]
        )

    def own_heads(received):
        mine = lax.dynamic_slice_in_dim(received, my_half * half_devices, half_devices, 0)
        return jnp.transpose(mine, (1, 0, 2))

    def exchange(values):
        return lax.all_to_all(values, CTX, split_axis=0, concat_axis=0, tiled=True)

    qkv_cols = (query_weight.shape[1], key_projection.shape[1], value_projection.shape[1])
    full_qkv = lax.all_gather(
        jnp.concatenate([query_weight, key_projection, value_projection], axis=1), FSDP, axis=0, tiled=True
    )
    full_output = permute_gather(output_weight)
    ff_cols = gate_weight.shape[1]
    full_gate_up = lax.all_gather(
        jnp.concatenate([gate_weight, up_weight], axis=1), FSDP, axis=0, tiled=True
    )
    full_down = permute_gather(down_weight)
    input_f32 = layer_input[0].astype(jnp.float32)
    gained, first_normed, first_scale = rms_apply(input_f32, first_gain)
    attention_input = gained.astype(jnp.bfloat16)
    qkv_pre = jnp.dot(attention_input, full_qkv, preferred_element_type=jnp.float32)
    query_pre = qkv_pre[:, : qkv_cols[0]].reshape(local_rows, HQ, HEAD_SIZE)
    query_gained, query_normed, query_scale = rms_apply(query_pre, query_gain)
    query_rotated = rotary_apply(query_gained, cosine_table, sine_values_table).astype(jnp.bfloat16)
    key_before_norm = qkv_pre[:, qkv_cols[0] : qkv_cols[0] + qkv_cols[1]].reshape(
        local_rows, KEY_VALUE_HEADS, HEAD_SIZE
    )
    key_after_gain, key_after_norm, key_norm_scale = rms_apply(key_before_norm, key_norm_gain)
    own_keys = rotary_apply(key_after_gain, cosine_table, sine_values_table).astype(jnp.bfloat16)
    own_values = (
        qkv_pre[:, qkv_cols[0] + qkv_cols[1] :]
        .astype(jnp.bfloat16)
        .reshape(local_rows, KEY_VALUE_HEADS, HEAD_SIZE)
    )
    group = HQ // KEY_VALUE_HEADS
    key_value = jnp.repeat(jnp.concatenate([own_keys, own_values], axis=-1), group, axis=1)
    sent = jnp.concatenate([to_heads(query_rotated), jnp.tile(
        jnp.transpose(key_value, (1, 0, 2)), (halves, 1, 1))], axis=-1)
    received = exchange(sent)
    head_query = gather_half(received[..., :HEAD_SIZE])
    head_key = received[..., HEAD_SIZE : 2 * HEAD_SIZE].reshape(-1, HEAD_SIZE)
    head_value = received[..., 2 * HEAD_SIZE :].reshape(-1, HEAD_SIZE)

    def head_scores():
        raw_scores = (
            jnp.einsum("qd,kd->qk", head_query, head_key, preferred_element_type=jnp.float32)
            * scale_factor
        )
        return jnp.where(allowed, raw_scores, MASKED)

    raw_scores = head_scores()
    row_max = jnp.max(raw_scores, axis=-1, keepdims=True)
    log_total = row_max + jnp.log(jnp.sum(jnp.exp(raw_scores - row_max), axis=-1, keepdims=True))
    weights_b = jnp.exp(raw_scores - log_total).astype(jnp.bfloat16)
    head_mixed = jnp.dot(weights_b, head_value, preferred_element_type=jnp.float32)
    mixed_b = own_heads(exchange(from_heads(head_mixed.astype(jnp.bfloat16)))).reshape(
        local_rows, HQ * HEAD_SIZE
    )
    residual_mid = input_f32 + jnp.dot(mixed_b, full_output, preferred_element_type=jnp.float32)
    gained_mid, second_normed, second_scale = rms_apply(residual_mid, second_gain)
    mlp_in = gained_mid.astype(jnp.bfloat16)
    gate_up_pre = jnp.dot(mlp_in, full_gate_up, preferred_element_type=jnp.float32)
    gate_pre = gate_up_pre[:, :ff_cols]
    up_pre = gate_up_pre[:, ff_cols:]
    sigmoid_gate = jax.nn.sigmoid(gate_pre)
    silu_gate = gate_pre * sigmoid_gate
    hidden = (silu_gate * up_pre).astype(jnp.bfloat16)
    layer_output = (
        residual_mid + jnp.dot(hidden, full_down, preferred_element_type=jnp.float32)
    ).astype(jnp.bfloat16)
    own_cotangent = cotangent[0]
    hidden_grad = right_dot(own_cotangent, full_down)
    gate_grad = (
        hidden_grad * up_pre * sigmoid_gate * (1.0 + gate_pre * (1.0 - sigmoid_gate))
    ).astype(jnp.bfloat16)
    up_grad = (hidden_grad * silu_gate).astype(jnp.bfloat16)
    gate_up_grad = jnp.concatenate([gate_grad, up_grad], axis=1)
    mlp_in_grad = right_dot(gate_up_grad, full_gate_up)
    second_gain_grad = jnp.sum(mlp_in_grad * second_normed, axis=0)
    mid_grad = own_cotangent.astype(jnp.float32) + root_mean_square_backward(
        mlp_in_grad, second_normed, second_scale, second_gain
    )
    mid_grad_b = mid_grad.astype(jnp.bfloat16)
    mixed_gradient = right_dot(mid_grad_b, full_output).astype(jnp.bfloat16)
    head_out_grad = gather_half(
        exchange(to_heads(mixed_gradient.reshape(local_rows, HQ, HEAD_SIZE)))
    )
    out_grad_f = head_out_grad.astype(jnp.float32)
    delta = jnp.sum(out_grad_f * head_mixed, axis=-1, keepdims=True)
    probabilities = jnp.exp(head_scores() - log_total)
    value_part = left_dot(probabilities.astype(jnp.bfloat16), head_out_grad)
    prob_grad = right_dot(head_out_grad, head_value)
    score_grad = (probabilities * (prob_grad - delta)).astype(jnp.bfloat16)
    query_part = jnp.dot(score_grad, head_key, preferred_element_type=jnp.float32) * scale_factor
    key_part = left_dot(score_grad, head_query) * scale_factor
    returned = exchange(jnp.concatenate([
        from_heads(query_part.astype(jnp.bfloat16)),
        jnp.concatenate([key_part, value_part], axis=-1).astype(jnp.bfloat16).reshape(
            ctx_size, local_rows, 2 * HEAD_SIZE),
    ], axis=-1))
    query_grad_rows = own_heads(returned[..., :HEAD_SIZE]).astype(jnp.float32)
    kv_parts = returned[..., HEAD_SIZE:].astype(jnp.float32).reshape(
        halves, KEY_VALUE_HEADS, group, local_rows, 2 * HEAD_SIZE)
    kv_grad = jnp.transpose(jnp.sum(kv_parts, axis=(0, 2)), (1, 0, 2))
    local_key_gradient = kv_grad[..., :HEAD_SIZE]
    own_value_grad = kv_grad[..., HEAD_SIZE:].reshape(local_rows, KEY_VALUE_HEADS * HEAD_SIZE)
    query_back = rotary_backward(query_grad_rows, cosine_table, sine_values_table)
    query_gain_grad = jnp.sum(query_back * query_normed, axis=(0, 1))
    query_pre_grad = (
        root_mean_square_backward(query_back, query_normed, query_scale, query_gain)
        .astype(jnp.bfloat16)
        .reshape(local_rows, HQ * HEAD_SIZE)
    )
    key_backward_pass = rotary_backward(
        local_key_gradient,
        cosine_table,
        sine_values_table,
    )
    key_gain_grad = jnp.sum(key_backward_pass * key_after_norm, axis=(0, 1))
    key_before_norm_gradient = (
        root_mean_square_backward(key_backward_pass, key_after_norm, key_norm_scale, key_norm_gain)
        .astype(jnp.bfloat16)
        .reshape(local_rows, KEY_VALUE_HEADS * HEAD_SIZE)
    )
    value_gradient_second = own_value_grad.astype(jnp.bfloat16)
    qkv_grad = jnp.concatenate([query_pre_grad, key_before_norm_gradient, value_gradient_second], axis=1)
    attn_in_grad = (
        right_dot(qkv_grad, full_qkv)
    )
    first_gain_grad = jnp.sum(attn_in_grad * first_normed, axis=0)
    input_grad = mid_grad + root_mean_square_backward(
        attn_in_grad, first_normed, first_scale, first_gain
    )
    fsdp_size = lax.axis_size(FSDP)
    col_parts = (attention_input, mixed_b, mlp_in, hidden)
    widths = [p.shape[1] // fsdp_size for p in col_parts]
    stacked = jnp.concatenate(
        [p.reshape(local_rows, fsdp_size, w) for p, w in zip(col_parts, widths)], axis=2
    )
    cols = lax.all_to_all(stacked, FSDP, split_axis=1, concat_axis=0, tiled=True).reshape(
        fsdp_size * local_rows, sum(widths)
    )
    bounds = [sum(widths[:i]) for i in range(5)]
    attn_cols, mixed_cols, mlp_cols, hidden_cols = (
        cols[:, bounds[i] : bounds[i + 1]] for i in range(4)
    )
    qkv_rows = lax.all_gather(qkv_grad, FSDP, axis=0, tiled=True)
    gate_up_rows = lax.all_gather(gate_up_grad, FSDP, axis=0, tiled=True)
    cot_mid_rows = lax.all_gather(
        jnp.concatenate([own_cotangent, mid_grad_b], axis=1), FSDP, axis=0, tiled=True
    )
    first_shard, second_shard, query_gain_shard, key_gain_shard = (
        lax.psum_scatter(first_gain_grad, FSDP, scatter_dimension=0, tiled=True),
        lax.psum_scatter(second_gain_grad, FSDP, scatter_dimension=0, tiled=True),
        lax.psum_scatter(query_gain_grad, FSDP, scatter_dimension=0, tiled=True),
        lax.psum_scatter(key_gain_grad, FSDP, scatter_dimension=0, tiled=True),
    )
    model_width = own_cotangent.shape[1]
    qkv_shard = left_dot(attn_cols, qkv_rows)
    output_shard = left_dot(mixed_cols, cot_mid_rows[:, model_width:])
    gate_up_shard = left_dot(mlp_cols, gate_up_rows)
    down_shard = left_dot(hidden_cols, cot_mid_rows[:, :model_width])
    shard_rows = qkv_shard.shape[0]
    gain_parts = (first_shard, second_shard, query_gain_shard, key_gain_shard)
    gain_block = jnp.zeros((shard_rows, 128), jnp.float32)
    for column, g in enumerate(gain_parts):
        gain_block = gain_block.at[: g.shape[0], column].set(g)
    packed = jnp.concatenate(
        [
            qkv_shard,
            output_shard.reshape(shard_rows, -1),
            gate_up_shard,
            down_shard.reshape(shard_rows, -1),
            gain_block,
        ],
        axis=1,
    ).astype(jnp.bfloat16)
    reduced = reduce_ctx(packed)
    pieces = []
    at = 0
    for width in (qkv_cols[0], qkv_cols[1], qkv_cols[2], output_shard.size // shard_rows, ff_cols, ff_cols,
                  down_shard.size // shard_rows):
        pieces.append(reduced[:, at : at + width])
        at += width
    query_total, key_total, value_total, output_total, gate_total, up_total, down_total = pieces
    output_total = output_total.reshape(output_shard.shape)
    down_total = down_total.reshape(down_shard.shape)
    first_total, second_total, query_gain_total, key_gain_total = (
        reduced[: g.shape[0], at + column] for column, g in enumerate(gain_parts)
    )
    return (
        layer_output[None],
        input_grad[None],
        query_total,
        key_total,
        value_total,
        output_total,
        gate_total,
        up_total,
        down_total,
        first_total,
        second_total,
        query_gain_total,
        key_gain_total,
    )


def solution(mesh):
    in_specs = (
        P(FSDP, CTX, None),
        P(FSDP, CTX, None),
        P(FSDP, None),
        P(FSDP, None),
        P(FSDP, None),
        P(FSDP, None),
        P(FSDP, None),
        P(FSDP, None),
        P(FSDP, None),
        P(FSDP, None),
        P(),
        P(),
        P(),
        P(),
    )
    out_specs = (
        P(FSDP, CTX, None),
        P(FSDP, CTX, None),
        P(FSDP, None),
        P(FSDP, None),
        P(FSDP, None),
        P(FSDP, None),
        P(FSDP, None),
        P(FSDP, None),
        P(FSDP, None),
        P(FSDP),
        P(FSDP),
        P(FSDP),
        P(FSDP),
    )
    torus_mesh = jax.sharding.Mesh(mesh.devices.reshape(2, 4, 4, 2, 2), ("yh", "x", "z", "yl", "c"))
    return jax.shard_map(
        on_device, mesh=torus_mesh, in_specs=in_specs, out_specs=out_specs, check_vma=False
    )
```

```python
import math

import jax
import jax.numpy as jnp
from jax import lax
from jax.sharding import PartitionSpec as P

HQ = 16
KEY_VALUE_HEADS = 8
HEAD_SIZE = 128
CTX = ("yh", "x", "z")
FSDP = ("yl", "c")


EPSILON = 1e-06
THETA = 1000000.0
MASKED = -1e30


def rms_apply(values, norm_gain):
    row_scale = lax.rsqrt(jnp.mean(values * values, axis=-1, keepdims=True) + EPSILON)
    normed = values * row_scale
    return (normed * norm_gain, normed, row_scale)


def root_mean_square_backward(gradient, normed, row_scale, norm_gain):
    normed_grad = gradient * norm_gain
    return row_scale * (
        normed_grad - normed * jnp.mean(normed_grad * normed, axis=-1, keepdims=True)
    )


def rope_tables(positions, head_width):
    half_width = head_width // 2
    inverse_freq = jnp.power(THETA, -2.0 * jnp.arange(half_width, dtype=jnp.float32) / head_width)
    angles = positions.astype(jnp.float32)[:, None] * inverse_freq[None, :]
    return (jnp.cos(angles)[:, None, :], jnp.sin(angles)[:, None, :])


def rotary_apply(values, cosine_table, sine_values_table):
    half_width = values.shape[-1] // 2
    front_half = values[..., :half_width]
    back_half = values[..., half_width:]
    return jnp.concatenate(
        [
            front_half * cosine_table - back_half * sine_values_table,
            back_half * cosine_table + front_half * sine_values_table,
        ],
        axis=-1,
    )


def rotary_backward(gradient, cosine_table, sine_values_table):
    half_width = gradient.shape[-1] // 2
    front_half = gradient[..., :half_width]
    back_half = gradient[..., half_width:]
    return jnp.concatenate(
        [
            front_half * cosine_table + back_half * sine_values_table,
            back_half * cosine_table - front_half * sine_values_table,
        ],
        axis=-1,
    )


def left_dot(left_side, right_side):
    return lax.dot_general(
        left_side, right_side, (((0,), (0,)), ((), ())), preferred_element_type=jnp.float32
    )


def right_dot(left_side, right_side):
    return lax.dot_general(
        left_side, right_side, (((1,), (1,)), ((), ())), preferred_element_type=jnp.float32
    )


def gather_fsdp(values):
    across = lax.all_gather(values, "yl", axis=0, tiled=False)
    both = lax.all_gather(across, "c", axis=1, tiled=False)
    return both.reshape((-1,) + values.shape[1:])


def reduce_ctx(packed):
    part = lax.psum_scatter(packed, "z", scatter_dimension=0, tiled=True)
    part = lax.psum_scatter(part, "x", scatter_dimension=0, tiled=True)
    part = lax.psum(part, "yh")
    part = lax.all_gather(part, "x", axis=0, tiled=True)
    return lax.all_gather(part, "z", axis=0, tiled=True).astype(jnp.float32)


def on_device(
    layer_input,
    cotangent,
    block_order,
    query_weight,
    key_projection,
    value_projection,
    output_weight,
    gate_weight,
    up_weight,
    down_weight,
    first_gain,
    second_gain,
    query_gain,
    key_norm_gain,
):
    local_rows = layer_input.shape[1]
    block_rows = local_rows // 2
    ctx_size = lax.axis_size(CTX)
    halves = ctx_size // HQ
    half_devices = ctx_size // halves
    order_row = block_order[0]
    device_place = lax.axis_index(CTX)
    my_half = device_place // half_devices
    all_positions = (
        order_row[:, None] * block_rows + jnp.arange(block_rows, dtype=jnp.int32)[None, :]
    ).reshape(-1)
    own_positions = lax.dynamic_slice_in_dim(all_positions, device_place * local_rows, local_rows)
    cosine_table, sine_values_table = rope_tables(own_positions, HEAD_SIZE)
    scale_factor = 1.0 / math.sqrt(HEAD_SIZE)
    half_rows = half_devices * local_rows
    query_positions = lax.dynamic_slice_in_dim(all_positions, my_half * half_rows, half_rows)
    allowed = all_positions[None, :] <= query_positions[:, None]
    half_select = (jnp.arange(halves, dtype=jnp.int32) == my_half)[:, None, None, None]

    def to_heads(per_head):
        by_head = jnp.transpose(per_head, (1, 0, 2))
        return jnp.where(half_select, by_head[None], jnp.zeros_like(by_head)[None]).reshape(
            ctx_size, local_rows, per_head.shape[-1]
        )

    def gather_half(received):
        return lax.dynamic_slice_in_dim(received, my_half * half_devices, half_devices, 0).reshape(
            half_rows, received.shape[-1]
        )

    def from_heads(per_head):
        blocks = per_head.reshape(half_devices, local_rows, per_head.shape[-1])
        return jnp.where(half_select, blocks[None], jnp.zeros_like(blocks)[None]).reshape(
            ctx_size, local_rows, per_head.shape[-1]
        )

    def own_heads(received):
        mine = lax.dynamic_slice_in_dim(received, my_half * half_devices, half_devices, 0)
        return jnp.transpose(mine, (1, 0, 2))

    def exchange(values):
        return lax.all_to_all(values, CTX, split_axis=0, concat_axis=0, tiled=True)

    qkv_cols = (query_weight.shape[1], key_projection.shape[1], value_projection.shape[1])
    full_qkv = lax.all_gather(
        jnp.concatenate([query_weight, key_projection, value_projection], axis=1), FSDP, axis=0, tiled=True
    )
    full_output = lax.all_gather(output_weight, FSDP, axis=0, tiled=True)
    ff_cols = gate_weight.shape[1]
    full_gate_up = lax.all_gather(
        jnp.concatenate([gate_weight, up_weight], axis=1), FSDP, axis=0, tiled=True
    )
    full_down = lax.all_gather(down_weight, FSDP, axis=0, tiled=True)
    input_f32 = layer_input[0].astype(jnp.float32)
    gained, first_normed, first_scale = rms_apply(input_f32, first_gain)
    attention_input = gained.astype(jnp.bfloat16)
    qkv_pre = jnp.dot(attention_input, full_qkv, preferred_element_type=jnp.float32)
    query_pre = qkv_pre[:, : qkv_cols[0]].reshape(local_rows, HQ, HEAD_SIZE)
    query_gained, query_normed, query_scale = rms_apply(query_pre, query_gain)
    query_rotated = rotary_apply(query_gained, cosine_table, sine_values_table).astype(jnp.bfloat16)
    key_before_norm = qkv_pre[:, qkv_cols[0] : qkv_cols[0] + qkv_cols[1]].reshape(
        local_rows, KEY_VALUE_HEADS, HEAD_SIZE
    )
    key_after_gain, key_after_norm, key_norm_scale = rms_apply(key_before_norm, key_norm_gain)
    own_keys = rotary_apply(key_after_gain, cosine_table, sine_values_table).astype(jnp.bfloat16)
    own_values = (
        qkv_pre[:, qkv_cols[0] + qkv_cols[1] :]
        .astype(jnp.bfloat16)
        .reshape(local_rows, KEY_VALUE_HEADS, HEAD_SIZE)
    )
    group = HQ // KEY_VALUE_HEADS
    key_value = jnp.repeat(jnp.concatenate([own_keys, own_values], axis=-1), group, axis=1)
    sent = jnp.concatenate([to_heads(query_rotated), jnp.tile(
        jnp.transpose(key_value, (1, 0, 2)), (halves, 1, 1))], axis=-1)
    received = exchange(sent)
    head_query = gather_half(received[..., :HEAD_SIZE])
    head_key = received[..., HEAD_SIZE : 2 * HEAD_SIZE].reshape(-1, HEAD_SIZE)
    head_value = received[..., 2 * HEAD_SIZE :].reshape(-1, HEAD_SIZE)

    def head_scores():
        raw_scores = (
            jnp.einsum("qd,kd->qk", head_query, head_key, preferred_element_type=jnp.float32)
            * scale_factor
        )
        return jnp.where(allowed, raw_scores, MASKED)

    raw_scores = head_scores()
    row_max = jnp.max(raw_scores, axis=-1, keepdims=True)
    log_total = row_max + jnp.log(jnp.sum(jnp.exp(raw_scores - row_max), axis=-1, keepdims=True))
    weights_b = jnp.exp(raw_scores - log_total).astype(jnp.bfloat16)
    head_mixed = jnp.dot(weights_b, head_value, preferred_element_type=jnp.float32)
    mixed_b = own_heads(exchange(from_heads(head_mixed.astype(jnp.bfloat16)))).reshape(
        local_rows, HQ * HEAD_SIZE
    )
    residual_mid = input_f32 + jnp.dot(mixed_b, full_output, preferred_element_type=jnp.float32)
    gained_mid, second_normed, second_scale = rms_apply(residual_mid, second_gain)
    mlp_in = gained_mid.astype(jnp.bfloat16)
    gate_up_pre = jnp.dot(mlp_in, full_gate_up, preferred_element_type=jnp.float32)
    gate_pre = gate_up_pre[:, :ff_cols]
    up_pre = gate_up_pre[:, ff_cols:]
    sigmoid_gate = jax.nn.sigmoid(gate_pre)
    silu_gate = gate_pre * sigmoid_gate
    hidden = (silu_gate * up_pre).astype(jnp.bfloat16)
    layer_output = (
        residual_mid + jnp.dot(hidden, full_down, preferred_element_type=jnp.float32)
    ).astype(jnp.bfloat16)
    own_cotangent = cotangent[0]
    hidden_grad = right_dot(own_cotangent, full_down)
    gate_grad = (
        hidden_grad * up_pre * sigmoid_gate * (1.0 + gate_pre * (1.0 - sigmoid_gate))
    ).astype(jnp.bfloat16)
    up_grad = (hidden_grad * silu_gate).astype(jnp.bfloat16)
    gate_up_grad = jnp.concatenate([gate_grad, up_grad], axis=1)
    mlp_in_grad = right_dot(gate_up_grad, full_gate_up)
    second_gain_grad = jnp.sum(mlp_in_grad * second_normed, axis=0)
    mid_grad = own_cotangent.astype(jnp.float32) + root_mean_square_backward(
        mlp_in_grad, second_normed, second_scale, second_gain
    )
    mid_grad_b = mid_grad.astype(jnp.bfloat16)
    mixed_gradient = right_dot(mid_grad_b, full_output).astype(jnp.bfloat16)
    head_out_grad = gather_half(
        exchange(to_heads(mixed_gradient.reshape(local_rows, HQ, HEAD_SIZE)))
    )
    out_grad_f = head_out_grad.astype(jnp.float32)
    delta = jnp.sum(out_grad_f * head_mixed, axis=-1, keepdims=True)
    probabilities = jnp.exp(head_scores() - log_total)
    value_part = left_dot(probabilities.astype(jnp.bfloat16), head_out_grad)
    prob_grad = right_dot(head_out_grad, head_value)
    score_grad = (probabilities * (prob_grad - delta)).astype(jnp.bfloat16)
    query_part = jnp.dot(score_grad, head_key, preferred_element_type=jnp.float32) * scale_factor
    key_part = left_dot(score_grad, head_query) * scale_factor
    returned = exchange(jnp.concatenate([
        from_heads(query_part.astype(jnp.bfloat16)),
        jnp.concatenate([key_part, value_part], axis=-1).astype(jnp.bfloat16).reshape(
            ctx_size, local_rows, 2 * HEAD_SIZE),
    ], axis=-1))
    query_grad_rows = own_heads(returned[..., :HEAD_SIZE]).astype(jnp.float32)
    kv_parts = returned[..., HEAD_SIZE:].astype(jnp.float32).reshape(
        halves, KEY_VALUE_HEADS, group, local_rows, 2 * HEAD_SIZE)
    kv_grad = jnp.transpose(jnp.sum(kv_parts, axis=(0, 2)), (1, 0, 2))
    local_key_gradient = kv_grad[..., :HEAD_SIZE]
    own_value_grad = kv_grad[..., HEAD_SIZE:].reshape(local_rows, KEY_VALUE_HEADS * HEAD_SIZE)
    query_back = rotary_backward(query_grad_rows, cosine_table, sine_values_table)
    query_gain_grad = jnp.sum(query_back * query_normed, axis=(0, 1))
    query_pre_grad = (
        root_mean_square_backward(query_back, query_normed, query_scale, query_gain)
        .astype(jnp.bfloat16)
        .reshape(local_rows, HQ * HEAD_SIZE)
    )
    key_backward_pass = rotary_backward(
        local_key_gradient,
        cosine_table,
        sine_values_table,
    )
    key_gain_grad = jnp.sum(key_backward_pass * key_after_norm, axis=(0, 1))
    key_before_norm_gradient = (
        root_mean_square_backward(key_backward_pass, key_after_norm, key_norm_scale, key_norm_gain)
        .astype(jnp.bfloat16)
        .reshape(local_rows, KEY_VALUE_HEADS * HEAD_SIZE)
    )
    value_gradient_second = own_value_grad.astype(jnp.bfloat16)
    qkv_grad = jnp.concatenate([query_pre_grad, key_before_norm_gradient, value_gradient_second], axis=1)
    attn_in_grad = (
        right_dot(qkv_grad, full_qkv)
    )
    first_gain_grad = jnp.sum(attn_in_grad * first_normed, axis=0)
    input_grad = mid_grad + root_mean_square_backward(
        attn_in_grad, first_normed, first_scale, first_gain
    )
    fsdp_size = lax.axis_size(FSDP)
    col_parts = (attention_input, mixed_b, mlp_in, hidden)
    widths = [p.shape[1] // fsdp_size for p in col_parts]
    stacked = jnp.concatenate(
        [p.reshape(local_rows, fsdp_size, w) for p, w in zip(col_parts, widths)], axis=2
    )
    cols = lax.all_to_all(stacked, FSDP, split_axis=1, concat_axis=0, tiled=True).reshape(
        fsdp_size * local_rows, sum(widths)
    )
    bounds = [sum(widths[:i]) for i in range(5)]
    attn_cols, mixed_cols, mlp_cols, hidden_cols = (
        cols[:, bounds[i] : bounds[i + 1]] for i in range(4)
    )
    qkv_rows = lax.all_gather(qkv_grad, FSDP, axis=0, tiled=True)
    gate_up_rows = lax.all_gather(gate_up_grad, FSDP, axis=0, tiled=True)
    cot_mid_rows = lax.all_gather(
        jnp.concatenate([own_cotangent, mid_grad_b], axis=1), FSDP, axis=0, tiled=True
    )
    first_shard, second_shard, query_gain_shard, key_gain_shard = (
        lax.psum_scatter(first_gain_grad, FSDP, scatter_dimension=0, tiled=True),
        lax.psum_scatter(second_gain_grad, FSDP, scatter_dimension=0, tiled=True),
        lax.psum_scatter(query_gain_grad, FSDP, scatter_dimension=0, tiled=True),
        lax.psum_scatter(key_gain_grad, FSDP, scatter_dimension=0, tiled=True),
    )
    model_width = own_cotangent.shape[1]
    qkv_shard = left_dot(attn_cols, qkv_rows)
    output_shard = left_dot(mixed_cols, cot_mid_rows[:, model_width:])
    gate_up_shard = left_dot(mlp_cols, gate_up_rows)
    down_shard = left_dot(hidden_cols, cot_mid_rows[:, :model_width])
    shard_rows = qkv_shard.shape[0]
    gain_parts = (first_shard, second_shard, query_gain_shard, key_gain_shard)
    gain_block = jnp.zeros((shard_rows, 128), jnp.float32)
    for column, g in enumerate(gain_parts):
        gain_block = gain_block.at[: g.shape[0], column].set(g)
    packed = jnp.concatenate(
        [
            qkv_shard,
            output_shard.reshape(shard_rows, -1),
            gate_up_shard,
            down_shard.reshape(shard_rows, -1),
            gain_block,
        ],
        axis=1,
    ).astype(jnp.bfloat16)
    reduced = reduce_ctx(packed)
    pieces = []
    at = 0
    for width in (qkv_cols[0], qkv_cols[1], qkv_cols[2], output_shard.size // shard_rows, ff_cols, ff_cols,
                  down_shard.size // shard_rows):
        pieces.append(reduced[:, at : at + width])
        at += width
    query_total, key_total, value_total, output_total, gate_total, up_total, down_total = pieces
    output_total = output_total.reshape(output_shard.shape)
    down_total = down_total.reshape(down_shard.shape)
    first_total, second_total, query_gain_total, key_gain_total = (
        reduced[: g.shape[0], at + column] for column, g in enumerate(gain_parts)
    )
    return (
        layer_output[None],
        input_grad[None],
        query_total,
        key_total,
        value_total,
        output_total,
        gate_total,
        up_total,
        down_total,
        first_total,
        second_total,
        query_gain_total,
        key_gain_total,
    )


def solution(mesh):
    in_specs = (
        P(FSDP, CTX, None),
        P(FSDP, CTX, None),
        P(FSDP, None),
        P(FSDP, None),
        P(FSDP, None),
        P(FSDP, None),
        P(FSDP, None),
        P(FSDP, None),
        P(FSDP, None),
        P(FSDP, None),
        P(),
        P(),
        P(),
        P(),
    )
    out_specs = (
        P(FSDP, CTX, None),
        P(FSDP, CTX, None),
        P(FSDP, None),
        P(FSDP, None),
        P(FSDP, None),
        P(FSDP, None),
        P(FSDP, None),
        P(FSDP, None),
        P(FSDP, None),
        P(FSDP),
        P(FSDP),
        P(FSDP),
        P(FSDP),
    )
    torus_mesh = jax.sharding.Mesh(mesh.devices.reshape(2, 4, 4, 2, 2), ("yh", "x", "z", "yl", "c"))
    return jax.shard_map(
        on_device, mesh=torus_mesh, in_specs=in_specs, out_specs=out_specs, check_vma=False
    )
```

```python
import math

import jax
import jax.numpy as jnp
from jax import lax
from jax.sharding import PartitionSpec as P

HQ = 16
KEY_VALUE_HEADS = 8
HEAD_SIZE = 128
CTX = ("yh", "x", "z")
FSDP = ("yl", "c")


EPSILON = 1e-06
THETA = 1000000.0
MASKED = -1e30


def rms_apply(values, norm_gain):
    row_scale = lax.rsqrt(jnp.mean(values * values, axis=-1, keepdims=True) + EPSILON)
    normed = values * row_scale
    return (normed * norm_gain, normed, row_scale)


def root_mean_square_backward(gradient, normed, row_scale, norm_gain):
    normed_grad = gradient * norm_gain
    return row_scale * (
        normed_grad - normed * jnp.mean(normed_grad * normed, axis=-1, keepdims=True)
    )


def rope_tables(positions, head_width):
    half_width = head_width // 2
    inverse_freq = jnp.power(THETA, -2.0 * jnp.arange(half_width, dtype=jnp.float32) / head_width)
    angles = positions.astype(jnp.float32)[:, None] * inverse_freq[None, :]
    return (jnp.cos(angles)[:, None, :], jnp.sin(angles)[:, None, :])


def rotary_apply(values, cosine_table, sine_values_table):
    half_width = values.shape[-1] // 2
    front_half = values[..., :half_width]
    back_half = values[..., half_width:]
    return jnp.concatenate(
        [
            front_half * cosine_table - back_half * sine_values_table,
            back_half * cosine_table + front_half * sine_values_table,
        ],
        axis=-1,
    )


def rotary_backward(gradient, cosine_table, sine_values_table):
    half_width = gradient.shape[-1] // 2
    front_half = gradient[..., :half_width]
    back_half = gradient[..., half_width:]
    return jnp.concatenate(
        [
            front_half * cosine_table + back_half * sine_values_table,
            back_half * cosine_table - front_half * sine_values_table,
        ],
        axis=-1,
    )


def left_dot(left_side, right_side):
    return lax.dot_general(
        left_side, right_side, (((0,), (0,)), ((), ())), preferred_element_type=jnp.float32
    )


def right_dot(left_side, right_side):
    return lax.dot_general(
        left_side, right_side, (((1,), (1,)), ((), ())), preferred_element_type=jnp.float32
    )


def gather_fsdp(values):
    across = lax.all_gather(values, "yl", axis=0, tiled=False)
    both = lax.all_gather(across, "c", axis=1, tiled=False)
    return both.reshape((-1,) + values.shape[1:])


def reduce_ctx(packed):
    part = lax.psum_scatter(packed, "z", scatter_dimension=0, tiled=True)
    part = lax.psum_scatter(part, "x", scatter_dimension=0, tiled=True)
    part = (part.astype(jnp.float32) + lax.ppermute(part, "yh", [(0, 1), (1, 0)]).astype(jnp.float32)).astype(
        part.dtype
    )
    part = lax.all_gather(part, "x", axis=0, tiled=True)
    return lax.all_gather(part, "z", axis=0, tiled=True).astype(jnp.float32)


def on_device(
    layer_input,
    cotangent,
    block_order,
    query_weight,
    key_projection,
    value_projection,
    output_weight,
    gate_weight,
    up_weight,
    down_weight,
    first_gain,
    second_gain,
    query_gain,
    key_norm_gain,
):
    local_rows = layer_input.shape[1]
    block_rows = local_rows // 2
    ctx_size = lax.axis_size(CTX)
    halves = ctx_size // HQ
    half_devices = ctx_size // halves
    order_row = block_order[0]
    device_place = lax.axis_index(CTX)
    my_half = device_place // half_devices
    all_positions = (
        order_row[:, None] * block_rows + jnp.arange(block_rows, dtype=jnp.int32)[None, :]
    ).reshape(-1)
    own_positions = lax.dynamic_slice_in_dim(all_positions, device_place * local_rows, local_rows)
    cosine_table, sine_values_table = rope_tables(own_positions, HEAD_SIZE)
    scale_factor = 1.0 / math.sqrt(HEAD_SIZE)
    half_rows = half_devices * local_rows
    query_positions = lax.dynamic_slice_in_dim(all_positions, my_half * half_rows, half_rows)
    allowed = all_positions[None, :] <= query_positions[:, None]
    half_select = (jnp.arange(halves, dtype=jnp.int32) == my_half)[:, None, None, None]

    def to_heads(per_head):
        by_head = jnp.transpose(per_head, (1, 0, 2))
        return jnp.where(half_select, by_head[None], jnp.zeros_like(by_head)[None]).reshape(
            ctx_size, local_rows, per_head.shape[-1]
        )

    def gather_half(received):
        return lax.dynamic_slice_in_dim(received, my_half * half_devices, half_devices, 0).reshape(
            half_rows, received.shape[-1]
        )

    def from_heads(per_head):
        blocks = per_head.reshape(half_devices, local_rows, per_head.shape[-1])
        return jnp.where(half_select, blocks[None], jnp.zeros_like(blocks)[None]).reshape(
            ctx_size, local_rows, per_head.shape[-1]
        )

    def own_heads(received):
        mine = lax.dynamic_slice_in_dim(received, my_half * half_devices, half_devices, 0)
        return jnp.transpose(mine, (1, 0, 2))

    def exchange(values):
        return lax.all_to_all(values, CTX, split_axis=0, concat_axis=0, tiled=True)

    qkv_cols = (query_weight.shape[1], key_projection.shape[1], value_projection.shape[1])
    full_qkv = lax.all_gather(
        jnp.concatenate([query_weight, key_projection, value_projection], axis=1), FSDP, axis=0, tiled=True
    )
    full_output = lax.all_gather(output_weight, FSDP, axis=0, tiled=True)
    ff_cols = gate_weight.shape[1]
    full_gate_up = lax.all_gather(
        jnp.concatenate([gate_weight, up_weight], axis=1), FSDP, axis=0, tiled=True
    )
    full_down = lax.all_gather(down_weight, FSDP, axis=0, tiled=True)
    input_f32 = layer_input[0].astype(jnp.float32)
    gained, first_normed, first_scale = rms_apply(input_f32, first_gain)
    attention_input = gained.astype(jnp.bfloat16)
    qkv_pre = jnp.dot(attention_input, full_qkv, preferred_element_type=jnp.float32)
    query_pre = qkv_pre[:, : qkv_cols[0]].reshape(local_rows, HQ, HEAD_SIZE)
    query_gained, query_normed, query_scale = rms_apply(query_pre, query_gain)
    query_rotated = rotary_apply(query_gained, cosine_table, sine_values_table).astype(jnp.bfloat16)
    key_before_norm = qkv_pre[:, qkv_cols[0] : qkv_cols[0] + qkv_cols[1]].reshape(
        local_rows, KEY_VALUE_HEADS, HEAD_SIZE
    )
    key_after_gain, key_after_norm, key_norm_scale = rms_apply(key_before_norm, key_norm_gain)
    own_keys = rotary_apply(key_after_gain, cosine_table, sine_values_table).astype(jnp.bfloat16)
    own_values = (
        qkv_pre[:, qkv_cols[0] + qkv_cols[1] :]
        .astype(jnp.bfloat16)
        .reshape(local_rows, KEY_VALUE_HEADS, HEAD_SIZE)
    )
    group = HQ // KEY_VALUE_HEADS
    key_value = jnp.repeat(jnp.concatenate([own_keys, own_values], axis=-1), group, axis=1)
    sent = jnp.concatenate([to_heads(query_rotated), jnp.tile(
        jnp.transpose(key_value, (1, 0, 2)), (halves, 1, 1))], axis=-1)
    received = exchange(sent)
    head_query = gather_half(received[..., :HEAD_SIZE])
    head_key = received[..., HEAD_SIZE : 2 * HEAD_SIZE].reshape(-1, HEAD_SIZE)
    head_value = received[..., 2 * HEAD_SIZE :].reshape(-1, HEAD_SIZE)

    def head_scores():
        raw_scores = (
            jnp.einsum("qd,kd->qk", head_query, head_key, preferred_element_type=jnp.float32)
            * scale_factor
        )
        return jnp.where(allowed, raw_scores, MASKED)

    raw_scores = head_scores()
    row_max = jnp.max(raw_scores, axis=-1, keepdims=True)
    log_total = row_max + jnp.log(jnp.sum(jnp.exp(raw_scores - row_max), axis=-1, keepdims=True))
    weights_b = jnp.exp(raw_scores - log_total).astype(jnp.bfloat16)
    head_mixed = jnp.dot(weights_b, head_value, preferred_element_type=jnp.float32)
    mixed_b = own_heads(exchange(from_heads(head_mixed.astype(jnp.bfloat16)))).reshape(
        local_rows, HQ * HEAD_SIZE
    )
    residual_mid = input_f32 + jnp.dot(mixed_b, full_output, preferred_element_type=jnp.float32)
    gained_mid, second_normed, second_scale = rms_apply(residual_mid, second_gain)
    mlp_in = gained_mid.astype(jnp.bfloat16)
    gate_up_pre = jnp.dot(mlp_in, full_gate_up, preferred_element_type=jnp.float32)
    gate_pre = gate_up_pre[:, :ff_cols]
    up_pre = gate_up_pre[:, ff_cols:]
    sigmoid_gate = jax.nn.sigmoid(gate_pre)
    silu_gate = gate_pre * sigmoid_gate
    hidden = (silu_gate * up_pre).astype(jnp.bfloat16)
    layer_output = (
        residual_mid + jnp.dot(hidden, full_down, preferred_element_type=jnp.float32)
    ).astype(jnp.bfloat16)
    own_cotangent = cotangent[0]
    hidden_grad = right_dot(own_cotangent, full_down)
    gate_grad = (
        hidden_grad * up_pre * sigmoid_gate * (1.0 + gate_pre * (1.0 - sigmoid_gate))
    ).astype(jnp.bfloat16)
    up_grad = (hidden_grad * silu_gate).astype(jnp.bfloat16)
    gate_up_grad = jnp.concatenate([gate_grad, up_grad], axis=1)
    mlp_in_grad = right_dot(gate_up_grad, full_gate_up)
    second_gain_grad = jnp.sum(mlp_in_grad * second_normed, axis=0)
    mid_grad = own_cotangent.astype(jnp.float32) + root_mean_square_backward(
        mlp_in_grad, second_normed, second_scale, second_gain
    )
    mid_grad_b = mid_grad.astype(jnp.bfloat16)
    mixed_gradient = right_dot(mid_grad_b, full_output).astype(jnp.bfloat16)
    fsdp_size = lax.axis_size(FSDP)
    col_parts = (attention_input, mixed_b, mlp_in, hidden)
    widths = [p.shape[1] // fsdp_size for p in col_parts]
    stacked = jnp.concatenate(
        [p.reshape(local_rows, fsdp_size, w) for p, w in zip(col_parts, widths)], axis=2
    )
    cols = lax.all_to_all(stacked, FSDP, split_axis=1, concat_axis=0, tiled=True).reshape(
        fsdp_size * local_rows, sum(widths)
    )
    bounds = [sum(widths[:i]) for i in range(5)]
    attn_cols, mixed_cols, mlp_cols, hidden_cols = (
        cols[:, bounds[i] : bounds[i + 1]] for i in range(4)
    )
    gate_up_rows = lax.all_gather(gate_up_grad, FSDP, axis=0, tiled=True)
    cot_mid_rows = lax.all_gather(
        jnp.concatenate([own_cotangent, mid_grad_b], axis=1), FSDP, axis=0, tiled=True
    )
    model_width = own_cotangent.shape[1]
    output_shard = left_dot(mixed_cols, cot_mid_rows[:, model_width:])
    gate_up_shard = left_dot(mlp_cols, gate_up_rows)
    down_shard = left_dot(hidden_cols, cot_mid_rows[:, :model_width])
    mlp_rows = gate_up_shard.shape[0]
    mlp_packed = jnp.concatenate(
        [output_shard.reshape(mlp_rows, -1), gate_up_shard, down_shard.reshape(mlp_rows, -1)],
        axis=1,
    ).astype(jnp.bfloat16)
    mlp_packed, mixed_gradient = lax.optimization_barrier((mlp_packed, mixed_gradient))
    mlp_reduced = reduce_ctx(mlp_packed)
    head_out_grad = gather_half(
        exchange(to_heads(mixed_gradient.reshape(local_rows, HQ, HEAD_SIZE)))
    )
    out_grad_f = head_out_grad.astype(jnp.float32)
    delta = jnp.sum(out_grad_f * head_mixed, axis=-1, keepdims=True)
    probabilities = jnp.exp(head_scores() - log_total)
    value_part = left_dot(probabilities.astype(jnp.bfloat16), head_out_grad)
    prob_grad = right_dot(head_out_grad, head_value)
    score_grad = (probabilities * (prob_grad - delta)).astype(jnp.bfloat16)
    query_part = jnp.dot(score_grad, head_key, preferred_element_type=jnp.float32) * scale_factor
    key_part = left_dot(score_grad, head_query) * scale_factor
    returned = exchange(jnp.concatenate([
        from_heads(query_part.astype(jnp.bfloat16)),
        jnp.concatenate([key_part, value_part], axis=-1).astype(jnp.bfloat16).reshape(
            ctx_size, local_rows, 2 * HEAD_SIZE),
    ], axis=-1))
    query_grad_rows = own_heads(returned[..., :HEAD_SIZE]).astype(jnp.float32)
    kv_parts = returned[..., HEAD_SIZE:].astype(jnp.float32).reshape(
        halves, KEY_VALUE_HEADS, group, local_rows, 2 * HEAD_SIZE)
    kv_grad = jnp.transpose(jnp.sum(kv_parts, axis=(0, 2)), (1, 0, 2))
    local_key_gradient = kv_grad[..., :HEAD_SIZE]
    own_value_grad = kv_grad[..., HEAD_SIZE:].reshape(local_rows, KEY_VALUE_HEADS * HEAD_SIZE)
    query_back = rotary_backward(query_grad_rows, cosine_table, sine_values_table)
    query_gain_grad = jnp.sum(query_back * query_normed, axis=(0, 1))
    query_pre_grad = (
        root_mean_square_backward(query_back, query_normed, query_scale, query_gain)
        .astype(jnp.bfloat16)
        .reshape(local_rows, HQ * HEAD_SIZE)
    )
    key_backward_pass = rotary_backward(
        local_key_gradient,
        cosine_table,
        sine_values_table,
    )
    key_gain_grad = jnp.sum(key_backward_pass * key_after_norm, axis=(0, 1))
    key_before_norm_gradient = (
        root_mean_square_backward(key_backward_pass, key_after_norm, key_norm_scale, key_norm_gain)
        .astype(jnp.bfloat16)
        .reshape(local_rows, KEY_VALUE_HEADS * HEAD_SIZE)
    )
    value_gradient_second = own_value_grad.astype(jnp.bfloat16)
    qkv_grad = jnp.concatenate([query_pre_grad, key_before_norm_gradient, value_gradient_second], axis=1)
    attn_in_grad = (
        right_dot(qkv_grad, full_qkv)
    )
    first_gain_grad = jnp.sum(attn_in_grad * first_normed, axis=0)
    input_grad = mid_grad + root_mean_square_backward(
        attn_in_grad, first_normed, first_scale, first_gain
    )
    qkv_rows = lax.all_gather(qkv_grad, FSDP, axis=0, tiled=True)
    first_shard, second_shard, query_gain_shard, key_gain_shard = (
        lax.psum_scatter(first_gain_grad, FSDP, scatter_dimension=0, tiled=True),
        lax.psum_scatter(second_gain_grad, FSDP, scatter_dimension=0, tiled=True),
        lax.psum_scatter(query_gain_grad, FSDP, scatter_dimension=0, tiled=True),
        lax.psum_scatter(key_gain_grad, FSDP, scatter_dimension=0, tiled=True),
    )
    qkv_shard = left_dot(attn_cols, qkv_rows)
    shard_rows = qkv_shard.shape[0]
    gain_parts = (first_shard, second_shard, query_gain_shard, key_gain_shard)
    gain_block = jnp.zeros((shard_rows, 128), jnp.float32)
    for column, g in enumerate(gain_parts):
        gain_block = gain_block.at[: g.shape[0], column].set(g)
    attn_reduced = reduce_ctx(jnp.concatenate([qkv_shard, gain_block], axis=1).astype(jnp.bfloat16))
    output_width = output_shard.size // shard_rows
    output_total = mlp_reduced[:, :output_width].reshape(output_shard.shape)
    gate_total = mlp_reduced[:, output_width : output_width + ff_cols]
    up_total = mlp_reduced[:, output_width + ff_cols : output_width + 2 * ff_cols]
    down_total = mlp_reduced[:, output_width + 2 * ff_cols :].reshape(down_shard.shape)
    query_total = attn_reduced[:, : qkv_cols[0]]
    key_total = attn_reduced[:, qkv_cols[0] : qkv_cols[0] + qkv_cols[1]]
    value_total = attn_reduced[:, qkv_cols[0] + qkv_cols[1] : sum(qkv_cols)]
    at = sum(qkv_cols)
    reduced = attn_reduced
    first_total, second_total, query_gain_total, key_gain_total = (
        reduced[: g.shape[0], at + column] for column, g in enumerate(gain_parts)
    )
    return (
        layer_output[None],
        input_grad[None],
        query_total,
        key_total,
        value_total,
        output_total,
        gate_total,
        up_total,
        down_total,
        first_total,
        second_total,
        query_gain_total,
        key_gain_total,
    )


def solution(mesh):
    in_specs = (
        P(FSDP, CTX, None),
        P(FSDP, CTX, None),
        P(FSDP, None),
        P(FSDP, None),
        P(FSDP, None),
        P(FSDP, None),
        P(FSDP, None),
        P(FSDP, None),
        P(FSDP, None),
        P(FSDP, None),
        P(),
        P(),
        P(),
        P(),
    )
    out_specs = (
        P(FSDP, CTX, None),
        P(FSDP, CTX, None),
        P(FSDP, None),
        P(FSDP, None),
        P(FSDP, None),
        P(FSDP, None),
        P(FSDP, None),
        P(FSDP, None),
        P(FSDP, None),
        P(FSDP),
        P(FSDP),
        P(FSDP),
        P(FSDP),
    )
    torus_mesh = jax.sharding.Mesh(mesh.devices.reshape(2, 4, 4, 2, 2), ("yh", "x", "z", "yl", "c"))
    return jax.shard_map(
        on_device, mesh=torus_mesh, in_specs=in_specs, out_specs=out_specs, check_vma=False
    )
```

```python
import math

import jax
import jax.numpy as jnp
from jax import lax
from jax.sharding import PartitionSpec as P

HQ = 16
KEY_VALUE_HEADS = 8
HEAD_SIZE = 128
CTX = ("yh", "x", "z")
FSDP = ("yl", "c")


EPSILON = 1e-06
THETA = 1000000.0
MASKED = -1e30


def rms_apply(values, norm_gain):
    row_scale = lax.rsqrt(jnp.mean(values * values, axis=-1, keepdims=True) + EPSILON)
    normed = values * row_scale
    return (normed * norm_gain, normed, row_scale)


def root_mean_square_backward(gradient, normed, row_scale, norm_gain):
    normed_grad = gradient * norm_gain
    return row_scale * (
        normed_grad - normed * jnp.mean(normed_grad * normed, axis=-1, keepdims=True)
    )


def rope_tables(positions, head_width):
    half_width = head_width // 2
    inverse_freq = jnp.power(THETA, -2.0 * jnp.arange(half_width, dtype=jnp.float32) / head_width)
    angles = positions.astype(jnp.float32)[:, None] * inverse_freq[None, :]
    return (jnp.cos(angles)[:, None, :], jnp.sin(angles)[:, None, :])


def rotary_apply(values, cosine_table, sine_values_table):
    half_width = values.shape[-1] // 2
    front_half = values[..., :half_width]
    back_half = values[..., half_width:]
    return jnp.concatenate(
        [
            front_half * cosine_table - back_half * sine_values_table,
            back_half * cosine_table + front_half * sine_values_table,
        ],
        axis=-1,
    )


def rotary_backward(gradient, cosine_table, sine_values_table):
    half_width = gradient.shape[-1] // 2
    front_half = gradient[..., :half_width]
    back_half = gradient[..., half_width:]
    return jnp.concatenate(
        [
            front_half * cosine_table + back_half * sine_values_table,
            back_half * cosine_table - front_half * sine_values_table,
        ],
        axis=-1,
    )


def left_dot(left_side, right_side):
    return lax.dot_general(
        left_side, right_side, (((0,), (0,)), ((), ())), preferred_element_type=jnp.float32
    )


def right_dot(left_side, right_side):
    return lax.dot_general(
        left_side, right_side, (((1,), (1,)), ((), ())), preferred_element_type=jnp.float32
    )


def gather_fsdp(values):
    across = lax.all_gather(values, "yl", axis=0, tiled=False)
    other = lax.ppermute(across, "c", [(0, 1), (1, 0)])
    first_core = lax.axis_index("c") == 0
    both = jnp.stack([jnp.where(first_core, across, other), jnp.where(first_core, other, across)], axis=1)
    return both.reshape((-1,) + values.shape[1:])


def reduce_ctx(packed):
    part = lax.psum_scatter(packed, "z", scatter_dimension=0, tiled=True)
    part = lax.psum_scatter(part, "x", scatter_dimension=0, tiled=True)
    part = (part.astype(jnp.float32) + lax.ppermute(part, "yh", [(0, 1), (1, 0)]).astype(jnp.float32)).astype(
        part.dtype
    )
    part = lax.all_gather(part, "x", axis=0, tiled=True)
    return lax.all_gather(part, "z", axis=0, tiled=True).astype(jnp.float32)


def on_device(
    layer_input,
    cotangent,
    block_order,
    query_weight,
    key_projection,
    value_projection,
    output_weight,
    gate_weight,
    up_weight,
    down_weight,
    first_gain,
    second_gain,
    query_gain,
    key_norm_gain,
):
    local_rows = layer_input.shape[1]
    block_rows = local_rows // 2
    ctx_size = lax.axis_size(CTX)
    halves = ctx_size // HQ
    half_devices = ctx_size // halves
    order_row = block_order[0]
    device_place = lax.axis_index(CTX)
    my_half = device_place // half_devices
    all_positions = (
        order_row[:, None] * block_rows + jnp.arange(block_rows, dtype=jnp.int32)[None, :]
    ).reshape(-1)
    own_positions = lax.dynamic_slice_in_dim(all_positions, device_place * local_rows, local_rows)
    cosine_table, sine_values_table = rope_tables(own_positions, HEAD_SIZE)
    scale_factor = 1.0 / math.sqrt(HEAD_SIZE)
    half_rows = half_devices * local_rows
    query_positions = lax.dynamic_slice_in_dim(all_positions, my_half * half_rows, half_rows)
    allowed = all_positions[None, :] <= query_positions[:, None]
    half_select = (jnp.arange(halves, dtype=jnp.int32) == my_half)[:, None, None, None]

    def to_heads(per_head):
        by_head = jnp.transpose(per_head, (1, 0, 2))
        return jnp.where(half_select, by_head[None], jnp.zeros_like(by_head)[None]).reshape(
            ctx_size, local_rows, per_head.shape[-1]
        )

    def gather_half(received):
        return lax.dynamic_slice_in_dim(received, my_half * half_devices, half_devices, 0).reshape(
            half_rows, received.shape[-1]
        )

    def from_heads(per_head):
        blocks = per_head.reshape(half_devices, local_rows, per_head.shape[-1])
        return jnp.where(half_select, blocks[None], jnp.zeros_like(blocks)[None]).reshape(
            ctx_size, local_rows, per_head.shape[-1]
        )

    def own_heads(received):
        mine = lax.dynamic_slice_in_dim(received, my_half * half_devices, half_devices, 0)
        return jnp.transpose(mine, (1, 0, 2))

    def exchange(values):
        return lax.all_to_all(values, CTX, split_axis=0, concat_axis=0, tiled=True)

    qkv_cols = (query_weight.shape[1], key_projection.shape[1], value_projection.shape[1])
    full_qkv = gather_fsdp(jnp.concatenate([query_weight, key_projection, value_projection], axis=1))
    full_output = gather_fsdp(output_weight)
    ff_cols = gate_weight.shape[1]
    full_gate_up = gather_fsdp(jnp.concatenate([gate_weight, up_weight], axis=1))
    full_down = gather_fsdp(down_weight)
    input_f32 = layer_input[0].astype(jnp.float32)
    gained, first_normed, first_scale = rms_apply(input_f32, first_gain)
    attention_input = gained.astype(jnp.bfloat16)
    qkv_pre = jnp.dot(attention_input, full_qkv, preferred_element_type=jnp.float32)
    query_pre = qkv_pre[:, : qkv_cols[0]].reshape(local_rows, HQ, HEAD_SIZE)
    query_gained, query_normed, query_scale = rms_apply(query_pre, query_gain)
    query_rotated = rotary_apply(query_gained, cosine_table, sine_values_table).astype(jnp.bfloat16)
    key_before_norm = qkv_pre[:, qkv_cols[0] : qkv_cols[0] + qkv_cols[1]].reshape(
        local_rows, KEY_VALUE_HEADS, HEAD_SIZE
    )
    key_after_gain, key_after_norm, key_norm_scale = rms_apply(key_before_norm, key_norm_gain)
    own_keys = rotary_apply(key_after_gain, cosine_table, sine_values_table).astype(jnp.bfloat16)
    own_values = (
        qkv_pre[:, qkv_cols[0] + qkv_cols[1] :]
        .astype(jnp.bfloat16)
        .reshape(local_rows, KEY_VALUE_HEADS, HEAD_SIZE)
    )
    group = HQ // KEY_VALUE_HEADS
    key_value = jnp.repeat(jnp.concatenate([own_keys, own_values], axis=-1), group, axis=1)
    sent = jnp.concatenate([to_heads(query_rotated), jnp.tile(
        jnp.transpose(key_value, (1, 0, 2)), (halves, 1, 1))], axis=-1)
    received = exchange(sent)
    head_query = gather_half(received[..., :HEAD_SIZE])
    head_key = received[..., HEAD_SIZE : 2 * HEAD_SIZE].reshape(-1, HEAD_SIZE)
    head_value = received[..., 2 * HEAD_SIZE :].reshape(-1, HEAD_SIZE)

    def head_scores():
        raw_scores = (
            jnp.einsum("qd,kd->qk", head_query, head_key, preferred_element_type=jnp.float32)
            * scale_factor
        )
        return jnp.where(allowed, raw_scores, MASKED)

    raw_scores = head_scores()
    row_max = jnp.max(raw_scores, axis=-1, keepdims=True)
    log_total = row_max + jnp.log(jnp.sum(jnp.exp(raw_scores - row_max), axis=-1, keepdims=True))
    weights_b = jnp.exp(raw_scores - log_total).astype(jnp.bfloat16)
    head_mixed = jnp.dot(weights_b, head_value, preferred_element_type=jnp.float32)
    mixed_b = own_heads(exchange(from_heads(head_mixed.astype(jnp.bfloat16)))).reshape(
        local_rows, HQ * HEAD_SIZE
    )
    residual_mid = input_f32 + jnp.dot(mixed_b, full_output, preferred_element_type=jnp.float32)
    gained_mid, second_normed, second_scale = rms_apply(residual_mid, second_gain)
    mlp_in = gained_mid.astype(jnp.bfloat16)
    gate_up_pre = jnp.dot(mlp_in, full_gate_up, preferred_element_type=jnp.float32)
    gate_pre = gate_up_pre[:, :ff_cols]
    up_pre = gate_up_pre[:, ff_cols:]
    sigmoid_gate = jax.nn.sigmoid(gate_pre)
    silu_gate = gate_pre * sigmoid_gate
    hidden = (silu_gate * up_pre).astype(jnp.bfloat16)
    layer_output = (
        residual_mid + jnp.dot(hidden, full_down, preferred_element_type=jnp.float32)
    ).astype(jnp.bfloat16)
    own_cotangent = cotangent[0]
    hidden_grad = right_dot(own_cotangent, full_down)
    gate_grad = (
        hidden_grad * up_pre * sigmoid_gate * (1.0 + gate_pre * (1.0 - sigmoid_gate))
    ).astype(jnp.bfloat16)
    up_grad = (hidden_grad * silu_gate).astype(jnp.bfloat16)
    gate_up_grad = jnp.concatenate([gate_grad, up_grad], axis=1)
    mlp_in_grad = right_dot(gate_up_grad, full_gate_up)
    second_gain_grad = jnp.sum(mlp_in_grad * second_normed, axis=0)
    mid_grad = own_cotangent.astype(jnp.float32) + root_mean_square_backward(
        mlp_in_grad, second_normed, second_scale, second_gain
    )
    mid_grad_b = mid_grad.astype(jnp.bfloat16)
    mixed_gradient = right_dot(mid_grad_b, full_output).astype(jnp.bfloat16)
    fsdp_size = lax.axis_size(FSDP)
    col_parts = (attention_input, mixed_b, mlp_in, hidden)
    widths = [p.shape[1] // fsdp_size for p in col_parts]
    stacked = jnp.concatenate(
        [p.reshape(local_rows, fsdp_size, w) for p, w in zip(col_parts, widths)], axis=2
    )
    cols = lax.all_to_all(stacked, FSDP, split_axis=1, concat_axis=0, tiled=True).reshape(
        fsdp_size * local_rows, sum(widths)
    )
    bounds = [sum(widths[:i]) for i in range(5)]
    attn_cols, mixed_cols, mlp_cols, hidden_cols = (
        cols[:, bounds[i] : bounds[i + 1]] for i in range(4)
    )
    gate_up_rows = lax.all_gather(gate_up_grad, FSDP, axis=0, tiled=True)
    cot_mid_rows = lax.all_gather(
        jnp.concatenate([own_cotangent, mid_grad_b], axis=1), FSDP, axis=0, tiled=True
    )
    model_width = own_cotangent.shape[1]
    output_shard = left_dot(mixed_cols, cot_mid_rows[:, model_width:])
    gate_up_shard = left_dot(mlp_cols, gate_up_rows)
    down_shard = left_dot(hidden_cols, cot_mid_rows[:, :model_width])
    mlp_rows = gate_up_shard.shape[0]
    mlp_packed = jnp.concatenate(
        [output_shard.reshape(mlp_rows, -1), gate_up_shard, down_shard.reshape(mlp_rows, -1)],
        axis=1,
    ).astype(jnp.bfloat16)
    mlp_packed, mixed_gradient = lax.optimization_barrier((mlp_packed, mixed_gradient))
    mlp_reduced = reduce_ctx(mlp_packed)
    head_out_grad = gather_half(
        exchange(to_heads(mixed_gradient.reshape(local_rows, HQ, HEAD_SIZE)))
    )
    out_grad_f = head_out_grad.astype(jnp.float32)
    delta = jnp.sum(out_grad_f * head_mixed, axis=-1, keepdims=True)
    probabilities = jnp.exp(head_scores() - log_total)
    value_part = left_dot(probabilities.astype(jnp.bfloat16), head_out_grad)
    prob_grad = right_dot(head_out_grad, head_value)
    score_grad = (probabilities * (prob_grad - delta)).astype(jnp.bfloat16)
    query_part = jnp.dot(score_grad, head_key, preferred_element_type=jnp.float32) * scale_factor
    key_part = left_dot(score_grad, head_query) * scale_factor
    returned = exchange(jnp.concatenate([
        from_heads(query_part.astype(jnp.bfloat16)),
        jnp.concatenate([key_part, value_part], axis=-1).astype(jnp.bfloat16).reshape(
            ctx_size, local_rows, 2 * HEAD_SIZE),
    ], axis=-1))
    query_grad_rows = own_heads(returned[..., :HEAD_SIZE]).astype(jnp.float32)
    kv_parts = returned[..., HEAD_SIZE:].astype(jnp.float32).reshape(
        halves, KEY_VALUE_HEADS, group, local_rows, 2 * HEAD_SIZE)
    kv_grad = jnp.transpose(jnp.sum(kv_parts, axis=(0, 2)), (1, 0, 2))
    local_key_gradient = kv_grad[..., :HEAD_SIZE]
    own_value_grad = kv_grad[..., HEAD_SIZE:].reshape(local_rows, KEY_VALUE_HEADS * HEAD_SIZE)
    query_back = rotary_backward(query_grad_rows, cosine_table, sine_values_table)
    query_gain_grad = jnp.sum(query_back * query_normed, axis=(0, 1))
    query_pre_grad = (
        root_mean_square_backward(query_back, query_normed, query_scale, query_gain)
        .astype(jnp.bfloat16)
        .reshape(local_rows, HQ * HEAD_SIZE)
    )
    key_backward_pass = rotary_backward(
        local_key_gradient,
        cosine_table,
        sine_values_table,
    )
    key_gain_grad = jnp.sum(key_backward_pass * key_after_norm, axis=(0, 1))
    key_before_norm_gradient = (
        root_mean_square_backward(key_backward_pass, key_after_norm, key_norm_scale, key_norm_gain)
        .astype(jnp.bfloat16)
        .reshape(local_rows, KEY_VALUE_HEADS * HEAD_SIZE)
    )
    value_gradient_second = own_value_grad.astype(jnp.bfloat16)
    qkv_grad = jnp.concatenate([query_pre_grad, key_before_norm_gradient, value_gradient_second], axis=1)
    attn_in_grad = (
        right_dot(qkv_grad, full_qkv)
    )
    first_gain_grad = jnp.sum(attn_in_grad * first_normed, axis=0)
    input_grad = mid_grad + root_mean_square_backward(
        attn_in_grad, first_normed, first_scale, first_gain
    )
    qkv_rows = lax.all_gather(qkv_grad, FSDP, axis=0, tiled=True)
    first_shard, second_shard, query_gain_shard, key_gain_shard = (
        lax.psum_scatter(first_gain_grad, FSDP, scatter_dimension=0, tiled=True),
        lax.psum_scatter(second_gain_grad, FSDP, scatter_dimension=0, tiled=True),
        lax.psum_scatter(query_gain_grad, FSDP, scatter_dimension=0, tiled=True),
        lax.psum_scatter(key_gain_grad, FSDP, scatter_dimension=0, tiled=True),
    )
    qkv_shard = left_dot(attn_cols, qkv_rows)
    shard_rows = qkv_shard.shape[0]
    gain_parts = (first_shard, second_shard, query_gain_shard, key_gain_shard)
    gain_block = jnp.zeros((shard_rows, 128), jnp.float32)
    for column, g in enumerate(gain_parts):
        gain_block = gain_block.at[: g.shape[0], column].set(g)
    attn_reduced = reduce_ctx(jnp.concatenate([qkv_shard, gain_block], axis=1).astype(jnp.bfloat16))
    output_width = output_shard.size // shard_rows
    output_total = mlp_reduced[:, :output_width].reshape(output_shard.shape)
    gate_total = mlp_reduced[:, output_width : output_width + ff_cols]
    up_total = mlp_reduced[:, output_width + ff_cols : output_width + 2 * ff_cols]
    down_total = mlp_reduced[:, output_width + 2 * ff_cols :].reshape(down_shard.shape)
    query_total = attn_reduced[:, : qkv_cols[0]]
    key_total = attn_reduced[:, qkv_cols[0] : qkv_cols[0] + qkv_cols[1]]
    value_total = attn_reduced[:, qkv_cols[0] + qkv_cols[1] : sum(qkv_cols)]
    at = sum(qkv_cols)
    reduced = attn_reduced
    first_total, second_total, query_gain_total, key_gain_total = (
        reduced[: g.shape[0], at + column] for column, g in enumerate(gain_parts)
    )
    return (
        layer_output[None],
        input_grad[None],
        query_total,
        key_total,
        value_total,
        output_total,
        gate_total,
        up_total,
        down_total,
        first_total,
        second_total,
        query_gain_total,
        key_gain_total,
    )


def solution(mesh):
    in_specs = (
        P(FSDP, CTX, None),
        P(FSDP, CTX, None),
        P(FSDP, None),
        P(FSDP, None),
        P(FSDP, None),
        P(FSDP, None),
        P(FSDP, None),
        P(FSDP, None),
        P(FSDP, None),
        P(FSDP, None),
        P(),
        P(),
        P(),
        P(),
    )
    out_specs = (
        P(FSDP, CTX, None),
        P(FSDP, CTX, None),
        P(FSDP, None),
        P(FSDP, None),
        P(FSDP, None),
        P(FSDP, None),
        P(FSDP, None),
        P(FSDP, None),
        P(FSDP, None),
        P(FSDP),
        P(FSDP),
        P(FSDP),
        P(FSDP),
    )
    torus_mesh = jax.sharding.Mesh(mesh.devices.reshape(2, 4, 4, 2, 2), ("yh", "x", "z", "yl", "c"))
    return jax.shard_map(
        on_device, mesh=torus_mesh, in_specs=in_specs, out_specs=out_specs, check_vma=False
    )
```

```python
import math

import jax
import jax.numpy as jnp
from jax import lax
from jax.sharding import PartitionSpec as P

HQ = 16
KEY_VALUE_HEADS = 8
HEAD_SIZE = 128
CTX = ("yh", "x", "z")
FSDP = ("yl", "c")


EPSILON = 1e-06
THETA = 1000000.0
MASKED = -1e30


def rms_apply(values, norm_gain):
    row_scale = lax.rsqrt(jnp.mean(values * values, axis=-1, keepdims=True) + EPSILON)
    normed = values * row_scale
    return (normed * norm_gain, normed, row_scale)


def root_mean_square_backward(gradient, normed, row_scale, norm_gain):
    normed_grad = gradient * norm_gain
    return row_scale * (
        normed_grad - normed * jnp.mean(normed_grad * normed, axis=-1, keepdims=True)
    )


def rope_tables(positions, head_width):
    half_width = head_width // 2
    inverse_freq = jnp.power(THETA, -2.0 * jnp.arange(half_width, dtype=jnp.float32) / head_width)
    angles = positions.astype(jnp.float32)[:, None] * inverse_freq[None, :]
    return (jnp.cos(angles)[:, None, :], jnp.sin(angles)[:, None, :])


def rotary_apply(values, cosine_table, sine_values_table):
    half_width = values.shape[-1] // 2
    front_half = values[..., :half_width]
    back_half = values[..., half_width:]
    return jnp.concatenate(
        [
            front_half * cosine_table - back_half * sine_values_table,
            back_half * cosine_table + front_half * sine_values_table,
        ],
        axis=-1,
    )


def rotary_backward(gradient, cosine_table, sine_values_table):
    half_width = gradient.shape[-1] // 2
    front_half = gradient[..., :half_width]
    back_half = gradient[..., half_width:]
    return jnp.concatenate(
        [
            front_half * cosine_table + back_half * sine_values_table,
            back_half * cosine_table - front_half * sine_values_table,
        ],
        axis=-1,
    )


def left_dot(left_side, right_side):
    return lax.dot_general(
        left_side, right_side, (((0,), (0,)), ((), ())), preferred_element_type=jnp.float32
    )


def right_dot(left_side, right_side):
    return lax.dot_general(
        left_side, right_side, (((1,), (1,)), ((), ())), preferred_element_type=jnp.float32
    )


def gather_across(values):
    return lax.all_gather(values, "yl", axis=0, tiled=False)


def gather_cores(across, shard_shape):
    other = lax.ppermute(across, "c", [(0, 1), (1, 0)])
    first_core = lax.axis_index("c") == 0
    both = jnp.stack([jnp.where(first_core, across, other), jnp.where(first_core, other, across)], axis=1)
    return both.reshape((-1,) + shard_shape[1:])


def gather_fsdp(values):
    return gather_cores(gather_across(values), values.shape)


def reduce_ctx(packed):
    part = lax.psum_scatter(packed, "z", scatter_dimension=0, tiled=True)
    part = lax.psum_scatter(part, "x", scatter_dimension=0, tiled=True)
    part = (part.astype(jnp.float32) + lax.ppermute(part, "yh", [(0, 1), (1, 0)]).astype(jnp.float32)).astype(
        part.dtype
    )
    part = lax.all_gather(part, "x", axis=0, tiled=True)
    return lax.all_gather(part, "z", axis=0, tiled=True).astype(jnp.float32)


def on_device(
    layer_input,
    cotangent,
    block_order,
    query_weight,
    key_projection,
    value_projection,
    output_weight,
    gate_weight,
    up_weight,
    down_weight,
    first_gain,
    second_gain,
    query_gain,
    key_norm_gain,
):
    local_rows = layer_input.shape[1]
    block_rows = local_rows // 2
    ctx_size = lax.axis_size(CTX)
    halves = ctx_size // HQ
    half_devices = ctx_size // halves
    order_row = block_order[0]
    device_place = lax.axis_index(CTX)
    my_half = device_place // half_devices
    all_positions = (
        order_row[:, None] * block_rows + jnp.arange(block_rows, dtype=jnp.int32)[None, :]
    ).reshape(-1)
    own_positions = lax.dynamic_slice_in_dim(all_positions, device_place * local_rows, local_rows)
    cosine_table, sine_values_table = rope_tables(own_positions, HEAD_SIZE)
    scale_factor = 1.0 / math.sqrt(HEAD_SIZE)
    half_rows = half_devices * local_rows
    query_positions = lax.dynamic_slice_in_dim(all_positions, my_half * half_rows, half_rows)
    allowed = all_positions[None, :] <= query_positions[:, None]
    half_select = (jnp.arange(halves, dtype=jnp.int32) == my_half)[:, None, None, None]

    def to_heads(per_head):
        by_head = jnp.transpose(per_head, (1, 0, 2))
        return jnp.where(half_select, by_head[None], jnp.zeros_like(by_head)[None]).reshape(
            ctx_size, local_rows, per_head.shape[-1]
        )

    def gather_half(received):
        return lax.dynamic_slice_in_dim(received, my_half * half_devices, half_devices, 0).reshape(
            half_rows, received.shape[-1]
        )

    def from_heads(per_head):
        blocks = per_head.reshape(half_devices, local_rows, per_head.shape[-1])
        return jnp.where(half_select, blocks[None], jnp.zeros_like(blocks)[None]).reshape(
            ctx_size, local_rows, per_head.shape[-1]
        )

    def own_heads(received):
        mine = lax.dynamic_slice_in_dim(received, my_half * half_devices, half_devices, 0)
        return jnp.transpose(mine, (1, 0, 2))

    def exchange(values):
        return lax.all_to_all(values, CTX, split_axis=0, concat_axis=0, tiled=True)

    qkv_cols = (query_weight.shape[1], key_projection.shape[1], value_projection.shape[1])
    full_qkv = gather_fsdp(jnp.concatenate([query_weight, key_projection, value_projection], axis=1))
    across_output = gather_across(output_weight)
    ff_cols = gate_weight.shape[1]
    gate_up_weight = jnp.concatenate([gate_weight, up_weight], axis=1)
    across_gate_up = gather_across(gate_up_weight)
    across_down = gather_across(down_weight)
    input_f32 = layer_input[0].astype(jnp.float32)
    gained, first_normed, first_scale = rms_apply(input_f32, first_gain)
    attention_input = gained.astype(jnp.bfloat16)
    qkv_pre = jnp.dot(attention_input, full_qkv, preferred_element_type=jnp.float32)
    query_pre = qkv_pre[:, : qkv_cols[0]].reshape(local_rows, HQ, HEAD_SIZE)
    query_gained, query_normed, query_scale = rms_apply(query_pre, query_gain)
    query_rotated = rotary_apply(query_gained, cosine_table, sine_values_table).astype(jnp.bfloat16)
    key_before_norm = qkv_pre[:, qkv_cols[0] : qkv_cols[0] + qkv_cols[1]].reshape(
        local_rows, KEY_VALUE_HEADS, HEAD_SIZE
    )
    key_after_gain, key_after_norm, key_norm_scale = rms_apply(key_before_norm, key_norm_gain)
    own_keys = rotary_apply(key_after_gain, cosine_table, sine_values_table).astype(jnp.bfloat16)
    own_values = (
        qkv_pre[:, qkv_cols[0] + qkv_cols[1] :]
        .astype(jnp.bfloat16)
        .reshape(local_rows, KEY_VALUE_HEADS, HEAD_SIZE)
    )
    group = HQ // KEY_VALUE_HEADS
    key_value = jnp.repeat(jnp.concatenate([own_keys, own_values], axis=-1), group, axis=1)
    sent = jnp.concatenate([to_heads(query_rotated), jnp.tile(
        jnp.transpose(key_value, (1, 0, 2)), (halves, 1, 1))], axis=-1)
    received = exchange(sent)
    head_query = gather_half(received[..., :HEAD_SIZE])
    head_key = received[..., HEAD_SIZE : 2 * HEAD_SIZE].reshape(-1, HEAD_SIZE)
    head_value = received[..., 2 * HEAD_SIZE :].reshape(-1, HEAD_SIZE)

    def head_scores():
        raw_scores = (
            jnp.einsum("qd,kd->qk", head_query, head_key, preferred_element_type=jnp.float32)
            * scale_factor
        )
        return jnp.where(allowed, raw_scores, MASKED)

    raw_scores = head_scores()
    row_max = jnp.max(raw_scores, axis=-1, keepdims=True)
    log_total = row_max + jnp.log(jnp.sum(jnp.exp(raw_scores - row_max), axis=-1, keepdims=True))
    weights_b = jnp.exp(raw_scores - log_total).astype(jnp.bfloat16)
    head_mixed = jnp.dot(weights_b, head_value, preferred_element_type=jnp.float32)
    head_mixed, across_output, across_gate_up, across_down = lax.optimization_barrier(
        (head_mixed, across_output, across_gate_up, across_down)
    )
    full_output = gather_cores(across_output, output_weight.shape)
    full_gate_up = gather_cores(across_gate_up, gate_up_weight.shape)
    full_down = gather_cores(across_down, down_weight.shape)
    mixed_b = own_heads(exchange(from_heads(head_mixed.astype(jnp.bfloat16)))).reshape(
        local_rows, HQ * HEAD_SIZE
    )
    residual_mid = input_f32 + jnp.dot(mixed_b, full_output, preferred_element_type=jnp.float32)
    gained_mid, second_normed, second_scale = rms_apply(residual_mid, second_gain)
    mlp_in = gained_mid.astype(jnp.bfloat16)
    gate_up_pre = jnp.dot(mlp_in, full_gate_up, preferred_element_type=jnp.float32)
    gate_pre = gate_up_pre[:, :ff_cols]
    up_pre = gate_up_pre[:, ff_cols:]
    sigmoid_gate = jax.nn.sigmoid(gate_pre)
    silu_gate = gate_pre * sigmoid_gate
    hidden = (silu_gate * up_pre).astype(jnp.bfloat16)
    layer_output = (
        residual_mid + jnp.dot(hidden, full_down, preferred_element_type=jnp.float32)
    ).astype(jnp.bfloat16)
    own_cotangent = cotangent[0]
    hidden_grad = right_dot(own_cotangent, full_down)
    gate_grad = (
        hidden_grad * up_pre * sigmoid_gate * (1.0 + gate_pre * (1.0 - sigmoid_gate))
    ).astype(jnp.bfloat16)
    up_grad = (hidden_grad * silu_gate).astype(jnp.bfloat16)
    gate_up_grad = jnp.concatenate([gate_grad, up_grad], axis=1)
    mlp_in_grad = right_dot(gate_up_grad, full_gate_up)
    second_gain_grad = jnp.sum(mlp_in_grad * second_normed, axis=0)
    mid_grad = own_cotangent.astype(jnp.float32) + root_mean_square_backward(
        mlp_in_grad, second_normed, second_scale, second_gain
    )
    mid_grad_b = mid_grad.astype(jnp.bfloat16)
    mixed_gradient = right_dot(mid_grad_b, full_output).astype(jnp.bfloat16)
    fsdp_size = lax.axis_size(FSDP)
    col_parts = (attention_input, mixed_b, mlp_in, hidden)
    widths = [p.shape[1] // fsdp_size for p in col_parts]
    stacked = jnp.concatenate(
        [p.reshape(local_rows, fsdp_size, w) for p, w in zip(col_parts, widths)], axis=2
    )
    cols = lax.all_to_all(stacked, FSDP, split_axis=1, concat_axis=0, tiled=True).reshape(
        fsdp_size * local_rows, sum(widths)
    )
    bounds = [sum(widths[:i]) for i in range(5)]
    attn_cols, mixed_cols, mlp_cols, hidden_cols = (
        cols[:, bounds[i] : bounds[i + 1]] for i in range(4)
    )
    gate_up_rows = lax.all_gather(gate_up_grad, FSDP, axis=0, tiled=True)
    cot_mid_rows = lax.all_gather(
        jnp.concatenate([own_cotangent, mid_grad_b], axis=1), FSDP, axis=0, tiled=True
    )
    model_width = own_cotangent.shape[1]
    output_shard = left_dot(mixed_cols, cot_mid_rows[:, model_width:])
    gate_up_shard = left_dot(mlp_cols, gate_up_rows)
    down_shard = left_dot(hidden_cols, cot_mid_rows[:, :model_width])
    mlp_rows = gate_up_shard.shape[0]
    mlp_packed = jnp.concatenate(
        [output_shard.reshape(mlp_rows, -1), gate_up_shard, down_shard.reshape(mlp_rows, -1)],
        axis=1,
    ).astype(jnp.bfloat16)
    mlp_packed, mixed_gradient = lax.optimization_barrier((mlp_packed, mixed_gradient))
    mlp_reduced = reduce_ctx(mlp_packed)
    head_out_grad = gather_half(
        exchange(to_heads(mixed_gradient.reshape(local_rows, HQ, HEAD_SIZE)))
    )
    out_grad_f = head_out_grad.astype(jnp.float32)
    delta = jnp.sum(out_grad_f * head_mixed, axis=-1, keepdims=True)
    probabilities = jnp.exp(head_scores() - log_total)
    value_part = left_dot(probabilities.astype(jnp.bfloat16), head_out_grad)
    prob_grad = right_dot(head_out_grad, head_value)
    score_grad = (probabilities * (prob_grad - delta)).astype(jnp.bfloat16)
    query_part = jnp.dot(score_grad, head_key, preferred_element_type=jnp.float32) * scale_factor
    key_part = left_dot(score_grad, head_query) * scale_factor
    returned = exchange(jnp.concatenate([
        from_heads(query_part.astype(jnp.bfloat16)),
        jnp.concatenate([key_part, value_part], axis=-1).astype(jnp.bfloat16).reshape(
            ctx_size, local_rows, 2 * HEAD_SIZE),
    ], axis=-1))
    query_grad_rows = own_heads(returned[..., :HEAD_SIZE]).astype(jnp.float32)
    kv_parts = returned[..., HEAD_SIZE:].astype(jnp.float32).reshape(
        halves, KEY_VALUE_HEADS, group, local_rows, 2 * HEAD_SIZE)
    kv_grad = jnp.transpose(jnp.sum(kv_parts, axis=(0, 2)), (1, 0, 2))
    local_key_gradient = kv_grad[..., :HEAD_SIZE]
    own_value_grad = kv_grad[..., HEAD_SIZE:].reshape(local_rows, KEY_VALUE_HEADS * HEAD_SIZE)
    query_back = rotary_backward(query_grad_rows, cosine_table, sine_values_table)
    query_gain_grad = jnp.sum(query_back * query_normed, axis=(0, 1))
    query_pre_grad = (
        root_mean_square_backward(query_back, query_normed, query_scale, query_gain)
        .astype(jnp.bfloat16)
        .reshape(local_rows, HQ * HEAD_SIZE)
    )
    key_backward_pass = rotary_backward(
        local_key_gradient,
        cosine_table,
        sine_values_table,
    )
    key_gain_grad = jnp.sum(key_backward_pass * key_after_norm, axis=(0, 1))
    key_before_norm_gradient = (
        root_mean_square_backward(key_backward_pass, key_after_norm, key_norm_scale, key_norm_gain)
        .astype(jnp.bfloat16)
        .reshape(local_rows, KEY_VALUE_HEADS * HEAD_SIZE)
    )
    value_gradient_second = own_value_grad.astype(jnp.bfloat16)
    qkv_grad = jnp.concatenate([query_pre_grad, key_before_norm_gradient, value_gradient_second], axis=1)
    attn_in_grad = (
        right_dot(qkv_grad, full_qkv)
    )
    first_gain_grad = jnp.sum(attn_in_grad * first_normed, axis=0)
    input_grad = mid_grad + root_mean_square_backward(
        attn_in_grad, first_normed, first_scale, first_gain
    )
    qkv_rows = lax.all_gather(qkv_grad, FSDP, axis=0, tiled=True)
    first_shard, second_shard, query_gain_shard, key_gain_shard = (
        lax.psum_scatter(first_gain_grad, FSDP, scatter_dimension=0, tiled=True),
        lax.psum_scatter(second_gain_grad, FSDP, scatter_dimension=0, tiled=True),
        lax.psum_scatter(query_gain_grad, FSDP, scatter_dimension=0, tiled=True),
        lax.psum_scatter(key_gain_grad, FSDP, scatter_dimension=0, tiled=True),
    )
    qkv_shard = left_dot(attn_cols, qkv_rows)
    shard_rows = qkv_shard.shape[0]
    gain_parts = (first_shard, second_shard, query_gain_shard, key_gain_shard)
    gain_block = jnp.zeros((shard_rows, 128), jnp.float32)
    for column, g in enumerate(gain_parts):
        gain_block = gain_block.at[: g.shape[0], column].set(g)
    attn_reduced = reduce_ctx(jnp.concatenate([qkv_shard, gain_block], axis=1).astype(jnp.bfloat16))
    output_width = output_shard.size // shard_rows
    output_total = mlp_reduced[:, :output_width].reshape(output_shard.shape)
    gate_total = mlp_reduced[:, output_width : output_width + ff_cols]
    up_total = mlp_reduced[:, output_width + ff_cols : output_width + 2 * ff_cols]
    down_total = mlp_reduced[:, output_width + 2 * ff_cols :].reshape(down_shard.shape)
    query_total = attn_reduced[:, : qkv_cols[0]]
    key_total = attn_reduced[:, qkv_cols[0] : qkv_cols[0] + qkv_cols[1]]
    value_total = attn_reduced[:, qkv_cols[0] + qkv_cols[1] : sum(qkv_cols)]
    at = sum(qkv_cols)
    reduced = attn_reduced
    first_total, second_total, query_gain_total, key_gain_total = (
        reduced[: g.shape[0], at + column] for column, g in enumerate(gain_parts)
    )
    return (
        layer_output[None],
        input_grad[None],
        query_total,
        key_total,
        value_total,
        output_total,
        gate_total,
        up_total,
        down_total,
        first_total,
        second_total,
        query_gain_total,
        key_gain_total,
    )


def solution(mesh):
    in_specs = (
        P(FSDP, CTX, None),
        P(FSDP, CTX, None),
        P(FSDP, None),
        P(FSDP, None),
        P(FSDP, None),
        P(FSDP, None),
        P(FSDP, None),
        P(FSDP, None),
        P(FSDP, None),
        P(FSDP, None),
        P(),
        P(),
        P(),
        P(),
    )
    out_specs = (
        P(FSDP, CTX, None),
        P(FSDP, CTX, None),
        P(FSDP, None),
        P(FSDP, None),
        P(FSDP, None),
        P(FSDP, None),
        P(FSDP, None),
        P(FSDP, None),
        P(FSDP, None),
        P(FSDP),
        P(FSDP),
        P(FSDP),
        P(FSDP),
    )
    torus_mesh = jax.sharding.Mesh(mesh.devices.reshape(2, 4, 4, 2, 2), ("yh", "x", "z", "yl", "c"))
    return jax.shard_map(
        on_device, mesh=torus_mesh, in_specs=in_specs, out_specs=out_specs, check_vma=False
    )
```

```python
import math

import jax
import jax.numpy as jnp
from jax import lax
from jax.sharding import PartitionSpec as P

HQ = 16
KEY_VALUE_HEADS = 8
HEAD_SIZE = 128
CTX = ("yh", "x", "z")
FSDP = ("yl", "c")


EPSILON = 1e-06
THETA = 1000000.0
MASKED = -1e30


def rms_apply(values, norm_gain):
    row_scale = lax.rsqrt(jnp.mean(values * values, axis=-1, keepdims=True) + EPSILON)
    normed = values * row_scale
    return (normed * norm_gain, normed, row_scale)


def root_mean_square_backward(gradient, normed, row_scale, norm_gain):
    normed_grad = gradient * norm_gain
    return row_scale * (
        normed_grad - normed * jnp.mean(normed_grad * normed, axis=-1, keepdims=True)
    )


def rope_tables(positions, head_width):
    half_width = head_width // 2
    inverse_freq = jnp.power(THETA, -2.0 * jnp.arange(half_width, dtype=jnp.float32) / head_width)
    angles = positions.astype(jnp.float32)[:, None] * inverse_freq[None, :]
    return (jnp.cos(angles)[:, None, :], jnp.sin(angles)[:, None, :])


def rotary_apply(values, cosine_table, sine_values_table):
    half_width = values.shape[-1] // 2
    front_half = values[..., :half_width]
    back_half = values[..., half_width:]
    return jnp.concatenate(
        [
            front_half * cosine_table - back_half * sine_values_table,
            back_half * cosine_table + front_half * sine_values_table,
        ],
        axis=-1,
    )


def rotary_backward(gradient, cosine_table, sine_values_table):
    half_width = gradient.shape[-1] // 2
    front_half = gradient[..., :half_width]
    back_half = gradient[..., half_width:]
    return jnp.concatenate(
        [
            front_half * cosine_table + back_half * sine_values_table,
            back_half * cosine_table - front_half * sine_values_table,
        ],
        axis=-1,
    )


def left_dot(left_side, right_side):
    return lax.dot_general(
        left_side, right_side, (((0,), (0,)), ((), ())), preferred_element_type=jnp.float32
    )


def right_dot(left_side, right_side):
    return lax.dot_general(
        left_side, right_side, (((1,), (1,)), ((), ())), preferred_element_type=jnp.float32
    )


def gather_across(values):
    return lax.all_gather(values, "yl", axis=0, tiled=False)


def gather_cores(across, shard_shape):
    other = lax.ppermute(across, "c", [(0, 1), (1, 0)])
    first_core = lax.axis_index("c") == 0
    both = jnp.stack([jnp.where(first_core, across, other), jnp.where(first_core, other, across)], axis=1)
    return both.reshape((-1,) + shard_shape[1:])


def gather_fsdp(values):
    return gather_cores(gather_across(values), values.shape)


def reduce_ctx(packed):
    part = lax.psum_scatter(packed, "z", scatter_dimension=0, tiled=True)
    part = lax.psum_scatter(part, "x", scatter_dimension=0, tiled=True)
    part = (part.astype(jnp.float32) + lax.ppermute(part, "yh", [(0, 1), (1, 0)]).astype(jnp.float32)).astype(
        part.dtype
    )
    part = lax.all_gather(part, "x", axis=0, tiled=True)
    return lax.all_gather(part, "z", axis=0, tiled=True).astype(jnp.float32)


def on_device(
    layer_input,
    cotangent,
    block_order,
    query_weight,
    key_projection,
    value_projection,
    output_weight,
    gate_weight,
    up_weight,
    down_weight,
    first_gain,
    second_gain,
    query_gain,
    key_norm_gain,
):
    local_rows = layer_input.shape[1]
    block_rows = local_rows // 2
    ctx_size = lax.axis_size(CTX)
    halves = ctx_size // HQ
    half_devices = ctx_size // halves
    order_row = block_order[0]
    device_place = lax.axis_index(CTX)
    my_half = device_place // half_devices
    all_positions = (
        order_row[:, None] * block_rows + jnp.arange(block_rows, dtype=jnp.int32)[None, :]
    ).reshape(-1)
    own_positions = lax.dynamic_slice_in_dim(all_positions, device_place * local_rows, local_rows)
    cosine_table, sine_values_table = rope_tables(own_positions, HEAD_SIZE)
    scale_factor = 1.0 / math.sqrt(HEAD_SIZE)
    half_rows = half_devices * local_rows
    query_positions = lax.dynamic_slice_in_dim(all_positions, my_half * half_rows, half_rows)
    allowed = all_positions[None, :] <= query_positions[:, None]
    half_select = (jnp.arange(halves, dtype=jnp.int32) == my_half)[:, None, None, None]

    def to_heads(per_head):
        by_head = jnp.transpose(per_head, (1, 0, 2))
        return jnp.where(half_select, by_head[None], jnp.zeros_like(by_head)[None]).reshape(
            ctx_size, local_rows, per_head.shape[-1]
        )

    def gather_half(received):
        return lax.dynamic_slice_in_dim(received, my_half * half_devices, half_devices, 0).reshape(
            half_rows, received.shape[-1]
        )

    def from_heads(per_head):
        blocks = per_head.reshape(half_devices, local_rows, per_head.shape[-1])
        return jnp.where(half_select, blocks[None], jnp.zeros_like(blocks)[None]).reshape(
            ctx_size, local_rows, per_head.shape[-1]
        )

    def own_heads(received):
        mine = lax.dynamic_slice_in_dim(received, my_half * half_devices, half_devices, 0)
        return jnp.transpose(mine, (1, 0, 2))

    def exchange(values):
        return lax.all_to_all(values, CTX, split_axis=0, concat_axis=0, tiled=True)

    qkv_cols = (query_weight.shape[1], key_projection.shape[1], value_projection.shape[1])
    full_qkv = gather_fsdp(jnp.concatenate([query_weight, key_projection, value_projection], axis=1))
    across_output = gather_across(output_weight)
    ff_cols = gate_weight.shape[1]
    gate_up_weight = jnp.concatenate([gate_weight, up_weight], axis=1)
    across_gate_up = gather_across(gate_up_weight)
    across_down = gather_across(down_weight)
    input_f32 = layer_input[0].astype(jnp.float32)
    gained, first_normed, first_scale = rms_apply(input_f32, first_gain)
    attention_input = gained.astype(jnp.bfloat16)
    qkv_pre = jnp.dot(attention_input, full_qkv, preferred_element_type=jnp.float32)
    query_pre = qkv_pre[:, : qkv_cols[0]].reshape(local_rows, HQ, HEAD_SIZE)
    query_gained, query_normed, query_scale = rms_apply(query_pre, query_gain)
    query_rotated = rotary_apply(query_gained, cosine_table, sine_values_table).astype(jnp.bfloat16)
    key_before_norm = qkv_pre[:, qkv_cols[0] : qkv_cols[0] + qkv_cols[1]].reshape(
        local_rows, KEY_VALUE_HEADS, HEAD_SIZE
    )
    key_after_gain, key_after_norm, key_norm_scale = rms_apply(key_before_norm, key_norm_gain)
    own_keys = rotary_apply(key_after_gain, cosine_table, sine_values_table).astype(jnp.bfloat16)
    own_values = (
        qkv_pre[:, qkv_cols[0] + qkv_cols[1] :]
        .astype(jnp.bfloat16)
        .reshape(local_rows, KEY_VALUE_HEADS, HEAD_SIZE)
    )
    group = HQ // KEY_VALUE_HEADS
    key_value = jnp.repeat(jnp.concatenate([own_keys, own_values], axis=-1), group, axis=1)
    sent = jnp.concatenate([to_heads(query_rotated), jnp.tile(
        jnp.transpose(key_value, (1, 0, 2)), (halves, 1, 1))], axis=-1)
    received = exchange(sent)
    head_query = gather_half(received[..., :HEAD_SIZE])
    head_key = received[..., HEAD_SIZE : 2 * HEAD_SIZE].reshape(-1, HEAD_SIZE)
    head_value = received[..., 2 * HEAD_SIZE :].reshape(-1, HEAD_SIZE)

    def head_scores():
        raw_scores = (
            jnp.einsum("qd,kd->qk", head_query, head_key, preferred_element_type=jnp.float32)
            * scale_factor
        )
        return jnp.where(allowed, raw_scores, MASKED)

    raw_scores = head_scores()
    row_max = jnp.max(raw_scores, axis=-1, keepdims=True)
    log_total = row_max + jnp.log(jnp.sum(jnp.exp(raw_scores - row_max), axis=-1, keepdims=True))
    weights_b = jnp.exp(raw_scores - log_total).astype(jnp.bfloat16)
    head_mixed = jnp.dot(weights_b, head_value, preferred_element_type=jnp.float32)
    head_mixed, across_output, across_gate_up, across_down = lax.optimization_barrier(
        (head_mixed, across_output, across_gate_up, across_down)
    )
    full_output = gather_cores(across_output, output_weight.shape)
    full_gate_up = gather_cores(across_gate_up, gate_up_weight.shape)
    full_down = gather_cores(across_down, down_weight.shape)
    mixed_b = own_heads(exchange(from_heads(head_mixed.astype(jnp.bfloat16)))).reshape(
        local_rows, HQ * HEAD_SIZE
    )
    residual_mid = input_f32 + jnp.dot(mixed_b, full_output, preferred_element_type=jnp.float32)
    gained_mid, second_normed, second_scale = rms_apply(residual_mid, second_gain)
    mlp_in = gained_mid.astype(jnp.bfloat16)
    gate_up_pre = jnp.dot(mlp_in, full_gate_up, preferred_element_type=jnp.float32)
    gate_pre = gate_up_pre[:, :ff_cols]
    up_pre = gate_up_pre[:, ff_cols:]
    sigmoid_gate = jax.nn.sigmoid(gate_pre)
    silu_gate = gate_pre * sigmoid_gate
    hidden = (silu_gate * up_pre).astype(jnp.bfloat16)
    layer_output = (
        residual_mid + jnp.dot(hidden, full_down, preferred_element_type=jnp.float32)
    ).astype(jnp.bfloat16)
    own_cotangent = cotangent[0]
    hidden_grad = right_dot(own_cotangent, full_down)
    gate_grad = (
        hidden_grad * up_pre * sigmoid_gate * (1.0 + gate_pre * (1.0 - sigmoid_gate))
    ).astype(jnp.bfloat16)
    up_grad = (hidden_grad * silu_gate).astype(jnp.bfloat16)
    gate_up_grad = jnp.concatenate([gate_grad, up_grad], axis=1)
    mlp_in_grad = right_dot(gate_up_grad, full_gate_up)
    second_gain_grad = jnp.sum(mlp_in_grad * second_normed, axis=0)
    mid_grad = own_cotangent.astype(jnp.float32) + root_mean_square_backward(
        mlp_in_grad, second_normed, second_scale, second_gain
    )
    mid_grad_b = mid_grad.astype(jnp.bfloat16)
    mixed_gradient = right_dot(mid_grad_b, full_output).astype(jnp.bfloat16)
    fsdp_size = lax.axis_size(FSDP)
    col_parts = (attention_input, mixed_b, mlp_in, hidden)
    widths = [p.shape[1] // fsdp_size for p in col_parts]
    stacked = jnp.concatenate(
        [p.reshape(local_rows, fsdp_size, w) for p, w in zip(col_parts, widths)], axis=2
    )
    cols = lax.all_to_all(stacked, FSDP, split_axis=1, concat_axis=0, tiled=True).reshape(
        fsdp_size * local_rows, sum(widths)
    )
    bounds = [sum(widths[:i]) for i in range(5)]
    attn_cols, mixed_cols, mlp_cols, hidden_cols = (
        cols[:, bounds[i] : bounds[i + 1]] for i in range(4)
    )
    gate_up_rows = lax.all_gather(gate_up_grad, FSDP, axis=0, tiled=True)
    cot_mid_rows = lax.all_gather(
        jnp.concatenate([own_cotangent, mid_grad_b], axis=1), FSDP, axis=0, tiled=True
    )
    model_width = own_cotangent.shape[1]
    output_shard = left_dot(mixed_cols, cot_mid_rows[:, model_width:])
    gate_up_shard = left_dot(mlp_cols, gate_up_rows)
    down_shard = left_dot(hidden_cols, cot_mid_rows[:, :model_width])
    mlp_rows = gate_up_shard.shape[0]
    mlp_packed = jnp.concatenate(
        [output_shard.reshape(mlp_rows, -1), gate_up_shard, down_shard.reshape(mlp_rows, -1)],
        axis=1,
    ).astype(jnp.bfloat16)
    head_out_grad = gather_half(
        exchange(to_heads(mixed_gradient.reshape(local_rows, HQ, HEAD_SIZE)))
    )
    mlp_packed, head_out_grad = lax.optimization_barrier((mlp_packed, head_out_grad))
    mlp_reduced = reduce_ctx(mlp_packed)
    out_grad_f = head_out_grad.astype(jnp.float32)
    delta = jnp.sum(out_grad_f * head_mixed, axis=-1, keepdims=True)
    probabilities = jnp.exp(head_scores() - log_total)
    value_part = left_dot(probabilities.astype(jnp.bfloat16), head_out_grad)
    prob_grad = right_dot(head_out_grad, head_value)
    score_grad = (probabilities * (prob_grad - delta)).astype(jnp.bfloat16)
    query_part = jnp.dot(score_grad, head_key, preferred_element_type=jnp.float32) * scale_factor
    key_part = left_dot(score_grad, head_query) * scale_factor
    returned = exchange(jnp.concatenate([
        from_heads(query_part.astype(jnp.bfloat16)),
        jnp.concatenate([key_part, value_part], axis=-1).astype(jnp.bfloat16).reshape(
            ctx_size, local_rows, 2 * HEAD_SIZE),
    ], axis=-1))
    query_grad_rows = own_heads(returned[..., :HEAD_SIZE]).astype(jnp.float32)
    kv_parts = returned[..., HEAD_SIZE:].astype(jnp.float32).reshape(
        halves, KEY_VALUE_HEADS, group, local_rows, 2 * HEAD_SIZE)
    kv_grad = jnp.transpose(jnp.sum(kv_parts, axis=(0, 2)), (1, 0, 2))
    local_key_gradient = kv_grad[..., :HEAD_SIZE]
    own_value_grad = kv_grad[..., HEAD_SIZE:].reshape(local_rows, KEY_VALUE_HEADS * HEAD_SIZE)
    query_back = rotary_backward(query_grad_rows, cosine_table, sine_values_table)
    query_gain_grad = jnp.sum(query_back * query_normed, axis=(0, 1))
    query_pre_grad = (
        root_mean_square_backward(query_back, query_normed, query_scale, query_gain)
        .astype(jnp.bfloat16)
        .reshape(local_rows, HQ * HEAD_SIZE)
    )
    key_backward_pass = rotary_backward(
        local_key_gradient,
        cosine_table,
        sine_values_table,
    )
    key_gain_grad = jnp.sum(key_backward_pass * key_after_norm, axis=(0, 1))
    key_before_norm_gradient = (
        root_mean_square_backward(key_backward_pass, key_after_norm, key_norm_scale, key_norm_gain)
        .astype(jnp.bfloat16)
        .reshape(local_rows, KEY_VALUE_HEADS * HEAD_SIZE)
    )
    value_gradient_second = own_value_grad.astype(jnp.bfloat16)
    qkv_grad = jnp.concatenate([query_pre_grad, key_before_norm_gradient, value_gradient_second], axis=1)
    attn_in_grad = (
        right_dot(qkv_grad, full_qkv)
    )
    first_gain_grad = jnp.sum(attn_in_grad * first_normed, axis=0)
    input_grad = mid_grad + root_mean_square_backward(
        attn_in_grad, first_normed, first_scale, first_gain
    )
    qkv_rows = lax.all_gather(qkv_grad, FSDP, axis=0, tiled=True)
    first_shard, second_shard, query_gain_shard, key_gain_shard = (
        lax.psum_scatter(first_gain_grad, FSDP, scatter_dimension=0, tiled=True),
        lax.psum_scatter(second_gain_grad, FSDP, scatter_dimension=0, tiled=True),
        lax.psum_scatter(query_gain_grad, FSDP, scatter_dimension=0, tiled=True),
        lax.psum_scatter(key_gain_grad, FSDP, scatter_dimension=0, tiled=True),
    )
    qkv_shard = left_dot(attn_cols, qkv_rows)
    shard_rows = qkv_shard.shape[0]
    gain_parts = (first_shard, second_shard, query_gain_shard, key_gain_shard)
    gain_block = jnp.zeros((shard_rows, 128), jnp.float32)
    for column, g in enumerate(gain_parts):
        gain_block = gain_block.at[: g.shape[0], column].set(g)
    attn_reduced = reduce_ctx(jnp.concatenate([qkv_shard, gain_block], axis=1).astype(jnp.bfloat16))
    output_width = output_shard.size // shard_rows
    output_total = mlp_reduced[:, :output_width].reshape(output_shard.shape)
    gate_total = mlp_reduced[:, output_width : output_width + ff_cols]
    up_total = mlp_reduced[:, output_width + ff_cols : output_width + 2 * ff_cols]
    down_total = mlp_reduced[:, output_width + 2 * ff_cols :].reshape(down_shard.shape)
    query_total = attn_reduced[:, : qkv_cols[0]]
    key_total = attn_reduced[:, qkv_cols[0] : qkv_cols[0] + qkv_cols[1]]
    value_total = attn_reduced[:, qkv_cols[0] + qkv_cols[1] : sum(qkv_cols)]
    at = sum(qkv_cols)
    reduced = attn_reduced
    first_total, second_total, query_gain_total, key_gain_total = (
        reduced[: g.shape[0], at + column] for column, g in enumerate(gain_parts)
    )
    return (
        layer_output[None],
        input_grad[None],
        query_total,
        key_total,
        value_total,
        output_total,
        gate_total,
        up_total,
        down_total,
        first_total,
        second_total,
        query_gain_total,
        key_gain_total,
    )


def solution(mesh):
    in_specs = (
        P(FSDP, CTX, None),
        P(FSDP, CTX, None),
        P(FSDP, None),
        P(FSDP, None),
        P(FSDP, None),
        P(FSDP, None),
        P(FSDP, None),
        P(FSDP, None),
        P(FSDP, None),
        P(FSDP, None),
        P(),
        P(),
        P(),
        P(),
    )
    out_specs = (
        P(FSDP, CTX, None),
        P(FSDP, CTX, None),
        P(FSDP, None),
        P(FSDP, None),
        P(FSDP, None),
        P(FSDP, None),
        P(FSDP, None),
        P(FSDP, None),
        P(FSDP, None),
        P(FSDP),
        P(FSDP),
        P(FSDP),
        P(FSDP),
    )
    torus_mesh = jax.sharding.Mesh(mesh.devices.reshape(2, 4, 4, 2, 2), ("yh", "x", "z", "yl", "c"))
    return jax.shard_map(
        on_device, mesh=torus_mesh, in_specs=in_specs, out_specs=out_specs, check_vma=False
    )
```

```python
import math

import jax
import jax.numpy as jnp
from jax import lax
from jax.sharding import PartitionSpec as P

HQ = 16
KEY_VALUE_HEADS = 8
HEAD_SIZE = 128
CTX = ("yh", "x", "z")
FSDP = ("yl", "c")


EPSILON = 1e-06
THETA = 1000000.0
MASKED = -1e30


def rms_apply(values, norm_gain):
    row_scale = lax.rsqrt(jnp.mean(values * values, axis=-1, keepdims=True) + EPSILON)
    normed = values * row_scale
    return (normed * norm_gain, normed, row_scale)


def root_mean_square_backward(gradient, normed, row_scale, norm_gain):
    normed_grad = gradient * norm_gain
    return row_scale * (
        normed_grad - normed * jnp.mean(normed_grad * normed, axis=-1, keepdims=True)
    )


def rope_tables(positions, head_width):
    half_width = head_width // 2
    inverse_freq = jnp.power(THETA, -2.0 * jnp.arange(half_width, dtype=jnp.float32) / head_width)
    angles = positions.astype(jnp.float32)[:, None] * inverse_freq[None, :]
    return (jnp.cos(angles)[:, None, :], jnp.sin(angles)[:, None, :])


def rotary_apply(values, cosine_table, sine_values_table):
    half_width = values.shape[-1] // 2
    front_half = values[..., :half_width]
    back_half = values[..., half_width:]
    return jnp.concatenate(
        [
            front_half * cosine_table - back_half * sine_values_table,
            back_half * cosine_table + front_half * sine_values_table,
        ],
        axis=-1,
    )


def rotary_backward(gradient, cosine_table, sine_values_table):
    half_width = gradient.shape[-1] // 2
    front_half = gradient[..., :half_width]
    back_half = gradient[..., half_width:]
    return jnp.concatenate(
        [
            front_half * cosine_table + back_half * sine_values_table,
            back_half * cosine_table - front_half * sine_values_table,
        ],
        axis=-1,
    )


def left_dot(left_side, right_side):
    return lax.dot_general(
        left_side, right_side, (((0,), (0,)), ((), ())), preferred_element_type=jnp.float32
    )


def right_dot(left_side, right_side):
    return lax.dot_general(
        left_side, right_side, (((1,), (1,)), ((), ())), preferred_element_type=jnp.float32
    )


def gather_across(values):
    return lax.all_gather(values, "yl", axis=0, tiled=False)


def gather_cores(across, shard_shape):
    other = lax.ppermute(across, "c", [(0, 1), (1, 0)])
    first_core = lax.axis_index("c") == 0
    both = jnp.stack([jnp.where(first_core, across, other), jnp.where(first_core, other, across)], axis=1)
    return both.reshape((-1,) + shard_shape[1:])


def gather_fsdp(values):
    return gather_cores(gather_across(values), values.shape)


def scatter_ctx(packed):
    part = lax.psum_scatter(packed, "z", scatter_dimension=0, tiled=True)
    part = lax.psum_scatter(part, "x", scatter_dimension=0, tiled=True)
    return (part.astype(jnp.float32) + lax.ppermute(part, "yh", [(0, 1), (1, 0)]).astype(jnp.float32)).astype(
        part.dtype
    )


def gather_ctx(part):
    part = lax.all_gather(part, "x", axis=0, tiled=True)
    return lax.all_gather(part, "z", axis=0, tiled=True).astype(jnp.float32)


def reduce_ctx(packed):
    return gather_ctx(scatter_ctx(packed))


def on_device(
    layer_input,
    cotangent,
    block_order,
    query_weight,
    key_projection,
    value_projection,
    output_weight,
    gate_weight,
    up_weight,
    down_weight,
    first_gain,
    second_gain,
    query_gain,
    key_norm_gain,
):
    local_rows = layer_input.shape[1]
    block_rows = local_rows // 2
    ctx_size = lax.axis_size(CTX)
    halves = ctx_size // HQ
    half_devices = ctx_size // halves
    order_row = block_order[0]
    device_place = lax.axis_index(CTX)
    my_half = device_place // half_devices
    all_positions = (
        order_row[:, None] * block_rows + jnp.arange(block_rows, dtype=jnp.int32)[None, :]
    ).reshape(-1)
    own_positions = lax.dynamic_slice_in_dim(all_positions, device_place * local_rows, local_rows)
    cosine_table, sine_values_table = rope_tables(own_positions, HEAD_SIZE)
    scale_factor = 1.0 / math.sqrt(HEAD_SIZE)
    half_rows = half_devices * local_rows
    query_positions = lax.dynamic_slice_in_dim(all_positions, my_half * half_rows, half_rows)
    allowed = all_positions[None, :] <= query_positions[:, None]
    half_select = (jnp.arange(halves, dtype=jnp.int32) == my_half)[:, None, None, None]

    def to_heads(per_head):
        by_head = jnp.transpose(per_head, (1, 0, 2))
        return jnp.where(half_select, by_head[None], jnp.zeros_like(by_head)[None]).reshape(
            ctx_size, local_rows, per_head.shape[-1]
        )

    def gather_half(received):
        return lax.dynamic_slice_in_dim(received, my_half * half_devices, half_devices, 0).reshape(
            half_rows, received.shape[-1]
        )

    def from_heads(per_head):
        blocks = per_head.reshape(half_devices, local_rows, per_head.shape[-1])
        return jnp.where(half_select, blocks[None], jnp.zeros_like(blocks)[None]).reshape(
            ctx_size, local_rows, per_head.shape[-1]
        )

    def own_heads(received):
        mine = lax.dynamic_slice_in_dim(received, my_half * half_devices, half_devices, 0)
        return jnp.transpose(mine, (1, 0, 2))

    def exchange(values):
        return lax.all_to_all(values, CTX, split_axis=0, concat_axis=0, tiled=True)

    qkv_cols = (query_weight.shape[1], key_projection.shape[1], value_projection.shape[1])
    full_qkv = gather_fsdp(jnp.concatenate([query_weight, key_projection, value_projection], axis=1))
    across_output = gather_across(output_weight)
    ff_cols = gate_weight.shape[1]
    gate_up_weight = jnp.concatenate([gate_weight, up_weight], axis=1)
    across_gate_up = gather_across(gate_up_weight)
    across_down = gather_across(down_weight)
    input_f32 = layer_input[0].astype(jnp.float32)
    gained, first_normed, first_scale = rms_apply(input_f32, first_gain)
    attention_input = gained.astype(jnp.bfloat16)
    qkv_pre = jnp.dot(attention_input, full_qkv, preferred_element_type=jnp.float32)
    query_pre = qkv_pre[:, : qkv_cols[0]].reshape(local_rows, HQ, HEAD_SIZE)
    query_gained, query_normed, query_scale = rms_apply(query_pre, query_gain)
    query_rotated = rotary_apply(query_gained, cosine_table, sine_values_table).astype(jnp.bfloat16)
    key_before_norm = qkv_pre[:, qkv_cols[0] : qkv_cols[0] + qkv_cols[1]].reshape(
        local_rows, KEY_VALUE_HEADS, HEAD_SIZE
    )
    key_after_gain, key_after_norm, key_norm_scale = rms_apply(key_before_norm, key_norm_gain)
    own_keys = rotary_apply(key_after_gain, cosine_table, sine_values_table).astype(jnp.bfloat16)
    own_values = (
        qkv_pre[:, qkv_cols[0] + qkv_cols[1] :]
        .astype(jnp.bfloat16)
        .reshape(local_rows, KEY_VALUE_HEADS, HEAD_SIZE)
    )
    group = HQ // KEY_VALUE_HEADS
    key_value = jnp.repeat(jnp.concatenate([own_keys, own_values], axis=-1), group, axis=1)
    sent = jnp.concatenate([to_heads(query_rotated), jnp.tile(
        jnp.transpose(key_value, (1, 0, 2)), (halves, 1, 1))], axis=-1)
    received = exchange(sent)
    head_query = gather_half(received[..., :HEAD_SIZE])
    head_key = received[..., HEAD_SIZE : 2 * HEAD_SIZE].reshape(-1, HEAD_SIZE)
    head_value = received[..., 2 * HEAD_SIZE :].reshape(-1, HEAD_SIZE)

    def head_scores():
        raw_scores = (
            jnp.einsum("qd,kd->qk", head_query, head_key, preferred_element_type=jnp.float32)
            * scale_factor
        )
        return jnp.where(allowed, raw_scores, MASKED)

    raw_scores = head_scores()
    row_max = jnp.max(raw_scores, axis=-1, keepdims=True)
    log_total = row_max + jnp.log(jnp.sum(jnp.exp(raw_scores - row_max), axis=-1, keepdims=True))
    weights_b = jnp.exp(raw_scores - log_total).astype(jnp.bfloat16)
    head_mixed = jnp.dot(weights_b, head_value, preferred_element_type=jnp.float32)
    head_mixed, across_output, across_gate_up, across_down = lax.optimization_barrier(
        (head_mixed, across_output, across_gate_up, across_down)
    )
    full_output = gather_cores(across_output, output_weight.shape)
    full_gate_up = gather_cores(across_gate_up, gate_up_weight.shape)
    full_down = gather_cores(across_down, down_weight.shape)
    mixed_b = own_heads(exchange(from_heads(head_mixed.astype(jnp.bfloat16)))).reshape(
        local_rows, HQ * HEAD_SIZE
    )
    residual_mid = input_f32 + jnp.dot(mixed_b, full_output, preferred_element_type=jnp.float32)
    gained_mid, second_normed, second_scale = rms_apply(residual_mid, second_gain)
    mlp_in = gained_mid.astype(jnp.bfloat16)
    gate_up_pre = jnp.dot(mlp_in, full_gate_up, preferred_element_type=jnp.float32)
    gate_pre = gate_up_pre[:, :ff_cols]
    up_pre = gate_up_pre[:, ff_cols:]
    sigmoid_gate = jax.nn.sigmoid(gate_pre)
    silu_gate = gate_pre * sigmoid_gate
    hidden = (silu_gate * up_pre).astype(jnp.bfloat16)
    layer_output = (
        residual_mid + jnp.dot(hidden, full_down, preferred_element_type=jnp.float32)
    ).astype(jnp.bfloat16)
    own_cotangent = cotangent[0]
    hidden_grad = right_dot(own_cotangent, full_down)
    gate_grad = (
        hidden_grad * up_pre * sigmoid_gate * (1.0 + gate_pre * (1.0 - sigmoid_gate))
    ).astype(jnp.bfloat16)
    up_grad = (hidden_grad * silu_gate).astype(jnp.bfloat16)
    gate_up_grad = jnp.concatenate([gate_grad, up_grad], axis=1)
    mlp_in_grad = right_dot(gate_up_grad, full_gate_up)
    second_gain_grad = jnp.sum(mlp_in_grad * second_normed, axis=0)
    mid_grad = own_cotangent.astype(jnp.float32) + root_mean_square_backward(
        mlp_in_grad, second_normed, second_scale, second_gain
    )
    mid_grad_b = mid_grad.astype(jnp.bfloat16)
    mixed_gradient = right_dot(mid_grad_b, full_output).astype(jnp.bfloat16)
    fsdp_size = lax.axis_size(FSDP)
    col_parts = (attention_input, mixed_b, mlp_in, hidden)
    widths = [p.shape[1] // fsdp_size for p in col_parts]
    stacked = jnp.concatenate(
        [p.reshape(local_rows, fsdp_size, w) for p, w in zip(col_parts, widths)], axis=2
    )
    cols = lax.all_to_all(stacked, FSDP, split_axis=1, concat_axis=0, tiled=True).reshape(
        fsdp_size * local_rows, sum(widths)
    )
    bounds = [sum(widths[:i]) for i in range(5)]
    attn_cols, mixed_cols, mlp_cols, hidden_cols = (
        cols[:, bounds[i] : bounds[i + 1]] for i in range(4)
    )
    gate_up_rows = lax.all_gather(gate_up_grad, FSDP, axis=0, tiled=True)
    cot_mid_rows = lax.all_gather(
        jnp.concatenate([own_cotangent, mid_grad_b], axis=1), FSDP, axis=0, tiled=True
    )
    model_width = own_cotangent.shape[1]
    output_shard = left_dot(mixed_cols, cot_mid_rows[:, model_width:])
    gate_up_shard = left_dot(mlp_cols, gate_up_rows)
    down_shard = left_dot(hidden_cols, cot_mid_rows[:, :model_width])
    mlp_rows = gate_up_shard.shape[0]
    mlp_packed = jnp.concatenate(
        [output_shard.reshape(mlp_rows, -1), gate_up_shard, down_shard.reshape(mlp_rows, -1)],
        axis=1,
    ).astype(jnp.bfloat16)
    head_out_grad = gather_half(
        exchange(to_heads(mixed_gradient.reshape(local_rows, HQ, HEAD_SIZE)))
    )
    mlp_packed, head_out_grad = lax.optimization_barrier((mlp_packed, head_out_grad))
    mlp_part = scatter_ctx(mlp_packed)
    out_grad_f = head_out_grad.astype(jnp.float32)
    delta = jnp.sum(out_grad_f * head_mixed, axis=-1, keepdims=True)
    probabilities = jnp.exp(head_scores() - log_total)
    value_part = left_dot(probabilities.astype(jnp.bfloat16), head_out_grad)
    prob_grad = right_dot(head_out_grad, head_value)
    score_grad = (probabilities * (prob_grad - delta)).astype(jnp.bfloat16)
    query_part = jnp.dot(score_grad, head_key, preferred_element_type=jnp.float32) * scale_factor
    key_part = left_dot(score_grad, head_query) * scale_factor
    returned = exchange(jnp.concatenate([
        from_heads(query_part.astype(jnp.bfloat16)),
        jnp.concatenate([key_part, value_part], axis=-1).astype(jnp.bfloat16).reshape(
            ctx_size, local_rows, 2 * HEAD_SIZE),
    ], axis=-1))
    mlp_part, returned = lax.optimization_barrier((mlp_part, returned))
    mlp_reduced = gather_ctx(mlp_part)
    query_grad_rows = own_heads(returned[..., :HEAD_SIZE]).astype(jnp.float32)
    kv_parts = returned[..., HEAD_SIZE:].astype(jnp.float32).reshape(
        halves, KEY_VALUE_HEADS, group, local_rows, 2 * HEAD_SIZE)
    kv_grad = jnp.transpose(jnp.sum(kv_parts, axis=(0, 2)), (1, 0, 2))
    local_key_gradient = kv_grad[..., :HEAD_SIZE]
    own_value_grad = kv_grad[..., HEAD_SIZE:].reshape(local_rows, KEY_VALUE_HEADS * HEAD_SIZE)
    query_back = rotary_backward(query_grad_rows, cosine_table, sine_values_table)
    query_gain_grad = jnp.sum(query_back * query_normed, axis=(0, 1))
    query_pre_grad = (
        root_mean_square_backward(query_back, query_normed, query_scale, query_gain)
        .astype(jnp.bfloat16)
        .reshape(local_rows, HQ * HEAD_SIZE)
    )
    key_backward_pass = rotary_backward(
        local_key_gradient,
        cosine_table,
        sine_values_table,
    )
    key_gain_grad = jnp.sum(key_backward_pass * key_after_norm, axis=(0, 1))
    key_before_norm_gradient = (
        root_mean_square_backward(key_backward_pass, key_after_norm, key_norm_scale, key_norm_gain)
        .astype(jnp.bfloat16)
        .reshape(local_rows, KEY_VALUE_HEADS * HEAD_SIZE)
    )
    value_gradient_second = own_value_grad.astype(jnp.bfloat16)
    qkv_grad = jnp.concatenate([query_pre_grad, key_before_norm_gradient, value_gradient_second], axis=1)
    attn_in_grad = (
        right_dot(qkv_grad, full_qkv)
    )
    first_gain_grad = jnp.sum(attn_in_grad * first_normed, axis=0)
    input_grad = mid_grad + root_mean_square_backward(
        attn_in_grad, first_normed, first_scale, first_gain
    )
    qkv_rows = lax.all_gather(qkv_grad, FSDP, axis=0, tiled=True)
    first_shard, second_shard, query_gain_shard, key_gain_shard = (
        lax.psum_scatter(first_gain_grad, FSDP, scatter_dimension=0, tiled=True),
        lax.psum_scatter(second_gain_grad, FSDP, scatter_dimension=0, tiled=True),
        lax.psum_scatter(query_gain_grad, FSDP, scatter_dimension=0, tiled=True),
        lax.psum_scatter(key_gain_grad, FSDP, scatter_dimension=0, tiled=True),
    )
    qkv_shard = left_dot(attn_cols, qkv_rows)
    shard_rows = qkv_shard.shape[0]
    gain_parts = (first_shard, second_shard, query_gain_shard, key_gain_shard)
    gain_block = jnp.zeros((shard_rows, 128), jnp.float32)
    for column, g in enumerate(gain_parts):
        gain_block = gain_block.at[: g.shape[0], column].set(g)
    attn_reduced = reduce_ctx(jnp.concatenate([qkv_shard, gain_block], axis=1).astype(jnp.bfloat16))
    output_width = output_shard.size // shard_rows
    output_total = mlp_reduced[:, :output_width].reshape(output_shard.shape)
    gate_total = mlp_reduced[:, output_width : output_width + ff_cols]
    up_total = mlp_reduced[:, output_width + ff_cols : output_width + 2 * ff_cols]
    down_total = mlp_reduced[:, output_width + 2 * ff_cols :].reshape(down_shard.shape)
    query_total = attn_reduced[:, : qkv_cols[0]]
    key_total = attn_reduced[:, qkv_cols[0] : qkv_cols[0] + qkv_cols[1]]
    value_total = attn_reduced[:, qkv_cols[0] + qkv_cols[1] : sum(qkv_cols)]
    at = sum(qkv_cols)
    reduced = attn_reduced
    first_total, second_total, query_gain_total, key_gain_total = (
        reduced[: g.shape[0], at + column] for column, g in enumerate(gain_parts)
    )
    return (
        layer_output[None],
        input_grad[None],
        query_total,
        key_total,
        value_total,
        output_total,
        gate_total,
        up_total,
        down_total,
        first_total,
        second_total,
        query_gain_total,
        key_gain_total,
    )


def solution(mesh):
    in_specs = (
        P(FSDP, CTX, None),
        P(FSDP, CTX, None),
        P(FSDP, None),
        P(FSDP, None),
        P(FSDP, None),
        P(FSDP, None),
        P(FSDP, None),
        P(FSDP, None),
        P(FSDP, None),
        P(FSDP, None),
        P(),
        P(),
        P(),
        P(),
    )
    out_specs = (
        P(FSDP, CTX, None),
        P(FSDP, CTX, None),
        P(FSDP, None),
        P(FSDP, None),
        P(FSDP, None),
        P(FSDP, None),
        P(FSDP, None),
        P(FSDP, None),
        P(FSDP, None),
        P(FSDP),
        P(FSDP),
        P(FSDP),
        P(FSDP),
    )
    torus_mesh = jax.sharding.Mesh(mesh.devices.reshape(2, 4, 4, 2, 2), ("yh", "x", "z", "yl", "c"))
    return jax.shard_map(
        on_device, mesh=torus_mesh, in_specs=in_specs, out_specs=out_specs, check_vma=False
    )
```

```python
import math

import jax
import jax.numpy as jnp
from jax import lax
from jax.sharding import PartitionSpec as P

HQ = 16
KEY_VALUE_HEADS = 8
HEAD_SIZE = 128
CTX = ("yh", "x", "z")
FSDP = ("yl", "c")


EPSILON = 1e-06
THETA = 1000000.0
MASKED = -1e30


def rms_apply(values, norm_gain):
    row_scale = lax.rsqrt(jnp.mean(values * values, axis=-1, keepdims=True) + EPSILON)
    normed = values * row_scale
    return (normed * norm_gain, normed, row_scale)


def root_mean_square_backward(gradient, normed, row_scale, norm_gain):
    normed_grad = gradient * norm_gain
    return row_scale * (
        normed_grad - normed * jnp.mean(normed_grad * normed, axis=-1, keepdims=True)
    )


def rope_tables(positions, head_width):
    half_width = head_width // 2
    inverse_freq = jnp.power(THETA, -2.0 * jnp.arange(half_width, dtype=jnp.float32) / head_width)
    angles = positions.astype(jnp.float32)[:, None] * inverse_freq[None, :]
    return (jnp.cos(angles)[:, None, :], jnp.sin(angles)[:, None, :])


def rotary_apply(values, cosine_table, sine_values_table):
    half_width = values.shape[-1] // 2
    front_half = values[..., :half_width]
    back_half = values[..., half_width:]
    return jnp.concatenate(
        [
            front_half * cosine_table - back_half * sine_values_table,
            back_half * cosine_table + front_half * sine_values_table,
        ],
        axis=-1,
    )


def rotary_backward(gradient, cosine_table, sine_values_table):
    half_width = gradient.shape[-1] // 2
    front_half = gradient[..., :half_width]
    back_half = gradient[..., half_width:]
    return jnp.concatenate(
        [
            front_half * cosine_table + back_half * sine_values_table,
            back_half * cosine_table - front_half * sine_values_table,
        ],
        axis=-1,
    )


def left_dot(left_side, right_side):
    return lax.dot_general(
        left_side, right_side, (((0,), (0,)), ((), ())), preferred_element_type=jnp.float32
    )


def right_dot(left_side, right_side):
    return lax.dot_general(
        left_side, right_side, (((1,), (1,)), ((), ())), preferred_element_type=jnp.float32
    )


def gather_across(values):
    return lax.all_gather(values, "yl", axis=0, tiled=False)


def gather_cores(across, shard_shape):
    other = lax.ppermute(across, "c", [(0, 1), (1, 0)])
    first_core = lax.axis_index("c") == 0
    both = jnp.stack([jnp.where(first_core, across, other), jnp.where(first_core, other, across)], axis=1)
    return both.reshape((-1,) + shard_shape[1:])


def gather_fsdp(values):
    return gather_cores(gather_across(values), values.shape)


def scatter_ctx(packed):
    part = lax.psum_scatter(packed, "z", scatter_dimension=0, tiled=True)
    part = lax.psum_scatter(part, "x", scatter_dimension=0, tiled=True)
    return (part.astype(jnp.float32) + lax.ppermute(part, "yh", [(0, 1), (1, 0)]).astype(jnp.float32)).astype(
        part.dtype
    )


def gather_ctx(part):
    part = lax.all_gather(part, "x", axis=0, tiled=True)
    return lax.all_gather(part, "z", axis=0, tiled=True).astype(jnp.float32)


def reduce_ctx(packed):
    return gather_ctx(scatter_ctx(packed))


def on_device(
    layer_input,
    cotangent,
    block_order,
    query_weight,
    key_projection,
    value_projection,
    output_weight,
    gate_weight,
    up_weight,
    down_weight,
    first_gain,
    second_gain,
    query_gain,
    key_norm_gain,
):
    local_rows = layer_input.shape[1]
    block_rows = local_rows // 2
    ctx_size = lax.axis_size(CTX)
    halves = ctx_size // HQ
    half_devices = ctx_size // halves
    order_row = block_order[0]
    device_place = lax.axis_index(CTX)
    my_half = device_place // half_devices
    all_positions = (
        order_row[:, None] * block_rows + jnp.arange(block_rows, dtype=jnp.int32)[None, :]
    ).reshape(-1)
    own_positions = lax.dynamic_slice_in_dim(all_positions, device_place * local_rows, local_rows)
    cosine_table, sine_values_table = rope_tables(own_positions, HEAD_SIZE)
    scale_factor = 1.0 / math.sqrt(HEAD_SIZE)
    half_rows = half_devices * local_rows
    query_positions = lax.dynamic_slice_in_dim(all_positions, my_half * half_rows, half_rows)
    allowed = all_positions[None, :] <= query_positions[:, None]
    half_select = (jnp.arange(halves, dtype=jnp.int32) == my_half)[:, None, None, None]

    def to_heads(per_head):
        by_head = jnp.transpose(per_head, (1, 0, 2))
        return jnp.where(half_select, by_head[None], jnp.zeros_like(by_head)[None]).reshape(
            ctx_size, local_rows, per_head.shape[-1]
        )

    def gather_half(received):
        return lax.dynamic_slice_in_dim(received, my_half * half_devices, half_devices, 0).reshape(
            half_rows, received.shape[-1]
        )

    def from_heads(per_head):
        blocks = per_head.reshape(half_devices, local_rows, per_head.shape[-1])
        return jnp.where(half_select, blocks[None], jnp.zeros_like(blocks)[None]).reshape(
            ctx_size, local_rows, per_head.shape[-1]
        )

    def own_heads(received):
        mine = lax.dynamic_slice_in_dim(received, my_half * half_devices, half_devices, 0)
        return jnp.transpose(mine, (1, 0, 2))

    def exchange(values):
        return lax.all_to_all(values, CTX, split_axis=0, concat_axis=0, tiled=True)

    qkv_cols = (query_weight.shape[1], key_projection.shape[1], value_projection.shape[1])
    full_qkv = gather_fsdp(jnp.concatenate([query_weight, key_projection, value_projection], axis=1))
    across_output = gather_across(output_weight)
    ff_cols = gate_weight.shape[1]
    gate_up_weight = jnp.concatenate([gate_weight, up_weight], axis=1)
    across_gate_up = gather_across(gate_up_weight)
    across_down = gather_across(down_weight)
    input_f32 = layer_input[0].astype(jnp.float32)
    gained, first_normed, first_scale = rms_apply(input_f32, first_gain)
    attention_input = gained.astype(jnp.bfloat16)
    qkv_pre = jnp.dot(attention_input, full_qkv, preferred_element_type=jnp.float32)
    query_pre = qkv_pre[:, : qkv_cols[0]].reshape(local_rows, HQ, HEAD_SIZE)
    query_gained, query_normed, query_scale = rms_apply(query_pre, query_gain)
    query_rotated = rotary_apply(query_gained, cosine_table, sine_values_table).astype(jnp.bfloat16)
    key_before_norm = qkv_pre[:, qkv_cols[0] : qkv_cols[0] + qkv_cols[1]].reshape(
        local_rows, KEY_VALUE_HEADS, HEAD_SIZE
    )
    key_after_gain, key_after_norm, key_norm_scale = rms_apply(key_before_norm, key_norm_gain)
    own_keys = rotary_apply(key_after_gain, cosine_table, sine_values_table).astype(jnp.bfloat16)
    own_values = (
        qkv_pre[:, qkv_cols[0] + qkv_cols[1] :]
        .astype(jnp.bfloat16)
        .reshape(local_rows, KEY_VALUE_HEADS, HEAD_SIZE)
    )
    group = HQ // KEY_VALUE_HEADS
    key_value = jnp.repeat(jnp.concatenate([own_keys, own_values], axis=-1), group, axis=1)
    sent = jnp.concatenate([to_heads(query_rotated), jnp.tile(
        jnp.transpose(key_value, (1, 0, 2)), (halves, 1, 1))], axis=-1)
    received = exchange(sent)
    head_query = gather_half(received[..., :HEAD_SIZE])
    head_key = received[..., HEAD_SIZE : 2 * HEAD_SIZE].reshape(-1, HEAD_SIZE)
    head_value = received[..., 2 * HEAD_SIZE :].reshape(-1, HEAD_SIZE)

    def head_scores():
        raw_scores = (
            jnp.einsum("qd,kd->qk", head_query, head_key, preferred_element_type=jnp.float32)
            * scale_factor
        )
        return jnp.where(allowed, raw_scores, MASKED)

    raw_scores = head_scores()
    row_max = jnp.max(raw_scores, axis=-1, keepdims=True)
    log_total = row_max + jnp.log(jnp.sum(jnp.exp(raw_scores - row_max), axis=-1, keepdims=True))
    weights_b = jnp.exp(raw_scores - log_total).astype(jnp.bfloat16)
    head_mixed = jnp.dot(weights_b, head_value, preferred_element_type=jnp.float32)
    head_mixed, across_output, across_gate_up, across_down = lax.optimization_barrier(
        (head_mixed, across_output, across_gate_up, across_down)
    )
    full_output = gather_cores(across_output, output_weight.shape)
    full_gate_up = gather_cores(across_gate_up, gate_up_weight.shape)
    full_down = gather_cores(across_down, down_weight.shape)
    mixed_b = own_heads(exchange(from_heads(head_mixed.astype(jnp.bfloat16)))).reshape(
        local_rows, HQ * HEAD_SIZE
    )
    residual_mid = input_f32 + jnp.dot(mixed_b, full_output, preferred_element_type=jnp.float32)
    gained_mid, second_normed, second_scale = rms_apply(residual_mid, second_gain)
    mlp_in = gained_mid.astype(jnp.bfloat16)
    gate_up_pre = jnp.dot(mlp_in, full_gate_up, preferred_element_type=jnp.float32)
    gate_pre = gate_up_pre[:, :ff_cols]
    up_pre = gate_up_pre[:, ff_cols:]
    sigmoid_gate = jax.nn.sigmoid(gate_pre)
    silu_gate = gate_pre * sigmoid_gate
    hidden = (silu_gate * up_pre).astype(jnp.bfloat16)
    layer_output = (
        residual_mid + jnp.dot(hidden, full_down, preferred_element_type=jnp.float32)
    ).astype(jnp.bfloat16)
    own_cotangent = cotangent[0]
    hidden_grad = right_dot(own_cotangent, full_down)
    gate_grad = (
        hidden_grad * up_pre * sigmoid_gate * (1.0 + gate_pre * (1.0 - sigmoid_gate))
    ).astype(jnp.bfloat16)
    up_grad = (hidden_grad * silu_gate).astype(jnp.bfloat16)
    gate_up_grad = jnp.concatenate([gate_grad, up_grad], axis=1)
    mlp_in_grad = right_dot(gate_up_grad, full_gate_up)
    second_gain_grad = jnp.sum(mlp_in_grad * second_normed, axis=0)
    mid_grad = own_cotangent.astype(jnp.float32) + root_mean_square_backward(
        mlp_in_grad, second_normed, second_scale, second_gain
    )
    mid_grad_b = mid_grad.astype(jnp.bfloat16)
    mixed_gradient = right_dot(mid_grad_b, full_output).astype(jnp.bfloat16)
    fsdp_size = lax.axis_size(FSDP)
    col_parts = (attention_input, mixed_b, mlp_in, hidden)
    widths = [p.shape[1] // fsdp_size for p in col_parts]
    stacked = jnp.concatenate(
        [p.reshape(local_rows, fsdp_size, w) for p, w in zip(col_parts, widths)], axis=2
    )
    cols = lax.all_to_all(stacked, FSDP, split_axis=1, concat_axis=0, tiled=True).reshape(
        fsdp_size * local_rows, sum(widths)
    )
    bounds = [sum(widths[:i]) for i in range(5)]
    attn_cols, mixed_cols, mlp_cols, hidden_cols = (
        cols[:, bounds[i] : bounds[i + 1]] for i in range(4)
    )
    gate_up_rows = lax.all_gather(gate_up_grad, FSDP, axis=0, tiled=True)
    cot_mid_rows = lax.all_gather(
        jnp.concatenate([own_cotangent, mid_grad_b], axis=1), FSDP, axis=0, tiled=True
    )
    model_width = own_cotangent.shape[1]
    output_shard = left_dot(mixed_cols, cot_mid_rows[:, model_width:])
    gate_up_shard = left_dot(mlp_cols, gate_up_rows)
    down_shard = left_dot(hidden_cols, cot_mid_rows[:, :model_width])
    mlp_rows = gate_up_shard.shape[0]
    mlp_packed = jnp.concatenate(
        [output_shard.reshape(mlp_rows, -1), gate_up_shard, down_shard.reshape(mlp_rows, -1)],
        axis=1,
    ).astype(jnp.bfloat16)
    head_out_grad = gather_half(
        exchange(to_heads(mixed_gradient.reshape(local_rows, HQ, HEAD_SIZE)))
    )
    mlp_packed, head_out_grad = lax.optimization_barrier((mlp_packed, head_out_grad))
    mlp_part = scatter_ctx(mlp_packed)
    out_grad_f = head_out_grad.astype(jnp.float32)
    delta = jnp.sum(out_grad_f * head_mixed, axis=-1, keepdims=True)
    probabilities = jnp.exp(head_scores() - log_total)
    value_part = left_dot(probabilities.astype(jnp.bfloat16), head_out_grad)
    prob_grad = right_dot(head_out_grad, head_value)
    score_grad = (probabilities * (prob_grad - delta)).astype(jnp.bfloat16)
    query_part = jnp.dot(score_grad, head_key, preferred_element_type=jnp.float32) * scale_factor
    key_part = left_dot(score_grad, head_query) * scale_factor
    returned = exchange(jnp.concatenate([
        from_heads(query_part.astype(jnp.bfloat16)),
        jnp.concatenate([key_part, value_part], axis=-1).astype(jnp.bfloat16).reshape(
            ctx_size, local_rows, 2 * HEAD_SIZE),
    ], axis=-1))
    query_grad_rows = own_heads(returned[..., :HEAD_SIZE]).astype(jnp.float32)
    kv_parts = returned[..., HEAD_SIZE:].astype(jnp.float32).reshape(
        halves, KEY_VALUE_HEADS, group, local_rows, 2 * HEAD_SIZE)
    kv_grad = jnp.transpose(jnp.sum(kv_parts, axis=(0, 2)), (1, 0, 2))
    local_key_gradient = kv_grad[..., :HEAD_SIZE]
    own_value_grad = kv_grad[..., HEAD_SIZE:].reshape(local_rows, KEY_VALUE_HEADS * HEAD_SIZE)
    query_back = rotary_backward(query_grad_rows, cosine_table, sine_values_table)
    query_gain_grad = jnp.sum(query_back * query_normed, axis=(0, 1))
    query_pre_grad = (
        root_mean_square_backward(query_back, query_normed, query_scale, query_gain)
        .astype(jnp.bfloat16)
        .reshape(local_rows, HQ * HEAD_SIZE)
    )
    key_backward_pass = rotary_backward(
        local_key_gradient,
        cosine_table,
        sine_values_table,
    )
    key_gain_grad = jnp.sum(key_backward_pass * key_after_norm, axis=(0, 1))
    key_before_norm_gradient = (
        root_mean_square_backward(key_backward_pass, key_after_norm, key_norm_scale, key_norm_gain)
        .astype(jnp.bfloat16)
        .reshape(local_rows, KEY_VALUE_HEADS * HEAD_SIZE)
    )
    value_gradient_second = own_value_grad.astype(jnp.bfloat16)
    qkv_grad = jnp.concatenate([query_pre_grad, key_before_norm_gradient, value_gradient_second], axis=1)
    attn_in_grad = (
        right_dot(qkv_grad, full_qkv)
    )
    first_gain_grad = jnp.sum(attn_in_grad * first_normed, axis=0)
    input_grad = mid_grad + root_mean_square_backward(
        attn_in_grad, first_normed, first_scale, first_gain
    )
    mlp_part, qkv_grad = lax.optimization_barrier((mlp_part, qkv_grad))
    mlp_reduced = gather_ctx(mlp_part)
    qkv_rows = lax.all_gather(qkv_grad, FSDP, axis=0, tiled=True)
    first_shard, second_shard, query_gain_shard, key_gain_shard = (
        lax.psum_scatter(first_gain_grad, FSDP, scatter_dimension=0, tiled=True),
        lax.psum_scatter(second_gain_grad, FSDP, scatter_dimension=0, tiled=True),
        lax.psum_scatter(query_gain_grad, FSDP, scatter_dimension=0, tiled=True),
        lax.psum_scatter(key_gain_grad, FSDP, scatter_dimension=0, tiled=True),
    )
    qkv_shard = left_dot(attn_cols, qkv_rows)
    shard_rows = qkv_shard.shape[0]
    gain_parts = (first_shard, second_shard, query_gain_shard, key_gain_shard)
    gain_block = jnp.zeros((shard_rows, 128), jnp.float32)
    for column, g in enumerate(gain_parts):
        gain_block = gain_block.at[: g.shape[0], column].set(g)
    attn_reduced = reduce_ctx(jnp.concatenate([qkv_shard, gain_block], axis=1).astype(jnp.bfloat16))
    output_width = output_shard.size // shard_rows
    output_total = mlp_reduced[:, :output_width].reshape(output_shard.shape)
    gate_total = mlp_reduced[:, output_width : output_width + ff_cols]
    up_total = mlp_reduced[:, output_width + ff_cols : output_width + 2 * ff_cols]
    down_total = mlp_reduced[:, output_width + 2 * ff_cols :].reshape(down_shard.shape)
    query_total = attn_reduced[:, : qkv_cols[0]]
    key_total = attn_reduced[:, qkv_cols[0] : qkv_cols[0] + qkv_cols[1]]
    value_total = attn_reduced[:, qkv_cols[0] + qkv_cols[1] : sum(qkv_cols)]
    at = sum(qkv_cols)
    reduced = attn_reduced
    first_total, second_total, query_gain_total, key_gain_total = (
        reduced[: g.shape[0], at + column] for column, g in enumerate(gain_parts)
    )
    return (
        layer_output[None],
        input_grad[None],
        query_total,
        key_total,
        value_total,
        output_total,
        gate_total,
        up_total,
        down_total,
        first_total,
        second_total,
        query_gain_total,
        key_gain_total,
    )


def solution(mesh):
    in_specs = (
        P(FSDP, CTX, None),
        P(FSDP, CTX, None),
        P(FSDP, None),
        P(FSDP, None),
        P(FSDP, None),
        P(FSDP, None),
        P(FSDP, None),
        P(FSDP, None),
        P(FSDP, None),
        P(FSDP, None),
        P(),
        P(),
        P(),
        P(),
    )
    out_specs = (
        P(FSDP, CTX, None),
        P(FSDP, CTX, None),
        P(FSDP, None),
        P(FSDP, None),
        P(FSDP, None),
        P(FSDP, None),
        P(FSDP, None),
        P(FSDP, None),
        P(FSDP, None),
        P(FSDP),
        P(FSDP),
        P(FSDP),
        P(FSDP),
    )
    torus_mesh = jax.sharding.Mesh(mesh.devices.reshape(2, 4, 4, 2, 2), ("yh", "x", "z", "yl", "c"))
    return jax.shard_map(
        on_device, mesh=torus_mesh, in_specs=in_specs, out_specs=out_specs, check_vma=False
    )
```

```python
import math

import jax
import jax.numpy as jnp
from jax import lax
from jax.sharding import PartitionSpec as P

HQ = 16
KEY_VALUE_HEADS = 8
HEAD_SIZE = 128
CTX = ("yh", "x", "z")
FSDP = ("yl", "c")


EPSILON = 1e-06
THETA = 1000000.0
MASKED = -1e30


def rms_apply(values, norm_gain):
    row_scale = lax.rsqrt(jnp.mean(values * values, axis=-1, keepdims=True) + EPSILON)
    normed = values * row_scale
    return (normed * norm_gain, normed, row_scale)


def root_mean_square_backward(gradient, normed, row_scale, norm_gain):
    normed_grad = gradient * norm_gain
    return row_scale * (
        normed_grad - normed * jnp.mean(normed_grad * normed, axis=-1, keepdims=True)
    )


def rope_tables(positions, head_width):
    half_width = head_width // 2
    inverse_freq = jnp.power(THETA, -2.0 * jnp.arange(half_width, dtype=jnp.float32) / head_width)
    angles = positions.astype(jnp.float32)[:, None] * inverse_freq[None, :]
    return (jnp.cos(angles)[:, None, :], jnp.sin(angles)[:, None, :])


def rotary_apply(values, cosine_table, sine_values_table):
    half_width = values.shape[-1] // 2
    front_half = values[..., :half_width]
    back_half = values[..., half_width:]
    return jnp.concatenate(
        [
            front_half * cosine_table - back_half * sine_values_table,
            back_half * cosine_table + front_half * sine_values_table,
        ],
        axis=-1,
    )


def rotary_backward(gradient, cosine_table, sine_values_table):
    half_width = gradient.shape[-1] // 2
    front_half = gradient[..., :half_width]
    back_half = gradient[..., half_width:]
    return jnp.concatenate(
        [
            front_half * cosine_table + back_half * sine_values_table,
            back_half * cosine_table - front_half * sine_values_table,
        ],
        axis=-1,
    )


def left_dot(left_side, right_side):
    return lax.dot_general(
        left_side, right_side, (((0,), (0,)), ((), ())), preferred_element_type=jnp.float32
    )


def right_dot(left_side, right_side):
    return lax.dot_general(
        left_side, right_side, (((1,), (1,)), ((), ())), preferred_element_type=jnp.float32
    )


def gather_across(values):
    return lax.all_gather(values, "yl", axis=0, tiled=False)


def gather_cores(across, shard_shape):
    other = lax.ppermute(across, "c", [(0, 1), (1, 0)])
    first_core = lax.axis_index("c") == 0
    both = jnp.stack([jnp.where(first_core, across, other), jnp.where(first_core, other, across)], axis=1)
    return both.reshape((-1,) + shard_shape[1:])


def gather_fsdp(values):
    return gather_cores(gather_across(values), values.shape)


def scatter_ctx(packed):
    part = lax.psum_scatter(packed, "x", scatter_dimension=0, tiled=True)
    part = lax.psum_scatter(part, "z", scatter_dimension=0, tiled=True)
    return (part.astype(jnp.float32) + lax.ppermute(part, "yh", [(0, 1), (1, 0)]).astype(jnp.float32)).astype(
        part.dtype
    )


def gather_ctx(part):
    return lax.all_gather(part, ("x", "z"), axis=0, tiled=True).astype(jnp.float32)


def reduce_ctx(packed):
    return gather_ctx(scatter_ctx(packed))


def on_device(
    layer_input,
    cotangent,
    block_order,
    query_weight,
    key_projection,
    value_projection,
    output_weight,
    gate_weight,
    up_weight,
    down_weight,
    first_gain,
    second_gain,
    query_gain,
    key_norm_gain,
):
    local_rows = layer_input.shape[1]
    block_rows = local_rows // 2
    ctx_size = lax.axis_size(CTX)
    halves = ctx_size // HQ
    half_devices = ctx_size // halves
    order_row = block_order[0]
    device_place = lax.axis_index(CTX)
    my_half = device_place // half_devices
    all_positions = (
        order_row[:, None] * block_rows + jnp.arange(block_rows, dtype=jnp.int32)[None, :]
    ).reshape(-1)
    own_positions = lax.dynamic_slice_in_dim(all_positions, device_place * local_rows, local_rows)
    cosine_table, sine_values_table = rope_tables(own_positions, HEAD_SIZE)
    scale_factor = 1.0 / math.sqrt(HEAD_SIZE)
    half_rows = half_devices * local_rows
    query_positions = lax.dynamic_slice_in_dim(all_positions, my_half * half_rows, half_rows)
    allowed = all_positions[None, :] <= query_positions[:, None]
    half_select = (jnp.arange(halves, dtype=jnp.int32) == my_half)[:, None, None, None]

    def to_heads(per_head):
        by_head = jnp.transpose(per_head, (1, 0, 2))
        return jnp.where(half_select, by_head[None], jnp.zeros_like(by_head)[None]).reshape(
            ctx_size, local_rows, per_head.shape[-1]
        )

    def gather_half(received):
        return lax.dynamic_slice_in_dim(received, my_half * half_devices, half_devices, 0).reshape(
            half_rows, received.shape[-1]
        )

    def from_heads(per_head):
        blocks = per_head.reshape(half_devices, local_rows, per_head.shape[-1])
        return jnp.where(half_select, blocks[None], jnp.zeros_like(blocks)[None]).reshape(
            ctx_size, local_rows, per_head.shape[-1]
        )

    def own_heads(received):
        mine = lax.dynamic_slice_in_dim(received, my_half * half_devices, half_devices, 0)
        return jnp.transpose(mine, (1, 0, 2))

    def exchange(values):
        return lax.all_to_all(values, CTX, split_axis=0, concat_axis=0, tiled=True)

    qkv_cols = (query_weight.shape[1], key_projection.shape[1], value_projection.shape[1])
    full_qkv = gather_fsdp(jnp.concatenate([query_weight, key_projection, value_projection], axis=1))
    across_output = gather_across(output_weight)
    ff_cols = gate_weight.shape[1]
    gate_up_weight = jnp.concatenate([gate_weight, up_weight], axis=1)
    across_gate_up = gather_across(gate_up_weight)
    across_down = gather_across(down_weight)
    input_f32 = layer_input[0].astype(jnp.float32)
    gained, first_normed, first_scale = rms_apply(input_f32, first_gain)
    attention_input = gained.astype(jnp.bfloat16)
    qkv_pre = jnp.dot(attention_input, full_qkv, preferred_element_type=jnp.float32)
    query_pre = qkv_pre[:, : qkv_cols[0]].reshape(local_rows, HQ, HEAD_SIZE)
    query_gained, query_normed, query_scale = rms_apply(query_pre, query_gain)
    query_rotated = rotary_apply(query_gained, cosine_table, sine_values_table).astype(jnp.bfloat16)
    key_before_norm = qkv_pre[:, qkv_cols[0] : qkv_cols[0] + qkv_cols[1]].reshape(
        local_rows, KEY_VALUE_HEADS, HEAD_SIZE
    )
    key_after_gain, key_after_norm, key_norm_scale = rms_apply(key_before_norm, key_norm_gain)
    own_keys = rotary_apply(key_after_gain, cosine_table, sine_values_table).astype(jnp.bfloat16)
    own_values = (
        qkv_pre[:, qkv_cols[0] + qkv_cols[1] :]
        .astype(jnp.bfloat16)
        .reshape(local_rows, KEY_VALUE_HEADS, HEAD_SIZE)
    )
    group = HQ // KEY_VALUE_HEADS
    key_value = jnp.repeat(jnp.concatenate([own_keys, own_values], axis=-1), group, axis=1)
    sent = jnp.concatenate([to_heads(query_rotated), jnp.tile(
        jnp.transpose(key_value, (1, 0, 2)), (halves, 1, 1))], axis=-1)
    received = exchange(sent)
    head_query = gather_half(received[..., :HEAD_SIZE])
    head_key = received[..., HEAD_SIZE : 2 * HEAD_SIZE].reshape(-1, HEAD_SIZE)
    head_value = received[..., 2 * HEAD_SIZE :].reshape(-1, HEAD_SIZE)

    def head_scores():
        raw_scores = (
            jnp.einsum("qd,kd->qk", head_query, head_key, preferred_element_type=jnp.float32)
            * scale_factor
        )
        return jnp.where(allowed, raw_scores, MASKED)

    raw_scores = head_scores()
    row_max = jnp.max(raw_scores, axis=-1, keepdims=True)
    log_total = row_max + jnp.log(jnp.sum(jnp.exp(raw_scores - row_max), axis=-1, keepdims=True))
    weights_b = jnp.exp(raw_scores - log_total).astype(jnp.bfloat16)
    head_mixed = jnp.dot(weights_b, head_value, preferred_element_type=jnp.float32)
    head_mixed, across_output, across_gate_up, across_down = lax.optimization_barrier(
        (head_mixed, across_output, across_gate_up, across_down)
    )
    full_output = gather_cores(across_output, output_weight.shape)
    full_gate_up = gather_cores(across_gate_up, gate_up_weight.shape)
    full_down = gather_cores(across_down, down_weight.shape)
    mixed_b = own_heads(exchange(from_heads(head_mixed.astype(jnp.bfloat16)))).reshape(
        local_rows, HQ * HEAD_SIZE
    )
    residual_mid = input_f32 + jnp.dot(mixed_b, full_output, preferred_element_type=jnp.float32)
    gained_mid, second_normed, second_scale = rms_apply(residual_mid, second_gain)
    mlp_in = gained_mid.astype(jnp.bfloat16)
    gate_up_pre = jnp.dot(mlp_in, full_gate_up, preferred_element_type=jnp.float32)
    gate_pre = gate_up_pre[:, :ff_cols]
    up_pre = gate_up_pre[:, ff_cols:]
    sigmoid_gate = jax.nn.sigmoid(gate_pre)
    silu_gate = gate_pre * sigmoid_gate
    hidden = (silu_gate * up_pre).astype(jnp.bfloat16)
    layer_output = (
        residual_mid + jnp.dot(hidden, full_down, preferred_element_type=jnp.float32)
    ).astype(jnp.bfloat16)
    own_cotangent = cotangent[0]
    hidden_grad = right_dot(own_cotangent, full_down)
    gate_grad = (
        hidden_grad * up_pre * sigmoid_gate * (1.0 + gate_pre * (1.0 - sigmoid_gate))
    ).astype(jnp.bfloat16)
    up_grad = (hidden_grad * silu_gate).astype(jnp.bfloat16)
    gate_up_grad = jnp.concatenate([gate_grad, up_grad], axis=1)
    mlp_in_grad = right_dot(gate_up_grad, full_gate_up)
    second_gain_grad = jnp.sum(mlp_in_grad * second_normed, axis=0)
    mid_grad = own_cotangent.astype(jnp.float32) + root_mean_square_backward(
        mlp_in_grad, second_normed, second_scale, second_gain
    )
    mid_grad_b = mid_grad.astype(jnp.bfloat16)
    mixed_gradient = right_dot(mid_grad_b, full_output).astype(jnp.bfloat16)
    fsdp_size = lax.axis_size(FSDP)
    col_parts = (attention_input, mixed_b, mlp_in, hidden)
    widths = [p.shape[1] // fsdp_size for p in col_parts]
    stacked = jnp.concatenate(
        [p.reshape(local_rows, fsdp_size, w) for p, w in zip(col_parts, widths)], axis=2
    )
    cols = lax.all_to_all(stacked, FSDP, split_axis=1, concat_axis=0, tiled=True).reshape(
        fsdp_size * local_rows, sum(widths)
    )
    bounds = [sum(widths[:i]) for i in range(5)]
    attn_cols, mixed_cols, mlp_cols, hidden_cols = (
        cols[:, bounds[i] : bounds[i + 1]] for i in range(4)
    )
    gate_up_rows = lax.all_gather(gate_up_grad, FSDP, axis=0, tiled=True)
    cot_mid_rows = lax.all_gather(
        jnp.concatenate([own_cotangent, mid_grad_b], axis=1), FSDP, axis=0, tiled=True
    )
    model_width = own_cotangent.shape[1]
    output_shard = left_dot(mixed_cols, cot_mid_rows[:, model_width:])
    gate_up_shard = left_dot(mlp_cols, gate_up_rows)
    down_shard = left_dot(hidden_cols, cot_mid_rows[:, :model_width])
    mlp_rows = gate_up_shard.shape[0]
    mlp_packed = jnp.concatenate(
        [output_shard.reshape(mlp_rows, -1), gate_up_shard, down_shard.reshape(mlp_rows, -1)],
        axis=1,
    ).astype(jnp.bfloat16)
    head_out_grad = gather_half(
        exchange(to_heads(mixed_gradient.reshape(local_rows, HQ, HEAD_SIZE)))
    )
    mlp_packed, head_out_grad = lax.optimization_barrier((mlp_packed, head_out_grad))
    mlp_part = scatter_ctx(mlp_packed)
    out_grad_f = head_out_grad.astype(jnp.float32)
    delta = jnp.sum(out_grad_f * head_mixed, axis=-1, keepdims=True)
    probabilities = jnp.exp(head_scores() - log_total)
    value_part = left_dot(probabilities.astype(jnp.bfloat16), head_out_grad)
    prob_grad = right_dot(head_out_grad, head_value)
    score_grad = (probabilities * (prob_grad - delta)).astype(jnp.bfloat16)
    query_part = jnp.dot(score_grad, head_key, preferred_element_type=jnp.float32) * scale_factor
    key_part = left_dot(score_grad, head_query) * scale_factor
    returned = exchange(jnp.concatenate([
        from_heads(query_part.astype(jnp.bfloat16)),
        jnp.concatenate([key_part, value_part], axis=-1).astype(jnp.bfloat16).reshape(
            ctx_size, local_rows, 2 * HEAD_SIZE),
    ], axis=-1))
    query_grad_rows = own_heads(returned[..., :HEAD_SIZE]).astype(jnp.float32)
    kv_parts = returned[..., HEAD_SIZE:].astype(jnp.float32).reshape(
        halves, KEY_VALUE_HEADS, group, local_rows, 2 * HEAD_SIZE)
    kv_grad = jnp.transpose(jnp.sum(kv_parts, axis=(0, 2)), (1, 0, 2))
    local_key_gradient = kv_grad[..., :HEAD_SIZE]
    own_value_grad = kv_grad[..., HEAD_SIZE:].reshape(local_rows, KEY_VALUE_HEADS * HEAD_SIZE)
    query_back = rotary_backward(query_grad_rows, cosine_table, sine_values_table)
    query_gain_grad = jnp.sum(query_back * query_normed, axis=(0, 1))
    query_pre_grad = (
        root_mean_square_backward(query_back, query_normed, query_scale, query_gain)
        .astype(jnp.bfloat16)
        .reshape(local_rows, HQ * HEAD_SIZE)
    )
    key_backward_pass = rotary_backward(
        local_key_gradient,
        cosine_table,
        sine_values_table,
    )
    key_gain_grad = jnp.sum(key_backward_pass * key_after_norm, axis=(0, 1))
    key_before_norm_gradient = (
        root_mean_square_backward(key_backward_pass, key_after_norm, key_norm_scale, key_norm_gain)
        .astype(jnp.bfloat16)
        .reshape(local_rows, KEY_VALUE_HEADS * HEAD_SIZE)
    )
    value_gradient_second = own_value_grad.astype(jnp.bfloat16)
    qkv_grad = jnp.concatenate([query_pre_grad, key_before_norm_gradient, value_gradient_second], axis=1)
    attn_in_grad = (
        right_dot(qkv_grad, full_qkv)
    )
    first_gain_grad = jnp.sum(attn_in_grad * first_normed, axis=0)
    input_grad = mid_grad + root_mean_square_backward(
        attn_in_grad, first_normed, first_scale, first_gain
    )
    mlp_part, qkv_grad = lax.optimization_barrier((mlp_part, qkv_grad))
    mlp_reduced = gather_ctx(mlp_part)
    qkv_rows = lax.all_gather(qkv_grad, FSDP, axis=0, tiled=True)
    first_shard, second_shard, query_gain_shard, key_gain_shard = (
        lax.psum_scatter(first_gain_grad, FSDP, scatter_dimension=0, tiled=True),
        lax.psum_scatter(second_gain_grad, FSDP, scatter_dimension=0, tiled=True),
        lax.psum_scatter(query_gain_grad, FSDP, scatter_dimension=0, tiled=True),
        lax.psum_scatter(key_gain_grad, FSDP, scatter_dimension=0, tiled=True),
    )
    qkv_shard = left_dot(attn_cols, qkv_rows)
    shard_rows = qkv_shard.shape[0]
    gain_parts = (first_shard, second_shard, query_gain_shard, key_gain_shard)
    gain_block = jnp.zeros((shard_rows, 128), jnp.float32)
    for column, g in enumerate(gain_parts):
        gain_block = gain_block.at[: g.shape[0], column].set(g)
    attn_reduced = reduce_ctx(jnp.concatenate([qkv_shard, gain_block], axis=1).astype(jnp.bfloat16))
    output_width = output_shard.size // shard_rows
    output_total = mlp_reduced[:, :output_width].reshape(output_shard.shape)
    gate_total = mlp_reduced[:, output_width : output_width + ff_cols]
    up_total = mlp_reduced[:, output_width + ff_cols : output_width + 2 * ff_cols]
    down_total = mlp_reduced[:, output_width + 2 * ff_cols :].reshape(down_shard.shape)
    query_total = attn_reduced[:, : qkv_cols[0]]
    key_total = attn_reduced[:, qkv_cols[0] : qkv_cols[0] + qkv_cols[1]]
    value_total = attn_reduced[:, qkv_cols[0] + qkv_cols[1] : sum(qkv_cols)]
    at = sum(qkv_cols)
    reduced = attn_reduced
    first_total, second_total, query_gain_total, key_gain_total = (
        reduced[: g.shape[0], at + column] for column, g in enumerate(gain_parts)
    )
    return (
        layer_output[None],
        input_grad[None],
        query_total,
        key_total,
        value_total,
        output_total,
        gate_total,
        up_total,
        down_total,
        first_total,
        second_total,
        query_gain_total,
        key_gain_total,
    )


def solution(mesh):
    in_specs = (
        P(FSDP, CTX, None),
        P(FSDP, CTX, None),
        P(FSDP, None),
        P(FSDP, None),
        P(FSDP, None),
        P(FSDP, None),
        P(FSDP, None),
        P(FSDP, None),
        P(FSDP, None),
        P(FSDP, None),
        P(),
        P(),
        P(),
        P(),
    )
    out_specs = (
        P(FSDP, CTX, None),
        P(FSDP, CTX, None),
        P(FSDP, None),
        P(FSDP, None),
        P(FSDP, None),
        P(FSDP, None),
        P(FSDP, None),
        P(FSDP, None),
        P(FSDP, None),
        P(FSDP),
        P(FSDP),
        P(FSDP),
        P(FSDP),
    )
    torus_mesh = jax.sharding.Mesh(mesh.devices.reshape(2, 4, 4, 2, 2), ("yh", "x", "z", "yl", "c"))
    return jax.shard_map(
        on_device, mesh=torus_mesh, in_specs=in_specs, out_specs=out_specs, check_vma=False
    )
```
